32 devices in a mesh: rep: 2 (over x), shard: 16 (over z, y, core).
Axes of the slice: x: 2, y: 2, z: 4, core: 2. Of those that a mesh axis runs over, the one named last changes fastest.
Arguments:
- tokens: bfloat16 [8192, 1536], P(('rep', 'shard')), may hold values from -6 to 6
- cotangent: bfloat16 [8192, 1536], P(('rep', 'shard')), may hold values from -6 to 6
- mix_gain: bfloat16 [1536], P('shard'), may hold values from 0.25 to 1.75
- branch_proj: bfloat16 [1536, 2048], P('shard'), may hold values from -0.15625 to 0.15625
- lruin_proj: bfloat16 [1536, 2048], P('shard'), may hold values from -0.15625 to 0.15625
- conv_kernel: bfloat16 [4, 2048], P(None, 'shard'), may hold values from -3 to 3
- conv_bias: bfloat16 [2048], P('shard'), may hold values from -3 to 3
- recur_proj: bfloat16 [2048, 2048], P('shard'), may hold values from -0.125 to 0.125
- recur_bias: bfloat16 [2048], P('shard'), may hold values from -4 to 4
- admit_proj: bfloat16 [2048, 2048], P('shard'), may hold values from -0.125 to 0.125
- admit_bias: bfloat16 [2048], P('shard'), may hold values from -4 to 4
- decay_param: bfloat16 [2048], P('shard'), may hold values from 3.5 to 7.5
- out_proj: bfloat16 [2048, 1536], P('shard'), may hold values from -0.5 to 0.5
- ffn_gain: bfloat16 [1536], P('shard'), may hold values from 0.25 to 1.75
- ffn_gate: bfloat16 [1536, 4608], P('shard'), may hold values from -0.15625 to 0.15625
- ffn_up: bfloat16 [1536, 4608], P('shard'), may hold values from -0.15625 to 0.15625
- ffn_down: bfloat16 [4608, 1536], P('shard'), may hold values from -0.1875 to 0.1875
Outputs:
- block_out: bfloat16 [8192, 1536], P(('rep', 'shard'))
- tokens_grad: float32 [8192, 1536], P(('rep', 'shard'))
- mixgain_grad: float32 [1536], P('shard')
- branch_grad: float32 [1536, 2048], P('shard')
- lruin_grad: float32 [1536, 2048], P('shard')
- kernel_grad: float32 [4, 2048], P(None, 'shard')
- convbias_grad: float32 [2048], P('shard')
- recur_grad: float32 [2048, 2048], P('shard')
- recurbias_grad: float32 [2048], P('shard')
- admit_grad: float32 [2048, 2048], P('shard')
- admitbias_grad: float32 [2048], P('shard')
- decay_grad: float32 [2048], P('shard')
- outproj_grad: float32 [2048, 1536], P('shard')
- ffngain_grad: float32 [1536], P('shard')
- ffngate_grad: float32 [1536, 4608], P('shard')
- ffnup_grad: float32 [1536, 4608], P('shard')
- ffndown_grad: float32 [4608, 1536], P('shard')
The draws below stay inside these ranges and needn't reach their ends.
All inputs are finite; a program needn't handle non-finite values.
Results may differ from the reference program's by a relative error of at most 0.0098.
Values may be sent and summed in bfloat16 or wider, within the bound.
No kernel may reach another device: no remote copies, remote signals or barrier semaphores. Data moves between devices by JAX's collectives and lax.ppermute only.
A program may use at most 384 MiB of HBM per device.

```python
import math
import jax
import jax.numpy as jnp
from jax import lax

D = 1536
R = 2048
FF = 4608
CONV = 4
LEN = 256
SEQS = 32
TOKENS = 8192


def block_scale(rng, dims, shards, smallest, top_value):
    level, own = 1.0, jax.random.fold_in(rng, 6)
    for dim, parts in shards:
        draws = jnp.exp(jax.random.uniform(jax.random.fold_in(own, dim), (parts,), jnp.float32, smallest / len(shards), top_value / len(shards)))
        level = level * jnp.repeat(draws, dims[dim] // parts).reshape([-1 if axis == dim else 1 for axis in range(len(dims))])
    return level


def bell_draw(stream_key, shape, spread, limit, pieces=(), kind=jnp.bfloat16):
    level = block_scale(stream_key, shape, pieces, -0.22, 0.18) if pieces else 1.0
    array = jax.random.normal(stream_key, shape, jnp.float32) * spread * level
    return jnp.minimum(jnp.maximum(array, -limit), limit).astype(kind)


def setup_inputs(seed: int = 0) -> dict:
    keys = jax.random.split(jax.random.key(seed), 18)
    return {
        "tokens": bell_draw(keys[0], (TOKENS, D), 1.0, 6.0, ((0, 32),)),
        "cotangent": bell_draw(keys[1], (TOKENS, D), 1.0, 6.0, ((0, 32),)),
        "mix_gain": jnp.clip(1.0 + 0.15 * jax.random.normal(keys[2], (D,), jnp.float32), 0.25, 1.75).astype(jnp.bfloat16),
        "branch_proj": bell_draw(keys[3], (D, R), D ** -0.5, 0.15625, ((0, 16),)),
        "lruin_proj": bell_draw(keys[4], (D, R), D ** -0.5, 0.15625, ((0, 16),)),
        "conv_kernel": bell_draw(keys[5], (CONV, R), CONV ** -0.5, 3.0, ((1, 16),)),
        "conv_bias": bell_draw(keys[6], (R,), 0.5, 3.0, ((0, 16),)),
        "recur_proj": bell_draw(keys[7], (R, R), R ** -0.5, 0.125, ((0, 16),)),
        "recur_bias": bell_draw(keys[8], (R,), 1.0, 4.0, ((0, 16),)),
        "admit_proj": bell_draw(keys[9], (R, R), R ** -0.5, 0.125, ((0, 16),)),
        "admit_bias": bell_draw(keys[10], (R,), 1.0, 4.0, ((0, 16),)),
        "decay_param": jnp.clip(3.5 + 4.0 * jax.random.uniform(keys[11], (R,), jnp.float32) ** block_scale(keys[11], (R,), ((0, 16),), -0.2, 0.2), 3.5, 7.5).astype(jnp.bfloat16),
        "out_proj": bell_draw(keys[12], (R, D), (R // 16) ** -0.5, 0.5, ((0, 16),)),
        "ffn_gain": jnp.clip(1.0 + 0.15 * jax.random.normal(keys[13], (D,), jnp.float32), 0.25, 1.75).astype(jnp.bfloat16),
        "ffn_gate": bell_draw(keys[14], (D, FF), D ** -0.5, 0.15625, ((0, 16),)),
        "ffn_up": bell_draw(keys[15], (D, FF), D ** -0.5, 0.15625, ((0, 16),)),
        "ffn_down": bell_draw(keys[16], (FF, D), (FF // 4) ** -0.5, 0.1875, ((0, 16),)),
    }


EPS = 1e-06
DECAY_SCALE = 8.0
ROOT_FLOOR = 0.001
HIGH = lax.Precision.HIGHEST

@jax.custom_vjp
def low(v):
    return lax.optimization_barrier(v.astype(jnp.bfloat16)).astype(jnp.float32)

@jax.custom_vjp
def low_back(v):
    return v

def low_keep(v):
    return (low(v), None)

def low_pass(kept, grad):
    return (grad,)

def back_keep(v):
    return (v, None)

def back_low(kept, grad):
    return (low(grad),)
low.defvjp(low_keep, low_pass)
low_back.defvjp(back_keep, back_low)

def project(left, right):
    return jnp.einsum('gtd,de->gte', left, right, precision=HIGH)

def rms_norm(values, gain):
    return values * lax.rsqrt(lax.optimization_barrier(jnp.mean(values * values, axis=-1, keepdims=True)) + EPS) * gain

def convolve(values, kernel, bias):
    length = values.shape[1]
    total = jnp.zeros_like(values) + bias
    for offset in range(kernel.shape[0]):
        shifted = jnp.pad(values, ((0, 0), (offset, 0), (0, 0)))[:, :length]
        total = total + kernel[offset] * shifted
    return total

def combine(earlier, later):
    return (earlier[0] * later[0], later[0] * earlier[1] + later[1])

def recurrence(branch_pre, admitted, recur_pre, admit_pre, recur_bias, admit_bias, decay_param):
    gate_r = jax.nn.sigmoid(recur_pre + recur_bias)
    gate_i = jax.nn.sigmoid(admit_pre + admit_bias)
    decay = jnp.exp(-DECAY_SCALE * gate_r * jax.nn.softplus(-decay_param))
    inflow = jnp.sqrt(jnp.maximum(1.0 - decay * decay, ROOT_FLOOR)) * gate_i * admitted
    factors, states = lax.associative_scan(combine, (decay, inflow), axis=1)
    return states * jax.nn.gelu(branch_pre, approximate=True)

def block(values, mix_gain, branch_proj, lruin_proj, conv_kernel, conv_bias, recur_proj, recur_bias, admit_proj, admit_bias, decay_param, out_proj, ffn_gain, ffn_gate, ffn_up, ffn_down):
    normed = low(rms_norm(values, mix_gain))
    branch_pre = low_back(project(normed, branch_proj))
    lru_pre = low_back(project(normed, lruin_proj))
    admitted = low(convolve(lru_pre, conv_kernel, conv_bias))
    recur_pre = low_back(project(admitted, recur_proj))
    admit_pre = low_back(project(admitted, admit_proj))
    mixed = low(recurrence(branch_pre, admitted, recur_pre, admit_pre, recur_bias, admit_bias, decay_param))
    middle = values + low_back(project(mixed, out_proj))
    normed_two = low(rms_norm(middle, ffn_gain))
    gate_pre = low_back(project(normed_two, ffn_gate))
    up_pre = low_back(project(normed_two, ffn_up))
    hidden = low(jax.nn.gelu(gate_pre, approximate=True) * up_pre)
    return middle + low_back(project(hidden, ffn_down))

def reference(tokens, cotangent, mix_gain, branch_proj, lruin_proj, conv_kernel, conv_bias, recur_proj, recur_bias, admit_proj, admit_bias, decay_param, out_proj, ffn_gain, ffn_gate, ffn_up, ffn_down):
    params = tuple((param.astype(jnp.float32) for param in (mix_gain, branch_proj, lruin_proj, conv_kernel, conv_bias, recur_proj, recur_bias, admit_proj, admit_bias, decay_param, out_proj, ffn_gain, ffn_gate, ffn_up, ffn_down)))
    group = math.gcd(SEQS, max(1, 4096 // LEN))
    inputs = tokens.astype(jnp.float32).reshape(SEQS // group, group, LEN, D)
    cotans = cotangent.astype(jnp.float32).reshape(SEQS // group, group, LEN, D)

    def step(totals, item):
        values, cotan = item
        result, pull = jax.vjp(block, values, *params)
        grads = pull(cotan)
        return (tuple((total + grad for total, grad in zip(totals, grads[1:]))), (result, grads[0]))
    start = tuple((jnp.zeros(param.shape, jnp.float32) for param in params))
    totals, (results, token_grads) = lax.scan(step, start, (inputs, cotans))
    block_out = results.reshape(TOKENS, D).astype(jnp.bfloat16)
    tokens_grad = token_grads.reshape(TOKENS, D)
    return (block_out, tokens_grad, totals[0], totals[1], totals[2], totals[3], totals[4], totals[5], totals[6], totals[7], totals[8], totals[9], totals[10], totals[11], totals[12], totals[13], totals[14])
```

```python
import functools
import math

import jax
import jax.numpy as jnp
from jax import lax
from jax.experimental import pallas as pl
from jax.experimental.pallas import tpu as pltpu
from jax.sharding import PartitionSpec as P

EPS = 1e-06
DECAY_SCALE = 8.0
ROOT_FLOOR = 0.001
GELU_K = math.sqrt(2.0 / math.pi)
GELU_C = 0.044715
ROWS = 16
BF16 = jnp.bfloat16
F32 = jnp.float32


def matmul(left, right):
    return jnp.dot(left, right, preferred_element_type=F32)


def rows_product(left, right):
    return lax.dot_general(left, right, (((0,), (0,)), ((), ())), preferred_element_type=F32)


def cols_product(left, right):
    return lax.dot_general(left, right, (((1,), (1,)), ((), ())), preferred_element_type=F32)


def widen(value):
    return value.astype(F32)


def gelu(v):
    return 0.5 * v * (1.0 + jnp.tanh(GELU_K * (v + GELU_C * v * v * v)))


def gelu_slope(v):
    t = jnp.tanh(GELU_K * (v + GELU_C * v * v * v))
    return 0.5 * (1.0 + t) + 0.5 * v * (1.0 - t * t) * GELU_K * (1.0 + 3.0 * GELU_C * v * v)


def forward_kernel(pre_ref, gates_r_ref, gates_i_ref, admitted_ref, params_ref, mixed_ref, before_ref):
    width = pre_ref.shape[1]
    rbias, abias, rate = params_ref[0:1, :], params_ref[1:2, :], params_ref[2:3, :]
    row = lax.broadcasted_iota(jnp.int32, (ROWS, width), 0)

    def step(i, carry):
        at = pl.ds(pl.multiple_of(i * ROWS, ROWS), ROWS)
        gate_r = jax.nn.sigmoid(gates_r_ref[at, :] + rbias)
        gate_i = jax.nn.sigmoid(gates_i_ref[at, :] + abias)
        a = jnp.exp(-(gate_r * rate))
        b = jnp.sqrt(jnp.maximum(1.0 - a * a, ROOT_FLOOR)) * gate_i * widen(admitted_ref[at, :])
        for d in (1, 2, 4, 8):
            keep = row >= d
            b = b + a * jnp.where(keep, pltpu.roll(b, d, 0), 0.0)
            a = a * jnp.where(keep, pltpu.roll(a, d, 0), 1.0)
        state = b + a * carry
        before_ref[at, :] = jnp.where(row >= 1, pltpu.roll(state, 1, 0), carry)
        mixed_ref[at, :] = (state * gelu(pre_ref[at, :])).astype(BF16)
        return jnp.broadcast_to(state[ROWS - 1 : ROWS, :], (ROWS, width))

    lax.fori_loop(0, pre_ref.shape[0] // ROWS, step, jnp.zeros((ROWS, width), F32))


def backward_kernel(
    cot_ref, pre_ref, gates_r_ref, gates_i_ref, admitted_ref, before_ref, params_ref,
    branch_ref, recur_ref, admit_ref, direct_ref, sums_ref,
):
    width = pre_ref.shape[1]
    rbias, abias, rate = params_ref[0:1, :], params_ref[1:2, :], params_ref[2:3, :]
    row = lax.broadcasted_iota(jnp.int32, (ROWS, width), 0)
    blocks = pre_ref.shape[0] // ROWS

    def step(i, state):
        carry, sum_r, sum_i, sum_d = state
        at = pl.ds(pl.multiple_of((blocks - 1 - i) * ROWS, ROWS), ROWS)
        gate_r = jax.nn.sigmoid(gates_r_ref[at, :] + rbias)
        gate_i = jax.nn.sigmoid(gates_i_ref[at, :] + abias)
        admitted = widen(admitted_ref[at, :])
        a = jnp.exp(-(gate_r * rate))
        rest = 1.0 - a * a
        root = jnp.sqrt(jnp.maximum(rest, ROOT_FLOOR))
        before = before_ref[at, :]
        state_now = a * before + root * gate_i * admitted
        pre = pre_ref[at, :]
        cot = cot_ref[at, :]
        branch_ref[at, :] = (cot * state_now * gelu_slope(pre)).astype(BF16)
        own = cot * gelu(pre)
        f = a
        e = a * own
        for d in (1, 2, 4, 8):
            keep = row < ROWS - d
            e = e + f * jnp.where(keep, pltpu.roll(e, ROWS - d, 0), 0.0)
            f = f * jnp.where(keep, pltpu.roll(f, ROWS - d, 0), 1.0)
        e = e + f * carry
        g = own + jnp.where(row < ROWS - 1, pltpu.roll(e, ROWS - 1, 0), carry)
        direct_ref[at, :] = g * root * gate_i
        share = jnp.where(rest > ROOT_FLOOR, 1.0, jnp.where(rest == ROOT_FLOOR, 0.5, 0.0))
        d_log = a * (g * before - g * gate_i * admitted * (share * a / root))
        d_gate_r = -(d_log * rate)
        d_gate_i = g * root * admitted
        recur = d_gate_r * gate_r * (1.0 - gate_r)
        admit = d_gate_i * gate_i * (1.0 - gate_i)
        recur_ref[at, :] = recur.astype(BF16)
        admit_ref[at, :] = admit.astype(BF16)
        carry = jnp.broadcast_to(e[0:1, :], (ROWS, width))
        return carry, sum_r + recur, sum_i + admit, sum_d + d_log * gate_r

    zero = jnp.zeros((ROWS, width), F32)
    _, sum_r, sum_i, sum_d = lax.fori_loop(0, blocks, step, (zero, zero, zero, zero))
    sums_ref[0:ROWS, :] = sum_r
    sums_ref[ROWS : 2 * ROWS, :] = sum_i
    sums_ref[2 * ROWS : 3 * ROWS, :] = sum_d


def recurrence_forward(pre, gates, admitted, params, length):
    tokens, width = admitted.shape
    tile = math.gcd(width, 512)
    n = width // tile
    near = pl.BlockSpec((length, tile), lambda s, j: (s, j))
    far = pl.BlockSpec((length, tile), lambda s, j: (s, j + n))
    vector = pl.BlockSpec((8, tile), lambda s, j: (0, j))
    return pl.pallas_call(
        forward_kernel,
        grid=(tokens // length, n),
        in_specs=[near, near, far, near, vector],
        out_specs=[near, near],
        out_shape=[
            jax.ShapeDtypeStruct((tokens, width), BF16),
            jax.ShapeDtypeStruct((tokens, width), F32),
        ],
        cost_estimate=pl.CostEstimate(flops=60 * tokens * width, bytes_accessed=20 * tokens * width, transcendentals=6 * tokens * width),
        name="recurrence_forward",
    )(pre, gates, gates, admitted, params)


def recurrence_backward(cot, pre, gates, admitted, before, params, length):
    tokens, width = admitted.shape
    tile = math.gcd(width, 512)
    n = width // tile
    near = pl.BlockSpec((length, tile), lambda s, j: (s, j))
    far = pl.BlockSpec((length, tile), lambda s, j: (s, j + n))
    vector = pl.BlockSpec((8, tile), lambda s, j: (0, j))
    low = jax.ShapeDtypeStruct((tokens, width), BF16)
    return pl.pallas_call(
        backward_kernel,
        grid=(tokens // length, n),
        in_specs=[near, near, near, far, near, near, vector],
        out_specs=[near, near, near, near, pl.BlockSpec((3 * ROWS, tile), lambda s, j: (s, j))],
        out_shape=[
            low, low, low,
            jax.ShapeDtypeStruct((tokens, width), F32),
            jax.ShapeDtypeStruct((3 * ROWS * (tokens // length), width), F32),
        ],
        cost_estimate=pl.CostEstimate(flops=120 * tokens * width, bytes_accessed=34 * tokens * width, transcendentals=8 * tokens * width),
        name="recurrence_backward",
    )(cot, pre, gates, gates, admitted, before, params)


def shifted(values, offset):
    if offset == 0:
        return values
    if offset > 0:
        return jnp.pad(values, ((0, 0), (offset, 0), (0, 0)))[:, : values.shape[1]]
    return jnp.pad(values, ((0, 0), (0, -offset), (0, 0)))[:, -offset:]


def body(
    groups, shards,
    tokens, cotangent, mix_gain, branch_proj, lruin_proj, conv_kernel, conv_bias, recur_proj, recur_bias,
    admit_proj, admit_bias, decay_param, out_proj, ffn_gain, ffn_gate, ffn_up, ffn_down,
):
    cores = 2
    f2 = 2 ** int(math.log2(math.isqrt(shards // cores)))
    f1 = shards // cores // f2
    side = lax.axis_index("rep") % 2
    here = lax.axis_index("shard")
    core, i2, i1 = here % cores, here // cores % f2, here // (cores * f2)
    taps = conv_kernel.shape[0]
    length, width = tokens.shape
    low_r = branch_proj.shape[1]
    half_r = low_r // 2
    half_f = ffn_gate.shape[1] // 2
    piece_f = half_f // shards

    def swap(v):
        return lax.ppermute(v, "rep", [(i, i ^ 1) for i in range(groups)])

    def swap_rows(v):
        v = swap(v)
        return jnp.concatenate([v[length:], v[:length]], axis=0)

    def mine(v, size, axis):
        return lax.dynamic_slice_in_dim(v, side * size, size, axis)

    def theirs(v, size, axis):
        return lax.dynamic_slice_in_dim(v, (1 - side) * size, size, axis)

    def natural(own, other):
        first = jnp.where(side == 0, own, other)
        second = jnp.where(side == 0, other, own)
        return jnp.concatenate([first, second], axis=-1)

    def with_pair(own):
        return jnp.concatenate([own, swap(own)], axis=0)

    clock = []

    def tick(*xs):
        return lax.optimization_barrier(tuple(xs) + tuple(clock))[: len(xs)]

    def tock(*ys):
        clock[:] = ys

    class Scatter:
        def __init__(self, v, kind=BF16):
            self.kind = kind
            rows, n = v.shape[0] // shards, v.shape[1]
            self.v = v.reshape(f1, f2, cores, rows, n)
            send = lax.dynamic_index_in_dim(self.v, 1 - core, 2, False)
            self.got = [lax.ppermute(send, "shard", [(s, s ^ 1) for s in range(shards)])]

        def step(self, v, at, count, axis, stride):
            keep = lax.dynamic_index_in_dim(v, at, axis, False)
            sends = [lax.dynamic_index_in_dim(v, (at + k) % count, axis, False).astype(self.kind) for k in range(1, count)]
            tock(keep, *sends)
            self.v, self.got = keep, []
            for k in range(1, count):
                perm = [(s, s + ((s // stride + k) % count - s // stride % count) * stride) for s in range(shards)]
                self.got.append(lax.ppermute(sends[k - 1], "shard", perm))

        def sum_core(self):
            v, got = tick(self.v, self.got[0])
            v = widen(lax.dynamic_index_in_dim(v, core, 2, False)) + widen(got)
            self.step(v, i2, f2, 1, cores)

        def sum_two(self):
            v, *got = tick(self.v, *self.got)
            for g in got:
                v = v + widen(g)
            self.step(v, i1, f1, 0, cores * f2)

        def sum_one(self):
            v, *got = tick(self.v, *self.got)
            for g in got:
                v = v + widen(g)
            for k in range(1, groups // 2):
                v = v + lax.ppermute(v, "rep", [(i, (i + 2 * k) % groups) for i in range(groups)])
            send = v.astype(self.kind)
            tock(v, send)
            self.v, self.got = v, swap(send)

        def both(self):
            v, got = tick(self.v, self.got)
            return v, widen(got)

    block = 512
    per_d, per_r = mix_gain.shape[0], conv_bias.shape[0]
    vectors = jnp.concatenate(
        [mix_gain, ffn_gain, conv_kernel.reshape(-1), conv_bias, recur_bias, admit_bias, decay_param]
    )
    count = vectors.shape[0]
    vectors = jnp.pad(vectors, (0, -count % 128)).reshape(-1, 128)
    vectors = lax.all_gather(vectors, "shard", axis=0).reshape(shards, -1)[:, :count]
    gain_one = widen(vectors[:, :per_d].reshape(width))
    gain_two = widen(vectors[:, per_d : 2 * per_d].reshape(width))
    channel = vectors[:, 2 * per_d :].reshape(shards, taps + 4, per_r).transpose(1, 0, 2).reshape(taps + 4, low_r)
    channel = widen(mine(channel, half_r, 1))
    taps_half, cbias = channel[:taps], channel[taps]
    rbias, abias, lam = channel[taps + 1], channel[taps + 2], channel[taps + 3]
    rate = DECAY_SCALE * jax.nn.softplus(-lam)
    params = jnp.concatenate([jnp.stack([rbias, abias, rate]), jnp.zeros((5, half_r), F32)])

    def ffn_half(v):
        return lax.dynamic_index_in_dim(v.reshape(v.shape[0], shards, 2, piece_f), side, 2, False).reshape(v.shape[0], half_f)

    def gather_blocks(parts):
        rows = [p[:, at : at + block] for p in parts for at in range(0, p.shape[1], block)]
        whole = lax.all_gather(jnp.concatenate(rows, axis=0), "shard", axis=0)
        out, at = [], 0
        for p in parts:
            cols = []
            for _ in range(0, p.shape[1], block):
                cols.append(whole[:, at : at + p.shape[0]].reshape(shards * p.shape[0], block))
                at += p.shape[0]
            out.append(jnp.concatenate(cols, axis=1))
        return out

    w1, w2, w3 = gather_blocks([
        jnp.concatenate([mine(branch_proj, half_r, 1), mine(lruin_proj, half_r, 1)], axis=1),
        jnp.concatenate([mine(recur_proj, half_r, 1), mine(admit_proj, half_r, 1)], axis=1),
        out_proj,
    ])
    w4, w5 = gather_blocks([
        jnp.concatenate([ffn_half(ffn_gate), ffn_half(ffn_up)], axis=1),
        mine(ffn_down, piece_f, 0),
    ])

    def norm_back(cot, v, scale, gain):
        g = cot * gain
        return scale * (g - v * (scale * scale * jnp.mean(g * v, axis=-1, keepdims=True)))

    values = widen(with_pair(tokens))
    cot_pair = with_pair(cotangent)
    scale_one = lax.rsqrt(jnp.mean(values * values, axis=-1, keepdims=True) + EPS)
    normed = (values * scale_one * gain_one).astype(BF16)
    pre = matmul(normed, w1)
    lru_pre = pre[:, half_r:].reshape(2, length, half_r)
    conv = cbias
    for k in range(taps):
        conv = conv + taps_half[k] * shifted(lru_pre, k)
    admitted = conv.reshape(2 * length, half_r).astype(BF16)
    admitted_all = natural(admitted, swap_rows(admitted))
    gates = matmul(admitted_all, w2)
    mixed, before = recurrence_forward(pre, gates, admitted, params, length)
    mixed_other = jnp.concatenate([swap(mixed[length:]), swap(mixed[:length])], axis=0)
    mixed_all = natural(mixed, mixed_other)
    middle = widen(tokens) + matmul(mixed_all[:length], w3)
    scale_two = lax.rsqrt(jnp.mean(middle * middle, axis=-1, keepdims=True) + EPS)
    normed_two = with_pair((middle * scale_two * gain_two).astype(BF16))
    wide = matmul(normed_two, w4)
    gate_pre, up_pre = wide[:, :half_f], wide[:, half_f:]
    hidden = (gelu(gate_pre) * up_pre).astype(BF16)

    hidden_cot = cols_product(cot_pair, w5)
    gate_cot = (hidden_cot * up_pre * gelu_slope(gate_pre)).astype(BF16)
    up_cot = (hidden_cot * gelu(gate_pre)).astype(BF16)
    wide_cot = jnp.concatenate([gate_cot, up_cot], axis=1)
    part = cols_product(wide_cot, w4)
    tock(part)
    near, far = part[:length], swap(part[length:].astype(BF16))

    def grad(left, right):
        left, right = tick(left, right)
        out = rows_product(left, right).astype(BF16)
        tock(out)
        return Scatter(out)

    down_s = grad(hidden, cot_pair)
    gate_s = grad(normed_two, gate_cot)
    down_s.sum_core()
    near, far = tick(near, far)
    middle_cot = widen(cotangent) + norm_back(near + widen(far), middle, scale_two, gain_two)
    middle_low = middle_cot.astype(BF16)
    tock(middle_low)
    out_cot = with_pair(middle_low)
    up_s = grad(normed_two, up_cot)
    gate_s.sum_core()
    out_cot, = tick(out_cot)
    mixed_cot = cols_product(out_cot, mine(w3, half_r, 0))
    branch_low, recur_low, admit_low, direct, sums = recurrence_backward(
        mixed_cot, pre, gates, admitted, before, params, length
    )
    gates_cot = jnp.concatenate([recur_low, admit_low], axis=1)
    part = cols_product(gates_cot, w2)
    tock(part)
    near, far = mine(part, half_r, 1), swap_rows(theirs(part, half_r, 1).astype(BF16))
    out_s = grad(mixed_all, mine(out_cot, width // 2, 1))
    down_s.sum_two()
    up_s.sum_core()
    branch_s = grad(normed, branch_low)
    recur_s = grad(admitted_all, recur_low)
    admit_s = grad(admitted_all, admit_low)
    direct, near, far = tick(direct, near, far)
    admitted_cot = (direct + near + widen(far)).reshape(2, length, half_r)
    lru_cot = jnp.zeros_like(admitted_cot)
    kernel_grad = []
    for k in range(taps):
        lru_cot = lru_cot + taps_half[k] * shifted(admitted_cot, -k)
        kernel_grad.append(jnp.sum(admitted_cot * shifted(lru_pre, k), axis=(0, 1)))
    lru_cot = lru_cot.reshape(2 * length, half_r).astype(BF16)
    part = cols_product(jnp.concatenate([branch_low, lru_cot], axis=1), w1)
    tock(part)
    near, far = part[:length], swap(part[length:].astype(BF16))
    lruin_s = grad(normed, lru_cot)
    sums = jnp.sum(sums.reshape(2, 3, ROWS, half_r), axis=(0, 2))
    small = jnp.stack(
        kernel_grad
        + [jnp.sum(admitted_cot, axis=(0, 1)), sums[0], sums[1], sums[2] * (DECAY_SCALE * jax.nn.sigmoid(-lam))]
    )
    small = natural(small, jnp.zeros_like(small))
    small_s = Scatter(small.reshape(taps + 4, shards, per_r).transpose(1, 0, 2).reshape(shards * (taps + 4), per_r), F32)
    gate_s.sum_two()
    out_s.sum_core()
    small_s.sum_core()
    near, far = tick(near, far)
    tokens_grad = middle_cot + norm_back(near + widen(far), values[:length], scale_one[:length], gain_one)
    tock(tokens_grad)
    small_s.sum_two()
    hidden_late, = tick(hidden)
    down = matmul(hidden_late, w5)
    tock(down)
    down_far = swap(down[length:].astype(BF16))
    down_s.sum_one()
    up_s.sum_two()
    branch_s.sum_core()
    small_s.sum_one()
    near, far = tick(down[:length], down_far)
    block_out = (middle + near + widen(far)).astype(BF16)
    tock(block_out)
    gate_s.sum_one()
    a, b = down_s.both()
    ffndown_grad = jnp.concatenate([jnp.where(side == 0, a, b), jnp.where(side == 0, b, a)], axis=0)
    tock(ffndown_grad)
    a, b = small_s.both()
    small = a + b

    def weave(own, other):
        first = jnp.where(side == 0, own, other).reshape(-1, shards, 1, piece_f)
        second = jnp.where(side == 0, other, own).reshape(-1, shards, 1, piece_f)
        return jnp.concatenate([first, second], axis=2).reshape(own.shape[0], 2 * half_f)

    out_s.sum_two()
    recur_s.sum_core()
    up_s.sum_one()
    ffngate_grad = weave(*gate_s.both())
    tock(ffngate_grad)
    branch_s.sum_two()
    admit_s.sum_core()
    out_s.sum_one()
    ffnup_grad = weave(*up_s.both())
    tock(ffnup_grad)
    recur_s.sum_two()
    lruin_s.sum_core()
    branch_s.sum_one()
    outproj_grad = natural(*out_s.both())
    tock(outproj_grad)
    admit_s.sum_two()
    recur_s.sum_one()
    branch_grad = natural(*branch_s.both())
    tock(branch_grad)
    lruin_s.sum_two()
    ffngain_grad = jnp.sum(ffngate_grad * widen(ffn_gate) + ffnup_grad * widen(ffn_up), axis=1) / widen(ffn_gain)
    admit_s.sum_one()
    recur_grad = natural(*recur_s.both())
    tock(recur_grad)
    lruin_s.sum_one()
    admit_grad = natural(*admit_s.both())
    tock(admit_grad)
    lruin_grad = natural(*lruin_s.both())
    mixgain_grad = jnp.sum(branch_grad * widen(branch_proj) + lruin_grad * widen(lruin_proj), axis=1) / widen(mix_gain)
    return (
        block_out, tokens_grad, mixgain_grad, branch_grad, lruin_grad, small[:taps], small[taps], recur_grad,
        small[taps + 1], admit_grad, small[taps + 2], small[taps + 3], outproj_grad, ffngain_grad, ffngate_grad,
        ffnup_grad, ffndown_grad,
    )


def solution(mesh):
    groups, shards = mesh.shape["rep"], mesh.shape["shard"]
    whole = P(("rep", "shard"), None)
    row, vec, col = P("shard", None), P("shard"), P(None, "shard")
    in_specs = (whole, whole, vec, row, row, col, vec, row, vec, row, vec, vec, row, vec, row, row, row)
    out_specs = (whole, whole, vec, row, row, col, vec, row, vec, row, vec, vec, row, vec, row, row, row)
    return jax.shard_map(
        functools.partial(body, groups, shards), mesh=mesh, in_specs=in_specs, out_specs=out_specs, check_vma=False
    )
```

```python
import functools
import math

import jax
import jax.numpy as jnp
from jax import lax
from jax.experimental import pallas as pl
from jax.experimental.pallas import tpu as pltpu
from jax.sharding import PartitionSpec as P

EPS = 1e-06
DECAY_SCALE = 8.0
ROOT_FLOOR = 0.001
GELU_K = math.sqrt(2.0 / math.pi)
GELU_C = 0.044715
ROWS = 16
VMEM = 48 << 20
SMALL = pl.CostEstimate(flops=1024, bytes_accessed=1024, transcendentals=0)
BF16 = jnp.bfloat16
F32 = jnp.float32


def matmul(left, right):
    return jnp.dot(left, right, preferred_element_type=F32)


def rows_product(left, right):
    return lax.dot_general(left, right, (((0,), (0,)), ((), ())), preferred_element_type=F32)


def cols_product(left, right):
    return lax.dot_general(left, right, (((1,), (1,)), ((), ())), preferred_element_type=F32)


def widen(value):
    return value.astype(F32)


def gelu(v):
    return 0.5 * v * (1.0 + jnp.tanh(GELU_K * (v + GELU_C * v * v * v)))


def gelu_slope(v):
    t = jnp.tanh(GELU_K * (v + GELU_C * v * v * v))
    return 0.5 * (1.0 + t) + 0.5 * v * (1.0 - t * t) * GELU_K * (1.0 + 3.0 * GELU_C * v * v)


def forward_kernel(pre_ref, gates_r_ref, gates_i_ref, admitted_ref, params_ref, mixed_ref, before_ref):
    width = pre_ref.shape[1]
    rbias, abias, rate = params_ref[0:1, :], params_ref[1:2, :], params_ref[2:3, :]
    row = lax.broadcasted_iota(jnp.int32, (ROWS, width), 0)

    def step(i, carry):
        at = pl.ds(pl.multiple_of(i * ROWS, ROWS), ROWS)
        gate_r = jax.nn.sigmoid(gates_r_ref[at, :] + rbias)
        gate_i = jax.nn.sigmoid(gates_i_ref[at, :] + abias)
        a = jnp.exp(-(gate_r * rate))
        b = jnp.sqrt(jnp.maximum(1.0 - a * a, ROOT_FLOOR)) * gate_i * widen(admitted_ref[at, :])
        for d in (1, 2, 4, 8):
            keep = row >= d
            b = b + a * jnp.where(keep, pltpu.roll(b, d, 0), 0.0)
            a = a * jnp.where(keep, pltpu.roll(a, d, 0), 1.0)
        state = b + a * carry
        before_ref[at, :] = jnp.where(row >= 1, pltpu.roll(state, 1, 0), carry)
        mixed_ref[at, :] = (state * gelu(pre_ref[at, :])).astype(BF16)
        return jnp.broadcast_to(state[ROWS - 1 : ROWS, :], (ROWS, width))

    lax.fori_loop(0, pre_ref.shape[0] // ROWS, step, jnp.zeros((ROWS, width), F32))


def backward_kernel(
    cot_ref, pre_ref, gates_r_ref, gates_i_ref, admitted_ref, before_ref, params_ref,
    branch_ref, recur_ref, admit_ref, direct_ref, sums_ref,
):
    width = pre_ref.shape[1]
    rbias, abias, rate = params_ref[0:1, :], params_ref[1:2, :], params_ref[2:3, :]
    row = lax.broadcasted_iota(jnp.int32, (ROWS, width), 0)
    blocks = pre_ref.shape[0] // ROWS

    def step(i, state):
        carry, sum_r, sum_i, sum_d = state
        at = pl.ds(pl.multiple_of((blocks - 1 - i) * ROWS, ROWS), ROWS)
        gate_r = jax.nn.sigmoid(gates_r_ref[at, :] + rbias)
        gate_i = jax.nn.sigmoid(gates_i_ref[at, :] + abias)
        admitted = widen(admitted_ref[at, :])
        a = jnp.exp(-(gate_r * rate))
        rest = 1.0 - a * a
        root = jnp.sqrt(jnp.maximum(rest, ROOT_FLOOR))
        before = before_ref[at, :]
        state_now = a * before + root * gate_i * admitted
        pre = pre_ref[at, :]
        cot = cot_ref[at, :]
        branch_ref[at, :] = (cot * state_now * gelu_slope(pre)).astype(BF16)
        own = cot * gelu(pre)
        f = a
        e = a * own
        for d in (1, 2, 4, 8):
            keep = row < ROWS - d
            e = e + f * jnp.where(keep, pltpu.roll(e, ROWS - d, 0), 0.0)
            f = f * jnp.where(keep, pltpu.roll(f, ROWS - d, 0), 1.0)
        e = e + f * carry
        g = own + jnp.where(row < ROWS - 1, pltpu.roll(e, ROWS - 1, 0), carry)
        direct_ref[at, :] = g * root * gate_i
        share = jnp.where(rest > ROOT_FLOOR, 1.0, jnp.where(rest == ROOT_FLOOR, 0.5, 0.0))
        d_log = a * (g * before - g * gate_i * admitted * (share * a / root))
        d_gate_r = -(d_log * rate)
        d_gate_i = g * root * admitted
        recur = d_gate_r * gate_r * (1.0 - gate_r)
        admit = d_gate_i * gate_i * (1.0 - gate_i)
        recur_ref[at, :] = recur.astype(BF16)
        admit_ref[at, :] = admit.astype(BF16)
        carry = jnp.broadcast_to(e[0:1, :], (ROWS, width))
        return carry, sum_r + recur, sum_i + admit, sum_d + d_log * gate_r

    zero = jnp.zeros((ROWS, width), F32)
    _, sum_r, sum_i, sum_d = lax.fori_loop(0, blocks, step, (zero, zero, zero, zero))
    sums_ref[0:ROWS, :] = sum_r
    sums_ref[ROWS : 2 * ROWS, :] = sum_i
    sums_ref[2 * ROWS : 3 * ROWS, :] = sum_d


def recurrence_forward(pre, gates, admitted, params, length):
    tokens, width = admitted.shape
    tile = math.gcd(width, 512)
    n = width // tile
    near = pl.BlockSpec((length, tile), lambda s, j: (s, j))
    far = pl.BlockSpec((length, tile), lambda s, j: (s, j + n))
    vector = pl.BlockSpec((8, tile), lambda s, j: (0, j))
    return pl.pallas_call(
        forward_kernel,
        grid=(tokens // length, n),
        in_specs=[near, near, far, near, vector],
        out_specs=[near, near],
        out_shape=[
            jax.ShapeDtypeStruct((tokens, width), BF16),
            jax.ShapeDtypeStruct((tokens, width), F32),
        ],
        cost_estimate=pl.CostEstimate(flops=60 * tokens * width, bytes_accessed=20 * tokens * width, transcendentals=6 * tokens * width),
        name="recurrence_forward",
    )(pre, gates, gates, admitted, params)


def recurrence_backward(cot, pre, gates, admitted, before, params, length):
    tokens, width = admitted.shape
    tile = math.gcd(width, 512)
    n = width // tile
    near = pl.BlockSpec((length, tile), lambda s, j: (s, j))
    far = pl.BlockSpec((length, tile), lambda s, j: (s, j + n))
    vector = pl.BlockSpec((8, tile), lambda s, j: (0, j))
    low = jax.ShapeDtypeStruct((tokens, width), BF16)
    return pl.pallas_call(
        backward_kernel,
        grid=(tokens // length, n),
        in_specs=[near, near, near, far, near, near, vector],
        out_specs=[near, near, near, near, pl.BlockSpec((3 * ROWS, tile), lambda s, j: (s, j))],
        out_shape=[
            low, low, low,
            jax.ShapeDtypeStruct((tokens, width), F32),
            jax.ShapeDtypeStruct((3 * ROWS * (tokens // length), width), F32),
        ],
        cost_estimate=SMALL,
        name="recurrence_backward",
    )(cot, pre, gates, gates, admitted, before, params)


def ffn_kernel(x_ref, cot_ref, gate_ref, up_ref, down_ref, hidden_ref, gate_cot_ref, up_cot_ref, near_ref, far_ref, sum_ref):
    depth, tile = x_ref.shape[1], gate_ref.shape[2]
    gate_w = gate_ref[...].reshape(depth, tile)
    up_w = up_ref[...].reshape(depth, tile)
    gate = matmul(x_ref[...], gate_w)
    up = matmul(x_ref[...], up_w)
    cot = cols_product(cot_ref[...], down_ref[...])
    t = jnp.tanh(GELU_K * (gate + GELU_C * gate * gate * gate))
    act = 0.5 * gate * (1.0 + t)
    slope = 0.5 * (1.0 + t) + 0.5 * gate * (1.0 - t * t) * GELU_K * (1.0 + 3.0 * GELU_C * gate * gate)
    hidden_ref[...] = (act * up).astype(BF16)
    gate_cot = (cot * up * slope).astype(BF16)
    up_cot = (cot * act).astype(BF16)
    gate_cot_ref[...] = gate_cot
    up_cot_ref[...] = up_cot
    part = cols_product(gate_cot, gate_w) + cols_product(up_cot, up_w)

    @pl.when(pl.program_id(0) == 0)
    def _():
        sum_ref[...] = part

    @pl.when(pl.program_id(0) > 0)
    def _():
        sum_ref[...] += part

    @pl.when(pl.program_id(0) == pl.num_programs(0) - 1)
    def _():
        half = near_ref.shape[0]
        near_ref[...] = sum_ref[:half, :]
        far_ref[...] = sum_ref[half:, :].astype(BF16)


def ffn_pass(x, cot, blocks, down, rows, tiles):
    tokens, depth = x.shape
    shards, _, tile = blocks.shape
    hidden = jax.ShapeDtypeStruct((tokens, tiles * tile), BF16)
    fixed = pl.BlockSpec((tokens, depth), lambda j: (0, 0))
    wide = pl.BlockSpec((tokens, tile), lambda j: (0, j))
    half = pl.BlockSpec((tokens // 2, depth), lambda j: (0, 0))
    return pl.pallas_call(
        ffn_kernel,
        grid=(tiles,),
        in_specs=[
            fixed, fixed,
            pl.BlockSpec((shards, rows, tile), lambda j: (0, j, 0)),
            pl.BlockSpec((shards, rows, tile), lambda j: (0, j + tiles, 0)),
            pl.BlockSpec((tile, depth), lambda j: (j, 0)),
        ],
        out_specs=[wide, wide, wide, half, half],
        out_shape=[
            hidden, hidden, hidden,
            jax.ShapeDtypeStruct((tokens // 2, depth), F32),
            jax.ShapeDtypeStruct((tokens // 2, depth), BF16),
        ],
        scratch_shapes=[pltpu.VMEM((tokens, depth), F32)],
        compiler_params=pltpu.CompilerParams(vmem_limit_bytes=VMEM),
        cost_estimate=SMALL,
        name="ffn_pass",
    )(x, cot, blocks, blocks, down)


def joined(ref):
    v = ref[...]
    if v.shape[1] % 16:
        return widen(v).reshape(-1, v.shape[2]).astype(BF16)
    return v.reshape(-1, v.shape[2])


def away_kernel(at_ref, left_ref, right_ref, out_ref):
    out_ref[...] = matmul(joined(left_ref), right_ref[...]).reshape(out_ref.shape).astype(out_ref.dtype)


def home_kernel(at_ref, left_ref, right_ref, got_ref, keep_ref, send_ref, sum_ref):
    shape = got_ref.shape
    v = matmul(joined(left_ref), right_ref[...]).reshape(shape) + widen(got_ref[...])
    sum_ref[...] = v.reshape(sum_ref.shape)
    n = sum_ref.shape[1]
    keep_ref[...] = sum_ref[:, at_ref[1]]
    for k in range(1, n):
        send_ref[k - 1] = sum_ref[:, lax.rem(at_ref[1] + k, n)].astype(send_ref.dtype)


def column_tile(n):
    return max(t for t in (1024, 768, 512, 256, 128) if n % t == 0)


def grad_away(left, right, at):
    owners, _, rows, tokens = left.shape
    n = right.shape[1]
    tile = column_tile(n)
    return pl.pallas_call(
        away_kernel,
        grid_spec=pltpu.PrefetchScalarGridSpec(
            num_scalar_prefetch=1,
            grid=(n // tile,),
            in_specs=[
                pl.BlockSpec((owners, None, rows, tokens), lambda j, at: (0, at[0], 0, 0)),
                pl.BlockSpec((tokens, tile), lambda j, at: (0, j)),
            ],
            out_specs=pl.BlockSpec((owners, rows, tile), lambda j, at: (0, 0, j)),
        ),
        out_shape=jax.ShapeDtypeStruct((owners, rows, n), BF16),
        compiler_params=pltpu.CompilerParams(vmem_limit_bytes=VMEM),
        cost_estimate=SMALL,
        name="grad_away",
    )(at, left, right)


def grad_home(left, right, got, at, f1, f2):
    owners, _, rows, tokens = left.shape
    n = right.shape[1]
    tile = column_tile(n)
    return pl.pallas_call(
        home_kernel,
        grid_spec=pltpu.PrefetchScalarGridSpec(
            num_scalar_prefetch=1,
            grid=(n // tile,),
            in_specs=[
                pl.BlockSpec((owners, None, rows, tokens), lambda j, at: (0, at[0], 0, 0)),
                pl.BlockSpec((tokens, tile), lambda j, at: (0, j)),
                pl.BlockSpec((owners, rows, tile), lambda j, at: (0, 0, j)),
            ],
            out_specs=[
                pl.BlockSpec((f1, rows, tile), lambda j, at: (0, 0, j)),
                pl.BlockSpec((f2 - 1, f1, rows, tile), lambda j, at: (0, 0, 0, j)),
            ],
            scratch_shapes=[pltpu.VMEM((f1, f2, rows, tile), F32)],
        ),
        out_shape=[
            jax.ShapeDtypeStruct((f1, rows, n), F32),
            jax.ShapeDtypeStruct((f2 - 1, f1, rows, n), BF16),
        ],
        compiler_params=pltpu.CompilerParams(vmem_limit_bytes=VMEM),
        cost_estimate=SMALL,
        name="grad_home",
    )(at, left, right, got)


def spread_kernel(count, gots, at_ref, own_ref, *refs):
    got_refs, keep_ref, send_refs = refs[:gots], refs[gots], refs[gots + 1 :]

    def total(i):
        v = own_ref[i]
        for ref in got_refs:
            v = v + widen(ref[i])
        return v

    keep_ref[...] = total(at_ref[2])
    for k in range(1, count):
        send_refs[k - 1][...] = total(lax.rem(at_ref[2] + k, count)).astype(BF16)


def spread(own, gots, at):
    count, rows, n = own.shape
    tile = column_tile(n)
    many = pl.BlockSpec((count, rows, tile), lambda j, at: (0, 0, j))
    one = pl.BlockSpec((rows, tile), lambda j, at: (0, j))
    out = pl.pallas_call(
        functools.partial(spread_kernel, count, len(gots)),
        grid_spec=pltpu.PrefetchScalarGridSpec(
            num_scalar_prefetch=1, grid=(n // tile,), in_specs=[many] * (1 + len(gots)), out_specs=[one] * count
        ),
        out_shape=[jax.ShapeDtypeStruct((rows, n), F32)] + [jax.ShapeDtypeStruct((rows, n), BF16)] * (count - 1),
        compiler_params=pltpu.CompilerParams(vmem_limit_bytes=VMEM),
        cost_estimate=SMALL,
        name="spread",
    )(at, own, *gots)
    return out[0], out[1:]


def settle_kernel(gots, own_ref, *refs):
    v = own_ref[...]
    for ref in refs[:gots]:
        v = v + widen(ref[...])
    refs[gots][...] = v
    refs[gots + 1][...] = v.astype(BF16)


def settle(own, gots):
    rows, n = own.shape
    tile = column_tile(n)
    one = pl.BlockSpec((rows, tile), lambda j: (0, j))
    return pl.pallas_call(
        functools.partial(settle_kernel, len(gots)),
        grid=(n // tile,),
        in_specs=[one] * (1 + len(gots)),
        out_specs=[one, one],
        out_shape=[jax.ShapeDtypeStruct((rows, n), F32), jax.ShapeDtypeStruct((rows, n), BF16)],
        compiler_params=pltpu.CompilerParams(vmem_limit_bytes=VMEM),
        cost_estimate=SMALL,
        name="settle",
    )(own, *gots)


def shifted(values, offset):
    if offset == 0:
        return values
    if offset > 0:
        return jnp.pad(values, ((0, 0), (offset, 0), (0, 0)))[:, : values.shape[1]]
    return jnp.pad(values, ((0, 0), (0, -offset), (0, 0)))[:, -offset:]


def body(
    groups, shards,
    tokens, cotangent, mix_gain, branch_proj, lruin_proj, conv_kernel, conv_bias, recur_proj, recur_bias,
    admit_proj, admit_bias, decay_param, out_proj, ffn_gain, ffn_gate, ffn_up, ffn_down,
):
    cores = 2
    f2 = 2 ** int(math.log2(math.isqrt(shards // cores)))
    f1 = shards // cores // f2
    side = lax.axis_index("rep") % 2
    here = lax.axis_index("shard")
    core, i2, i1 = here % cores, here // cores % f2, here // (cores * f2)
    taps = conv_kernel.shape[0]
    length, width = tokens.shape
    low_r = branch_proj.shape[1]
    half_r = low_r // 2
    half_f = ffn_gate.shape[1] // 2
    piece_f = half_f // shards

    def swap(v):
        return lax.ppermute(v, "rep", [(i, i ^ 1) for i in range(groups)])

    def swap_rows(v):
        v = swap(v)
        return jnp.concatenate([v[length:], v[:length]], axis=0)

    def mine(v, size, axis):
        return lax.dynamic_slice_in_dim(v, side * size, size, axis)

    def theirs(v, size, axis):
        return lax.dynamic_slice_in_dim(v, (1 - side) * size, size, axis)

    def natural(own, other):
        first = jnp.where(side == 0, own, other)
        second = jnp.where(side == 0, other, own)
        return jnp.concatenate([first, second], axis=-1)

    def with_pair(own):
        return jnp.concatenate([own, swap(own)], axis=0)

    clock = []

    def tick(*xs):
        return lax.optimization_barrier(tuple(xs) + tuple(clock))[: len(xs)]

    def tock(*ys):
        clock[:] = ys

    def along(k, count, stride):
        return [(s, s + ((s // stride + k) % count - s // stride % count) * stride) for s in range(shards)]

    home = jnp.stack([core, i2, i1]).astype(jnp.int32)
    away = jnp.stack([1 - core, i2, i1]).astype(jnp.int32)

    class Scatter:
        def __init__(self, left, right):
            left, self.right = tick(left, right)
            self.left = left.reshape(shards // cores, cores, left.shape[0] // shards, left.shape[1])
            send = grad_away(self.left, self.right, away)
            tock(send)
            self.got = [lax.ppermute(send, "shard", along(1, cores, 1))]

        def sum_core(self):
            left, right, got = tick(self.left, self.right, self.got[0])
            self.v, sends = grad_home(left, right, got, home, f1, f2)
            tock(self.v, sends)
            self.got = [lax.ppermute(sends[k - 1], "shard", along(k, f2, cores)) for k in range(1, f2)]

        def sum_two(self):
            v, *got = tick(self.v, *self.got)
            self.v, sends = spread(v, got, home)
            tock(self.v, *sends)
            self.got = [lax.ppermute(sends[k - 1], "shard", along(k, f1, cores * f2)) for k in range(1, f1)]

        def sum_one(self):
            v, *got = tick(self.v, *self.got)
            v, send = settle(v, got)
            tock(v, send)
            if groups > 2:
                total = v
                for k in range(1, groups // 2):
                    total = total + lax.ppermute(v, "rep", [(i, (i + 2 * k) % groups) for i in range(groups)])
                v, send = total, total.astype(BF16)
            self.v, self.got = v, swap(send)

        def both(self):
            v, got = tick(self.v, self.got)
            return v, widen(got)

    class SmallScatter:
        def __init__(self, v):
            self.v = v.reshape(f1, f2, cores, -1, v.shape[-1])

        def start(self, at, count, axis, stride):
            v = self.v
            sends = [lax.dynamic_index_in_dim(v, (at + k) % count, axis, False) for k in range(1, count)]
            self.v = lax.dynamic_index_in_dim(v, at, axis, False)
            self.got = [lax.ppermute(sends[k - 1], "shard", along(k, count, stride)) for k in range(1, count)]

        def start_pair(self):
            v = self.v
            for k in range(1, groups // 2):
                self.v = self.v + lax.ppermute(v, "rep", [(i, (i + 2 * k) % groups) for i in range(groups)])
            self.got = [swap(self.v)]

        def take(self):
            v, *got = tick(self.v, *self.got)
            for g in got:
                v = v + g
            tock(v)
            self.v = v

    per_d, per_r = mix_gain.shape[0], conv_bias.shape[0]
    vectors = jnp.concatenate(
        [mix_gain, ffn_gain, conv_kernel.reshape(-1), conv_bias, recur_bias, admit_bias, decay_param]
    )
    count = vectors.shape[0]
    vectors = jnp.pad(vectors, (0, -count % 128)).reshape(-1, 128)
    vectors = lax.all_gather(vectors, "shard", axis=0).reshape(shards, -1)[:, :count]
    gain_one = widen(vectors[:, :per_d].reshape(width))
    gain_two = widen(vectors[:, per_d : 2 * per_d].reshape(width))
    channel = vectors[:, 2 * per_d :].reshape(shards, taps + 4, per_r).transpose(1, 0, 2).reshape(taps + 4, low_r)
    channel = widen(mine(channel, half_r, 1))
    taps_half, cbias = channel[:taps], channel[taps]
    rbias, abias, lam = channel[taps + 1], channel[taps + 2], channel[taps + 3]
    rate = DECAY_SCALE * jax.nn.softplus(-lam)
    params = jnp.concatenate([jnp.stack([rbias, abias, rate]), jnp.zeros((5, half_r), F32)])

    def ffn_half(v):
        return lax.dynamic_index_in_dim(v.reshape(v.shape[0], shards, 2, piece_f), side, 2, False).reshape(v.shape[0], half_f)

    def gather_blocks(parts, block):
        rows = [p[:, at : at + block] for p in parts for at in range(0, p.shape[1], block)]
        return lax.all_gather(jnp.concatenate(rows, axis=0), "shard", axis=0)

    def unpack(whole, at, rows, columns):
        block = whole.shape[2]
        cols = [whole[:, at + i * rows : at + (i + 1) * rows].reshape(shards * rows, block) for i in range(columns // block)]
        return jnp.concatenate(cols, axis=1)

    per_f, tiles = 2 * piece_f, 3
    whole = gather_blocks([
        jnp.concatenate([mine(branch_proj, half_r, 1), mine(lruin_proj, half_r, 1)], axis=1),
        jnp.concatenate([mine(recur_proj, half_r, 1), mine(admit_proj, half_r, 1)], axis=1),
        out_proj,
    ], 512)
    ffn_blocks = gather_blocks(
        [ffn_half(ffn_gate), ffn_half(ffn_up), mine(ffn_down, piece_f, 0)], half_f // tiles
    )
    at = low_r // 512 * per_d
    w1 = unpack(whole, 0, per_d, low_r)
    w2 = unpack(whole, at, per_r, low_r)
    w3 = unpack(whole, at + low_r // 512 * per_r, per_r, width)

    def norm_back(cot, v, scale, gain):
        g = cot * gain
        return scale * (g - v * (scale * scale * jnp.mean(g * v, axis=-1, keepdims=True)))

    values = widen(with_pair(tokens))
    cot_pair = with_pair(cotangent)
    scale_one = lax.rsqrt(jnp.mean(values * values, axis=-1, keepdims=True) + EPS)
    normed = (values * scale_one * gain_one).astype(BF16)
    pre = matmul(normed, w1)
    lru_pre = pre[:, half_r:].reshape(2, length, half_r)
    conv = cbias
    for k in range(taps):
        conv = conv + taps_half[k] * shifted(lru_pre, k)
    admitted = conv.reshape(2 * length, half_r).astype(BF16)
    admitted_all = natural(admitted, swap_rows(admitted))
    normed_t, admitted_t = normed.T, admitted_all.T
    gates = matmul(admitted_all, w2)
    mixed, before = recurrence_forward(pre, gates, admitted, params, length)
    mixed_other = jnp.concatenate([swap(mixed[length:]), swap(mixed[:length])], axis=0)
    mixed_all = natural(mixed, mixed_other)
    mixed_all_t = mixed_all.T
    middle = widen(tokens) + matmul(mixed_all[:length], w3)
    scale_two = lax.rsqrt(jnp.mean(middle * middle, axis=-1, keepdims=True) + EPS)
    normed_two = (middle * scale_two * gain_two).astype(BF16)
    tock(normed_two)
    normed_two = with_pair(normed_two)
    ffn_blocks, = tick(ffn_blocks)
    w5 = unpack(ffn_blocks, 2 * tiles * per_d, piece_f, width)

    hidden, gate_cot, up_cot, near, far = ffn_pass(normed_two, cot_pair, ffn_blocks, w5, per_d, tiles)
    tock(near, far)
    far = swap(far)
    down_s = Scatter(hidden.T, cot_pair)
    normed_two_t = normed_two.T
    gate_s = Scatter(normed_two_t, gate_cot)
    down_s.sum_core()
    up_s = Scatter(normed_two_t, up_cot)
    near, far = tick(near, far)
    middle_cot = widen(cotangent) + norm_back(near + widen(far), middle, scale_two, gain_two)
    middle_low = middle_cot.astype(BF16)
    tock(middle_low)
    out_cot = with_pair(middle_low)
    gate_s.sum_core()
    out_cot, = tick(out_cot)
    mixed_cot = cols_product(out_cot, mine(w3, half_r, 0))
    branch_low, recur_low, admit_low, direct, sums = recurrence_backward(
        mixed_cot, pre, gates, admitted, before, params, length
    )
    part = cols_product(jnp.concatenate([recur_low, admit_low], axis=1), w2)
    far = theirs(part, half_r, 1).astype(BF16)
    tock(part, far)
    near, far = mine(part, half_r, 1), swap_rows(far)
    down_s.sum_two()
    up_s.sum_core()
    out_s = Scatter(mixed_all_t, mine(out_cot, width // 2, 1))
    branch_s = Scatter(normed_t, branch_low)
    recur_s = Scatter(admitted_t, recur_low)
    direct, near, far = tick(direct, near, far)
    admitted_cot = (direct + near + widen(far)).reshape(2, length, half_r)
    lru_cot = jnp.zeros_like(admitted_cot)
    kernel_grad = []
    for k in range(taps):
        lru_cot = lru_cot + taps_half[k] * shifted(admitted_cot, -k)
        kernel_grad.append(jnp.sum(admitted_cot * shifted(lru_pre, k), axis=(0, 1)))
    lru_cot = lru_cot.reshape(2 * length, half_r).astype(BF16)
    part = cols_product(jnp.concatenate([branch_low, lru_cot], axis=1), w1)
    far = part[length:].astype(BF16)
    tock(part, far)
    near, far = part[:length], swap(far)
    admit_s = Scatter(admitted_t, admit_low)
    lruin_s = Scatter(normed_t, lru_cot)
    sums = jnp.sum(sums.reshape(2, 3, ROWS, half_r), axis=(0, 2))
    small = jnp.stack(
        kernel_grad
        + [jnp.sum(admitted_cot, axis=(0, 1)), sums[0], sums[1], sums[2] * (DECAY_SCALE * jax.nn.sigmoid(-lam))]
    )
    small = natural(small, jnp.zeros_like(small))
    small_s = SmallScatter(small.reshape(taps + 4, shards, per_r).transpose(1, 0, 2))
    small_s.start(core, cores, 2, 1)
    gate_s.sum_two()
    out_s.sum_core()
    near, far = tick(near, far)
    tokens_grad = middle_cot + norm_back(near + widen(far), values[:length], scale_one[:length], gain_one)
    tock(tokens_grad)
    small_s.take()
    small_s.start(i2, f2, 1, cores)
    hidden_late, = tick(hidden)
    down = matmul(hidden_late, w5)
    down_far = down[length:].astype(BF16)
    tock(down, down_far)
    down_far = swap(down_far)
    down_s.sum_one()
    up_s.sum_two()
    branch_s.sum_core()
    small_s.take()
    small_s.start(i1, f1, 0, cores * f2)
    near, far = tick(down[:length], down_far)
    block_out = (middle + near + widen(far)).astype(BF16)
    tock(block_out)
    gate_s.sum_one()
    out_s.sum_two()
    recur_s.sum_core()
    small_s.take()
    small_s.start_pair()
    a, b = down_s.both()
    ffndown_grad = jnp.concatenate([jnp.where(side == 0, a, b), jnp.where(side == 0, b, a)], axis=0)
    tock(ffndown_grad)

    def weave(own, other):
        first = jnp.where(side == 0, own, other).reshape(-1, shards, 1, piece_f)
        second = jnp.where(side == 0, other, own).reshape(-1, shards, 1, piece_f)
        return jnp.concatenate([first, second], axis=2).reshape(own.shape[0], 2 * half_f)

    branch_s.sum_two()
    admit_s.sum_core()
    up_s.sum_one()
    ffngate_grad = weave(*gate_s.both())
    tock(ffngate_grad)
    recur_s.sum_two()
    lruin_s.sum_core()
    out_s.sum_one()
    ffnup_grad = weave(*up_s.both())
    tock(ffnup_grad)
    small_s.take()
    small = small_s.v.reshape(taps + 4, per_r)
    admit_s.sum_two()
    branch_s.sum_one()
    outproj_grad = natural(*out_s.both())
    tock(outproj_grad)
    lruin_s.sum_two()
    ffngain_grad = jnp.sum(ffngate_grad * widen(ffn_gate) + ffnup_grad * widen(ffn_up), axis=1) / widen(ffn_gain)
    recur_s.sum_one()
    branch_grad = natural(*branch_s.both())
    tock(branch_grad)
    admit_s.sum_one()
    recur_grad = natural(*recur_s.both())
    tock(recur_grad)
    lruin_s.sum_one()
    admit_grad = natural(*admit_s.both())
    tock(admit_grad)
    lruin_grad = natural(*lruin_s.both())
    mixgain_grad = jnp.sum(branch_grad * widen(branch_proj) + lruin_grad * widen(lruin_proj), axis=1) / widen(mix_gain)
    return (
        block_out, tokens_grad, mixgain_grad, branch_grad, lruin_grad, small[:taps], small[taps], recur_grad,
        small[taps + 1], admit_grad, small[taps + 2], small[taps + 3], outproj_grad, ffngain_grad, ffngate_grad,
        ffnup_grad, ffndown_grad,
    )


def solution(mesh):
    groups, shards = mesh.shape["rep"], mesh.shape["shard"]
    whole = P(("rep", "shard"), None)
    row, vec, col = P("shard", None), P("shard"), P(None, "shard")
    in_specs = (whole, whole, vec, row, row, col, vec, row, vec, row, vec, vec, row, vec, row, row, row)
    out_specs = (whole, whole, vec, row, row, col, vec, row, vec, row, vec, vec, row, vec, row, row, row)
    return jax.shard_map(
        functools.partial(body, groups, shards), mesh=mesh, in_specs=in_specs, out_specs=out_specs, check_vma=False
    )
```

```python
import functools
import math

import jax
import jax.numpy as jnp
from jax import lax
from jax.experimental import pallas as pl
from jax.experimental.pallas import tpu as pltpu
from jax.sharding import PartitionSpec as P

EPS = 1e-06
DECAY_SCALE = 8.0
ROOT_FLOOR = 0.001
GELU_K = math.sqrt(2.0 / math.pi)
GELU_C = 0.044715
ROWS = 16
VMEM = 44 << 20
LESS = 24 << 20
SMALL = pl.CostEstimate(flops=1024, bytes_accessed=1024, transcendentals=0)
BF16 = jnp.bfloat16
F32 = jnp.float32


def sent(shape):
    return pltpu.HBM(shape, BF16)


def matmul(left, right):
    return jnp.dot(left, right, preferred_element_type=F32)


def rows_product(left, right):
    return lax.dot_general(left, right, (((0,), (0,)), ((), ())), preferred_element_type=F32)


def cols_product(left, right):
    return lax.dot_general(left, right, (((1,), (1,)), ((), ())), preferred_element_type=F32)


def widen(value):
    return value.astype(F32)


def gelu(v):
    return 0.5 * v * (1.0 + jnp.tanh(GELU_K * (v + GELU_C * v * v * v)))


def gelu_slope(v):
    t = jnp.tanh(GELU_K * (v + GELU_C * v * v * v))
    return 0.5 * (1.0 + t) + 0.5 * v * (1.0 - t * t) * GELU_K * (1.0 + 3.0 * GELU_C * v * v)


def forward_kernel(pre_ref, gates_r_ref, gates_i_ref, admitted_ref, params_ref, mixed_ref, before_ref):
    width = pre_ref.shape[1]
    rbias, abias, rate = params_ref[0:1, :], params_ref[1:2, :], params_ref[2:3, :]
    row = lax.broadcasted_iota(jnp.int32, (ROWS, width), 0)

    def step(i, carry):
        at = pl.ds(pl.multiple_of(i * ROWS, ROWS), ROWS)
        gate_r = jax.nn.sigmoid(gates_r_ref[at, :] + rbias)
        gate_i = jax.nn.sigmoid(gates_i_ref[at, :] + abias)
        a = jnp.exp(-(gate_r * rate))
        b = jnp.sqrt(jnp.maximum(1.0 - a * a, ROOT_FLOOR)) * gate_i * widen(admitted_ref[at, :])
        for d in (1, 2, 4, 8):
            keep = row >= d
            b = b + a * jnp.where(keep, pltpu.roll(b, d, 0), 0.0)
            a = a * jnp.where(keep, pltpu.roll(a, d, 0), 1.0)
        state = b + a * carry
        before_ref[at, :] = jnp.where(row >= 1, pltpu.roll(state, 1, 0), carry)
        mixed_ref[at, :] = (state * gelu(pre_ref[at, :])).astype(BF16)
        return jnp.broadcast_to(state[ROWS - 1 : ROWS, :], (ROWS, width))

    lax.fori_loop(0, pre_ref.shape[0] // ROWS, step, jnp.zeros((ROWS, width), F32))


def chain_kernel(
    side_ref, own_ref, other_ref, out_a_ref, out_b_ref, out_c_ref, recur_w_ref, admit_w_ref, pre_ref, gates_r_ref, gates_i_ref, admitted_ref,
    before_ref, params_ref, branch_ref, gates_cot_ref, direct_ref, sums_ref, near_ref, far_ref, cot_ref, sum_ref,
):
    length = own_ref.shape[0]
    width = pre_ref.shape[1]
    out_w = jnp.concatenate([joined(out_a_ref), joined(out_b_ref), joined(out_c_ref)], axis=1)
    cot_ref[:length, :] = cols_product(own_ref[...], out_w)
    cot_ref[length:, :] = cols_product(other_ref[...], out_w)
    rbias, abias, rate = params_ref[0:1, :], params_ref[1:2, :], params_ref[2:3, :]
    row = lax.broadcasted_iota(jnp.int32, (ROWS, width), 0)
    blocks = length // ROWS
    zero = jnp.zeros((ROWS, width), F32)

    def step(first, i, state):
        carry, sum_r, sum_i, sum_d = state
        at = pl.ds(pl.multiple_of(first + (blocks - 1 - i) * ROWS, ROWS), ROWS)
        gate_r = jax.nn.sigmoid(gates_r_ref[at, :] + rbias)
        gate_i = jax.nn.sigmoid(gates_i_ref[at, :] + abias)
        admitted = widen(admitted_ref[at, :])
        a = jnp.exp(-(gate_r * rate))
        rest = 1.0 - a * a
        root = jnp.sqrt(jnp.maximum(rest, ROOT_FLOOR))
        before = before_ref[at, :]
        state_now = a * before + root * gate_i * admitted
        pre = pre_ref[at, :]
        cot = cot_ref[at, :]
        branch_ref[at, :] = (cot * state_now * gelu_slope(pre)).astype(BF16)
        own = cot * gelu(pre)
        f = a
        e = a * own
        for d in (1, 2, 4, 8):
            keep = row < ROWS - d
            e = e + f * jnp.where(keep, pltpu.roll(e, ROWS - d, 0), 0.0)
            f = f * jnp.where(keep, pltpu.roll(f, ROWS - d, 0), 1.0)
        e = e + f * carry
        g = own + jnp.where(row < ROWS - 1, pltpu.roll(e, ROWS - 1, 0), carry)
        direct_ref[at, :] = g * root * gate_i
        share = jnp.where(rest > ROOT_FLOOR, 1.0, jnp.where(rest == ROOT_FLOOR, 0.5, 0.0))
        d_log = a * (g * before - g * gate_i * admitted * (share * a / root))
        recur = -(d_log * rate) * gate_r * (1.0 - gate_r)
        admit = g * root * admitted * gate_i * (1.0 - gate_i)
        gates_cot_ref[0, at, :] = recur.astype(BF16)
        gates_cot_ref[1, at, :] = admit.astype(BF16)
        carry = jnp.broadcast_to(e[0:1, :], (ROWS, width))
        return carry, sum_r + recur, sum_i + admit, sum_d + d_log * gate_r

    sums = (zero, zero, zero)
    for first in (0, length):
        _, *sums = lax.fori_loop(0, blocks, functools.partial(step, first), (zero, *sums))
    for i in range(3):
        sums_ref[i * ROWS : (i + 1) * ROWS, :] = sums[i]
    depth = sum_ref.shape[1]
    part = cols_product(gates_cot_ref[0], joined(recur_w_ref)) + cols_product(gates_cot_ref[1], joined(admit_w_ref))

    @pl.when(pl.program_id(0) == 0)
    def _():
        sum_ref[...] = part

    @pl.when(pl.program_id(0) > 0)
    def _():
        sum_ref[...] += part

    half = depth // 2
    for side in range(2):
        @pl.when((pl.program_id(0) == pl.num_programs(0) - 1) & (side_ref[0] == side))
        def _(side=side):
            near_ref[...] = sum_ref[:, side * half : (side + 1) * half]
            away = slice((1 - side) * half, (2 - side) * half)
            far_ref[:length, :] = sum_ref[length:, away].astype(BF16)
            far_ref[length:, :] = sum_ref[:length, away].astype(BF16)


def chain_back(side, own, other, whole, at, rows, pre, gates, admitted, before, params):
    length, depth = own.shape
    tokens, width = admitted.shape
    shards, _, tile = whole.shape
    n = width // tile
    at = at // rows
    low = jax.ShapeDtypeStruct((tokens, width), BF16)
    full = pl.BlockSpec((length, depth), lambda j, s: (0, 0))
    near = pl.BlockSpec((tokens, tile), lambda j, s: (0, j))
    fixed = pl.BlockSpec((tokens, width), lambda j, s: (0, 0))
    return pl.pallas_call(
        chain_kernel,
        grid_spec=pltpu.PrefetchScalarGridSpec(
            num_scalar_prefetch=1,
            grid=(n,),
            in_specs=[
                full, full,
                *[
                    pl.BlockSpec((tile // rows, rows, tile), lambda j, s, k=k: (s[0] * n + j, at + 2 * n + k, 0))
                    for k in range(3)
                ],
                pl.BlockSpec((shards, rows, tile), lambda j, s: (0, at + j, 0)),
                pl.BlockSpec((shards, rows, tile), lambda j, s: (0, at + n + j, 0)),
                near, near,
                pl.BlockSpec((tokens, tile), lambda j, s: (0, j + n)),
                near, near,
                pl.BlockSpec((8, tile), lambda j, s: (0, j)),
            ],
            out_specs=[
                near, pl.BlockSpec((2, tokens, tile), lambda j, s: (0, 0, j)), near,
                pl.BlockSpec((3 * ROWS, tile), lambda j, s: (0, j)), fixed, fixed,
            ],
            scratch_shapes=[pltpu.VMEM((tokens, tile), F32), pltpu.VMEM((tokens, 2 * width), F32)],
        ),
        out_shape=[
            low, jax.ShapeDtypeStruct((2, tokens, width), BF16), jax.ShapeDtypeStruct((tokens, width), F32),
            jax.ShapeDtypeStruct((3 * ROWS, width), F32), jax.ShapeDtypeStruct((tokens, width), F32), sent((tokens, width)),
        ],
        compiler_params=pltpu.CompilerParams(vmem_limit_bytes=VMEM),
        cost_estimate=pl.CostEstimate(flops=660000000000, bytes_accessed=1024, transcendentals=0),
        name="chain_back",
    )(side, own, other, *[whole] * 5, pre, gates, gates, admitted, before, params)


def conv_kernel(
    direct_ref, near_in_ref, far_in_ref, lru_ref, branch_ref, taps_ref, branch_w_ref, lruin_w_ref,
    pre_cot_ref, sums_ref, near_ref, far_ref, sum_ref,
):
    tokens, width = direct_ref.shape
    length = tokens // 2
    cot = direct_ref[...] + near_in_ref[...] + widen(far_in_ref[...])
    lru = lru_ref[...]
    token = lax.broadcasted_iota(jnp.int32, (tokens, width), 0)
    token = jnp.where(token >= length, token - length, token)
    total = jnp.zeros_like(cot)
    count = 4
    for k in range(count):
        later = cot if k == 0 else jnp.where(token < length - k, pltpu.roll(cot, tokens - k, 0), 0.0)
        total = total + taps_ref[k : k + 1, :] * later
        sums_ref[k : k + 1, :] = jnp.sum(later * lru, axis=0, keepdims=True)
    sums_ref[count : count + 1, :] = jnp.sum(cot, axis=0, keepdims=True)
    low = total.astype(BF16)
    pre_cot_ref[0] = branch_ref[...]
    pre_cot_ref[1] = low
    part = cols_product(branch_ref[...], joined(branch_w_ref)) + cols_product(low, joined(lruin_w_ref))

    @pl.when(pl.program_id(0) == 0)
    def _():
        sum_ref[...] = part

    @pl.when(pl.program_id(0) > 0)
    def _():
        sum_ref[...] += part

    @pl.when(pl.program_id(0) == pl.num_programs(0) - 1)
    def _():
        near_ref[...] = sum_ref[:length, :]
        far_ref[...] = sum_ref[length:, :].astype(BF16)


def conv_back(direct, near, far, pre, branch, taps, whole, rows, depth):
    tokens, width = direct.shape
    shards, _, tile = whole.shape
    n = width // tile
    one = pl.BlockSpec((tokens, tile), lambda j: (0, j))
    half = pl.BlockSpec((tokens // 2, depth), lambda j: (0, 0))
    return pl.pallas_call(
        conv_kernel,
        grid=(n,),
        in_specs=[
            one, one, one, pl.BlockSpec((tokens, tile), lambda j: (0, j + n)), one,
            pl.BlockSpec((8, tile), lambda j: (0, j)),
            pl.BlockSpec((shards, rows, tile), lambda j: (0, j, 0)),
            pl.BlockSpec((shards, rows, tile), lambda j: (0, n + j, 0)),
        ],
        out_specs=[
            pl.BlockSpec((2, tokens, tile), lambda j: (0, 0, j)), pl.BlockSpec((8, tile), lambda j: (0, j)), half, half,
        ],
        out_shape=[
            jax.ShapeDtypeStruct((2, tokens, width), BF16), jax.ShapeDtypeStruct((8, width), F32),
            jax.ShapeDtypeStruct((tokens // 2, depth), F32), sent((tokens // 2, depth)),
        ],
        scratch_shapes=[pltpu.VMEM((tokens, depth), F32)],
        compiler_params=pltpu.CompilerParams(vmem_limit_bytes=VMEM),
        cost_estimate=pl.CostEstimate(flops=300000000000, bytes_accessed=1024, transcendentals=0),
        name="conv_back",
    )(direct, near, far, pre, branch, taps, whole, whole)


def norm_kernel(near_ref, far_ref, base_ref, v_ref, gain_ref, out_ref, low_ref):
    v = widen(v_ref[...])
    scale = lax.rsqrt(jnp.mean(v * v, axis=-1, keepdims=True) + EPS)
    g = (near_ref[...] + widen(far_ref[...])) * gain_ref[0:1, :]
    out = widen(base_ref[...]) + scale * (g - v * (scale * scale * jnp.mean(g * v, axis=-1, keepdims=True)))
    out_ref[...] = out
    low_ref[...] = out.astype(BF16)


def norm_back(near, far, base, v, gain):
    rows, width = near.shape
    tile = rows // 4
    one = pl.BlockSpec((tile, width), lambda j: (j, 0))
    return pl.pallas_call(
        norm_kernel,
        grid=(rows // tile,),
        in_specs=[one, one, one, one, pl.BlockSpec((8, width), lambda j: (0, 0))],
        out_specs=[one, one],
        out_shape=[jax.ShapeDtypeStruct((rows, width), F32), sent((rows, width))],
        compiler_params=pltpu.CompilerParams(vmem_limit_bytes=LESS),
        cost_estimate=pl.CostEstimate(flops=150000000000, bytes_accessed=1024, transcendentals=0),
        name="norm_back",
    )(near, far, base, v, jnp.broadcast_to(gain, (8, width)))


def flip_kernel(x_ref, out_ref):
    out_ref[...] = widen(x_ref[...]).T.astype(BF16)


def flip(x):
    tokens, n = x.shape
    tile = 256
    return pl.pallas_call(
        flip_kernel,
        grid=(n // tile,),
        in_specs=[pl.BlockSpec((tokens, tile), lambda j: (0, j))],
        out_specs=pl.BlockSpec((tile, tokens), lambda j: (j, 0)),
        out_shape=jax.ShapeDtypeStruct((n, tokens), BF16),
        compiler_params=pltpu.CompilerParams(vmem_limit_bytes=LESS),
        cost_estimate=pl.CostEstimate(flops=150000000000, bytes_accessed=1024, transcendentals=0),
        name="flip",
    )(x)


def pack_kernel(block, side_ref, *refs):
    out_ref, at = refs[-1], 0
    for ref in refs[:-1]:
        rows, n = ref.shape
        for first in range(0, n, block):
            out_ref[at : at + rows, :] = ref[:, first : first + block]
            at += rows


def pack(side, halves, full, block):
    specs = [pl.BlockSpec((p.shape[0], p.shape[1] // 2), lambda j, s: (0, s[0])) for p in halves]
    specs.append(pl.BlockSpec(full.shape, lambda j, s: (0, 0)))
    size = sum(p.shape[0] * p.shape[1] // 2 for p in halves) + full.size
    return pl.pallas_call(
        functools.partial(pack_kernel, block),
        grid_spec=pltpu.PrefetchScalarGridSpec(
            num_scalar_prefetch=1, grid=(1,), in_specs=specs,
            out_specs=pl.BlockSpec((size // block, block), lambda j, s: (0, 0)),
        ),
        out_shape=jax.ShapeDtypeStruct((size // block, block), BF16),
        compiler_params=pltpu.CompilerParams(vmem_limit_bytes=LESS),
        cost_estimate=pl.CostEstimate(flops=30000000000, bytes_accessed=1024, transcendentals=0),
        name="pack",
    )(side, *halves, full)


def columns_kernel(parts, side_ref, own_ref, got_ref, *out_refs):
    n = out_refs[0].shape[1]
    mine = pl.program_id(0) == side_ref[0]

    @pl.when(mine)
    def _():
        for i in range(parts):
            out_refs[i][...] = own_ref[:, i * n : (i + 1) * n]

    @pl.when(jnp.logical_not(mine))
    def _():
        for i in range(parts):
            out_refs[i][...] = widen(got_ref[:, i * n : (i + 1) * n])


def join_columns(side, own, got, parts):
    rows, n = own.shape[0], own.shape[1] // parts
    full = pl.BlockSpec(own.shape, lambda h, s: (0, 0))
    return pl.pallas_call(
        functools.partial(columns_kernel, parts),
        grid_spec=pltpu.PrefetchScalarGridSpec(
            num_scalar_prefetch=1, grid=(2,), in_specs=[full, full],
            out_specs=[pl.BlockSpec((rows, n), lambda h, s: (0, h))] * parts,
        ),
        out_shape=[jax.ShapeDtypeStruct((rows, 2 * n), F32)] * parts,
        compiler_params=pltpu.CompilerParams(vmem_limit_bytes=LESS),
        cost_estimate=pl.CostEstimate(flops=36000000000, bytes_accessed=1024, transcendentals=0),
        name="join_columns",
    )(side, own, got)


def rows_kernel(side_ref, own_a_ref, own_b_ref, got_a_ref, got_b_ref, out_ref):
    n = own_a_ref.shape[1]
    mine = pl.program_id(0) == side_ref[0]

    @pl.when(mine)
    def _():
        out_ref[:, :n] = own_a_ref[...]
        out_ref[:, n:] = own_b_ref[...]

    @pl.when(jnp.logical_not(mine))
    def _():
        out_ref[:, :n] = widen(got_a_ref[...])
        out_ref[:, n:] = widen(got_b_ref[...])


def join_rows(side, a, b):
    rows, n = a[0].shape
    full = pl.BlockSpec((rows, n), lambda h, s: (0, 0))
    return pl.pallas_call(
        rows_kernel,
        grid_spec=pltpu.PrefetchScalarGridSpec(
            num_scalar_prefetch=1, grid=(2,), in_specs=[full] * 4,
            out_specs=pl.BlockSpec((rows, 2 * n), lambda h, s: (h, 0)),
        ),
        out_shape=jax.ShapeDtypeStruct((2 * rows, 2 * n), F32),
        compiler_params=pltpu.CompilerParams(vmem_limit_bytes=LESS),
        cost_estimate=pl.CostEstimate(flops=36000000000, bytes_accessed=1024, transcendentals=0),
        name="join_rows",
    )(side, a[0], b[0], a[1], b[1])


def weave_kernel(piece, side_ref, own_ref, got_ref, out_ref):
    for side in range(2):
        @pl.when(side_ref[0] == side)
        def _(side=side):
            parts = []
            for at in range(0, own_ref.shape[1], piece):
                own = own_ref[:, at : at + piece]
                got = widen(got_ref[:, at : at + piece])
                parts += [got, own] if side else [own, got]
            out_ref[...] = jnp.concatenate(parts, axis=1)


def weave(side, own, got, piece):
    rows, n = own.shape
    return pl.pallas_call(
        functools.partial(weave_kernel, piece),
        grid_spec=pltpu.PrefetchScalarGridSpec(
            num_scalar_prefetch=1, grid=(1,),
            in_specs=[pl.BlockSpec((rows, n), lambda h, s: (0, 0))] * 2,
            out_specs=pl.BlockSpec((rows, 2 * n), lambda h, s: (0, 0)),
        ),
        out_shape=jax.ShapeDtypeStruct((rows, 2 * n), F32),
        compiler_params=pltpu.CompilerParams(vmem_limit_bytes=LESS),
        cost_estimate=pl.CostEstimate(flops=90000000000, bytes_accessed=1024, transcendentals=0),
        name="weave",
    )(side, own, got)


def recurrence_forward(pre, gates, admitted, params, length):
    tokens, width = admitted.shape
    tile = math.gcd(width, 512)
    n = width // tile
    near = pl.BlockSpec((length, tile), lambda s, j: (s, j))
    far = pl.BlockSpec((length, tile), lambda s, j: (s, j + n))
    vector = pl.BlockSpec((8, tile), lambda s, j: (0, j))
    return pl.pallas_call(
        forward_kernel,
        grid=(tokens // length, n),
        in_specs=[near, near, far, near, vector],
        out_specs=[near, near],
        out_shape=[
            jax.ShapeDtypeStruct((tokens, width), BF16),
            jax.ShapeDtypeStruct((tokens, width), F32),
        ],
        cost_estimate=pl.CostEstimate(flops=60 * tokens * width, bytes_accessed=20 * tokens * width, transcendentals=6 * tokens * width),
        name="recurrence_forward",
    )(pre, gates, gates, admitted, params)


def hidden_kernel(x_ref, gate_ref, up_ref, hidden_ref, flipped_ref, act_ref, slope_ref):
    x = x_ref[...]
    gate = matmul(x, joined(gate_ref))
    up = matmul(x, joined(up_ref))
    t = jnp.tanh(GELU_K * (gate + GELU_C * gate * gate * gate))
    act = 0.5 * gate * (1.0 + t)
    slope = 0.5 * (1.0 + t) + 0.5 * gate * (1.0 - t * t) * GELU_K * (1.0 + 3.0 * GELU_C * gate * gate)
    hidden = act * up
    hidden_ref[...] = hidden.astype(BF16)
    flipped_ref[...] = hidden.T.astype(BF16)
    act_ref[...] = act
    slope_ref[...] = up * slope


def hidden_pass(x, blocks, rows, tiles):
    tokens, depth = x.shape
    shards, _, tile = blocks.shape
    n = tiles * tile
    wide = pl.BlockSpec((tokens, tile), lambda j: (0, j))
    return pl.pallas_call(
        hidden_kernel,
        grid=(tiles,),
        in_specs=[
            pl.BlockSpec((tokens, depth), lambda j: (0, 0)),
            pl.BlockSpec((shards, rows, tile), lambda j: (0, j, 0)),
            pl.BlockSpec((shards, rows, tile), lambda j: (0, j + tiles, 0)),
        ],
        out_specs=[wide, pl.BlockSpec((tile, tokens), lambda j: (j, 0)), wide, wide],
        out_shape=[
            jax.ShapeDtypeStruct((tokens, n), BF16), jax.ShapeDtypeStruct((n, tokens), BF16),
            jax.ShapeDtypeStruct((tokens, n), F32), jax.ShapeDtypeStruct((tokens, n), F32),
        ],
        compiler_params=pltpu.CompilerParams(vmem_limit_bytes=VMEM),
        cost_estimate=pl.CostEstimate(flops=420000000000, bytes_accessed=1024, transcendentals=0),
        name="hidden_pass",
    )(x, blocks, blocks)


def halves(sum_ref, part, near_ref, far_ref):
    @pl.when(pl.program_id(0) == 0)
    def _():
        sum_ref[...] = part

    @pl.when(pl.program_id(0) > 0)
    def _():
        sum_ref[...] += part

    @pl.when(pl.program_id(0) == pl.num_programs(0) - 1)
    def _():
        half = near_ref.shape[0]
        near_ref[...] = sum_ref[:half, :]
        far_ref[...] = sum_ref[half:, :].astype(BF16)


def take_tile(down_a_ref, down_b_ref, down_ref):
    rows, n = down_ref.shape[0], down_a_ref.shape[2]
    for j in range(shape_rows(down_a_ref) // rows):
        @pl.when(pl.program_id(0) == j)
        def _(j=j):
            down_ref[:, :n] = joined(down_a_ref)[j * rows : (j + 1) * rows]
            down_ref[:, n:] = joined(down_b_ref)[j * rows : (j + 1) * rows]


def shape_rows(ref):
    return ref.shape[0] * ref.shape[1]


def ffn_back_kernel(
    cot_ref, gate_ref, up_ref, down_a_ref, down_b_ref, act_ref, slope_ref,
    gate_cot_ref, up_cot_ref, near_ref, far_ref, sum_ref, down_ref,
):
    take_tile(down_a_ref, down_b_ref, down_ref)
    cot = cols_product(cot_ref[...], down_ref[...])
    gate_cot = (cot * slope_ref[...]).astype(BF16)
    up_cot = (cot * act_ref[...]).astype(BF16)
    gate_cot_ref[...] = gate_cot
    up_cot_ref[...] = up_cot
    halves(sum_ref, cols_product(gate_cot, joined(gate_ref)) + cols_product(up_cot, joined(up_ref)), near_ref, far_ref)


def down_specs(blocks, rows, tiles, piece):
    shards, _, tile = blocks.shape
    at = 2 * tiles * rows // piece
    return [pl.BlockSpec((shards, piece, tile), lambda j, k=k: (0, at + k, 0), pipeline_mode=pl.Buffered(1)) for k in range(2)]


def ffn_back(cot, blocks, act, slope, rows, tiles, piece):
    tokens, depth = cot.shape
    shards, _, tile = blocks.shape
    low = jax.ShapeDtypeStruct((tokens, tiles * tile), BF16)
    wide = pl.BlockSpec((tokens, tile), lambda j: (0, j))
    half = pl.BlockSpec((tokens // 2, depth), lambda j: (0, 0))
    return pl.pallas_call(
        ffn_back_kernel,
        grid=(tiles,),
        in_specs=[
            pl.BlockSpec((tokens, depth), lambda j: (0, 0)),
            pl.BlockSpec((shards, rows, tile), lambda j: (0, j, 0)),
            pl.BlockSpec((shards, rows, tile), lambda j: (0, j + tiles, 0)),
            *down_specs(blocks, rows, tiles, piece),
            wide, wide,
        ],
        out_specs=[wide, wide, half, half],
        out_shape=[
            low, low,
            jax.ShapeDtypeStruct((tokens // 2, depth), F32), sent((tokens // 2, depth)),
        ],
        scratch_shapes=[pltpu.VMEM((tokens, depth), F32), pltpu.VMEM((tile, depth), BF16)],
        compiler_params=pltpu.CompilerParams(vmem_limit_bytes=VMEM),
        cost_estimate=pl.CostEstimate(flops=690000000000, bytes_accessed=1024, transcendentals=0),
        name="ffn_back",
    )(cot, blocks, blocks, blocks, blocks, act, slope)


def down_kernel(hidden_ref, down_a_ref, down_b_ref, near_ref, far_ref, sum_ref, down_ref):
    take_tile(down_a_ref, down_b_ref, down_ref)
    halves(sum_ref, matmul(hidden_ref[...], down_ref[...]), near_ref, far_ref)


def down_pass(hidden, blocks, depth, rows, tiles, piece):
    tokens, n = hidden.shape
    half = pl.BlockSpec((tokens // 2, depth), lambda j: (0, 0))
    return pl.pallas_call(
        down_kernel,
        grid=(tiles,),
        in_specs=[pl.BlockSpec((tokens, n // tiles), lambda j: (0, j)), *down_specs(blocks, rows, tiles, piece)],
        out_specs=[half, half],
        out_shape=[
            jax.ShapeDtypeStruct((tokens // 2, depth), F32), sent((tokens // 2, depth)),
        ],
        scratch_shapes=[pltpu.VMEM((tokens, depth), F32), pltpu.VMEM((n // tiles, depth), BF16)],
        compiler_params=pltpu.CompilerParams(vmem_limit_bytes=VMEM),
        cost_estimate=pl.CostEstimate(flops=270000000000, bytes_accessed=1024, transcendentals=0),
        name="down_pass",
    )(hidden, blocks, blocks)


def joined(ref):
    v = ref[...]
    if v.shape[1] % 16:
        return widen(v).reshape(-1, v.shape[2]).astype(BF16)
    return v.reshape(-1, v.shape[2])


def away_kernel(at_ref, left_ref, right_ref, out_ref):
    out_ref[...] = matmul(joined(left_ref), right_ref[...]).reshape(out_ref.shape).astype(out_ref.dtype)


def home_kernel(bit, at_ref, left_ref, right_ref, got_ref, keep_ref, send_ref, sum_ref):
    v = matmul(joined(left_ref), right_ref[...]).reshape(got_ref.shape) + widen(got_ref[...])
    sum_ref[...] = v.reshape(sum_ref.shape)
    keep_ref[...] = sum_ref[:, at_ref[bit]]
    send_ref[...] = sum_ref[:, 1 - at_ref[bit]].astype(send_ref.dtype)


def column_tile(n, choices=(1024, 768, 512, 256, 128)):
    return max(t for t in choices if n % t == 0)


def tiling(right, columns, skip):
    parts, _, n = right.shape
    tile = column_tile(columns or n)
    each = n // tile

    def index(j, at):
        at_tile = j + (at[0] if skip < 0 else skip)
        return at_tile // each, 0, at_tile % each

    return tile, columns or parts * n, index


def grad_away(left, right, at, columns=0, skip=0):
    owners, _, rows, tokens = left.shape
    tile, n, index = tiling(right, columns, skip)
    return pl.pallas_call(
        away_kernel,
        grid_spec=pltpu.PrefetchScalarGridSpec(
            num_scalar_prefetch=1,
            grid=(n // tile,),
            in_specs=[
                pl.BlockSpec((owners, None, rows, tokens), lambda j, at: (0, 1 - at[1], 0, 0)),
                pl.BlockSpec((None, tokens, tile), index),
            ],
            out_specs=pl.BlockSpec((owners, rows, tile), lambda j, at: (0, 0, j)),
        ),
        out_shape=sent((owners, rows, n)),
        compiler_params=pltpu.CompilerParams(vmem_limit_bytes=LESS),
        cost_estimate=pl.CostEstimate(flops=105000000000, bytes_accessed=1024, transcendentals=0),
        name="grad_away",
    )(at, left, right)


def grad_home(left, right, got, at, bit, low, columns=0, skip=0):
    owners, _, rows, tokens = left.shape
    tile, n, index = tiling(right, columns, skip)
    high = owners // (2 * low)
    half = pl.BlockSpec((high, low, rows, tile), lambda j, at: (0, 0, 0, j))
    return pl.pallas_call(
        functools.partial(home_kernel, bit),
        grid_spec=pltpu.PrefetchScalarGridSpec(
            num_scalar_prefetch=1,
            grid=(n // tile,),
            in_specs=[
                pl.BlockSpec((owners, None, rows, tokens), lambda j, at: (0, at[1], 0, 0)),
                pl.BlockSpec((None, tokens, tile), index),
                pl.BlockSpec((owners, rows, tile), lambda j, at: (0, 0, j)),
            ],
            out_specs=[half, half],
            scratch_shapes=[pltpu.VMEM((high, 2, low, rows, tile), F32)],
        ),
        out_shape=[
            jax.ShapeDtypeStruct((high, low, rows, n), F32), sent((high, low, rows, n)),
        ],
        compiler_params=pltpu.CompilerParams(vmem_limit_bytes=LESS),
        cost_estimate=pl.CostEstimate(flops=165000000000, bytes_accessed=1024, transcendentals=0),
        name="grad_home",
    )(at, left, right, got)


def fold_kernel(bit, at_ref, own_ref, got_ref, keep_ref, send_ref):
    mine, other = at_ref[bit], 1 - at_ref[bit]
    keep_ref[...] = own_ref[:, mine] + widen(got_ref[:, mine])
    send_ref[...] = (own_ref[:, other] + widen(got_ref[:, other])).astype(BF16)


def fold(own, got, at, bit, low):
    rows, n = own.shape[2:]
    high = own.shape[0] * own.shape[1] // (2 * low)
    tile = column_tile(n, (1024, 768, 512, 256, 128))
    both = pl.BlockSpec((high, 2, low, rows, tile), lambda j, at: (0, 0, 0, 0, j))
    half = pl.BlockSpec((high, low, rows, tile), lambda j, at: (0, 0, 0, j))
    shape = (high, 2, low, rows, n)
    return pl.pallas_call(
        functools.partial(fold_kernel, bit),
        grid_spec=pltpu.PrefetchScalarGridSpec(
            num_scalar_prefetch=1, grid=(n // tile,), in_specs=[both, both], out_specs=[half, half]
        ),
        out_shape=[
            jax.ShapeDtypeStruct((high, low, rows, n), F32), sent((high, low, rows, n)),
        ],
        compiler_params=pltpu.CompilerParams(vmem_limit_bytes=LESS),
        cost_estimate=pl.CostEstimate(flops=75000000000, bytes_accessed=1024, transcendentals=0),
        name="fold",
    )(at, own.reshape(shape), got.reshape(shape))


def settle_kernel(own_ref, got_ref, out_ref, low_ref):
    v = own_ref[...] + widen(got_ref[...])
    out_ref[...] = v
    low_ref[...] = v.astype(BF16)


def settle(own, got):
    rows, n = own.shape
    tile = column_tile(n, (1024, 768, 512, 256, 128))
    one = pl.BlockSpec((rows, tile), lambda j: (0, j))
    return pl.pallas_call(
        settle_kernel,
        grid=(n // tile,),
        in_specs=[one, one],
        out_specs=[one, one],
        out_shape=[jax.ShapeDtypeStruct((rows, n), F32), sent((rows, n))],
        compiler_params=pltpu.CompilerParams(vmem_limit_bytes=LESS),
        cost_estimate=pl.CostEstimate(flops=45000000000, bytes_accessed=1024, transcendentals=0),
        name="settle",
    )(own, got)


def shifted(values, offset):
    if offset == 0:
        return values
    if offset > 0:
        return jnp.pad(values, ((0, 0), (offset, 0), (0, 0)))[:, : values.shape[1]]
    return jnp.pad(values, ((0, 0), (0, -offset), (0, 0)))[:, -offset:]


def body(
    groups, shards,
    tokens, cotangent, mix_gain, branch_proj, lruin_proj, conv_kernel, conv_bias, recur_proj, recur_bias,
    admit_proj, admit_bias, decay_param, out_proj, ffn_gain, ffn_gate, ffn_up, ffn_down,
):
    cores, bits = 2, shards.bit_length() - 1
    side = lax.axis_index("rep") % 2
    here = lax.axis_index("shard")
    taps = conv_kernel.shape[0]
    length, width = tokens.shape
    low_r = branch_proj.shape[1]
    half_r = low_r // 2
    half_f = ffn_gate.shape[1] // 2
    piece_f = half_f // shards

    def swap(v):
        return lax.ppermute(v, "rep", [(i, i ^ 1) for i in range(groups)])

    def swap_rows(v):
        v = swap(v)
        return jnp.concatenate([v[length:], v[:length]], axis=0)

    def mine(v, size, axis):
        return lax.dynamic_slice_in_dim(v, side * size, size, axis)

    def theirs(v, size, axis):
        return lax.dynamic_slice_in_dim(v, (1 - side) * size, size, axis)

    def natural(own, other):
        first = jnp.where(side == 0, own, other)
        second = jnp.where(side == 0, other, own)
        return jnp.concatenate([first, second], axis=-1)

    def with_pair(own):
        return jnp.concatenate([own, swap(own)], axis=0)

    clock = []

    def tick(*xs):
        return lax.optimization_barrier(tuple(xs) + tuple(clock))[: len(xs)]

    def tock(*ys):
        clock[:] = ys

    place = jnp.stack([side] + [(here >> i) & 1 for i in range(bits)]).astype(jnp.int32)
    here_side = place[:1]

    def cross(v, bit):
        return lax.ppermute(v, "shard", [(i, i ^ (1 << bit)) for i in range(shards)])

    class Scatter:
        def __init__(self, left, right, order=None, columns=0, skip=0):
            self.right, = tick(right if right.ndim == 3 else right[None])
            self.left = left.reshape(shards // cores, cores, left.shape[0] // shards, left.shape[1])
            self.order = list(order or range(1, bits))
            self.span = dict(columns=columns, skip=skip)
            send = grad_away(self.left, self.right, place, **self.span)
            tock(send)
            self.got = cross(send, 0)

        def next(self):
            bit, rest = self.order[0], self.order[1:]
            self.order = rest
            return bit, 2 ** sum(other < bit for other in rest)

        def home(self):
            right, got = tick(self.right, self.got)
            bit, low = self.next()
            self.v, send = grad_home(self.left, right, got, place, bit + 1, low, **self.span)
            tock(self.v, send)
            self.got = cross(send, bit)

        def fold(self):
            v, got = tick(self.v, self.got)
            bit, low = self.next()
            self.v, send = fold(v, got, place, bit + 1, low)
            tock(self.v, send)
            self.got = cross(send, bit)

        def two(self):
            while len(self.order) > 1:
                self.fold()

        def settle(self):
            v, got = tick(self.v, self.got)
            v, send = settle(v.reshape(v.shape[2:]), got.reshape(got.shape[2:]))
            tock(v, send)
            if groups > 2:
                total = v
                for k in range(1, groups // 2):
                    total = total + lax.ppermute(v, "rep", [(i, (i + 2 * k) % groups) for i in range(groups)])
                v, send = total, total.astype(BF16)
            self.v, self.got = v, swap(send)

        def both(self):
            return tick(self.v, self.got)

    class SmallScatter:
        def __init__(self, v):
            self.v = v

        def start(self, bit):
            v = self.v.reshape((-1, 2) + self.v.shape[1:]) if bit < bits else self.v
            if bit == bits:
                for k in range(1, groups // 2):
                    self.v = self.v + lax.ppermute(v, "rep", [(i, (i + 2 * k) % groups) for i in range(groups)])
                self.got = swap(self.v)
                return
            self.v = lax.dynamic_index_in_dim(v, (here >> bit) & 1, 1, False)
            self.got = cross(lax.dynamic_index_in_dim(v, 1 - ((here >> bit) & 1), 1, False), bit)

        def take(self):
            v, got = tick(self.v, self.got)
            self.v = v + got
            tock(self.v)

    per_d, per_r = mix_gain.shape[0], conv_bias.shape[0]
    vectors = jnp.concatenate(
        [mix_gain, ffn_gain, conv_kernel.reshape(-1), conv_bias, recur_bias, admit_bias, decay_param]
    )
    count = vectors.shape[0]
    vectors = jnp.pad(vectors, (0, -count % 128)).reshape(-1, 128)
    vectors = lax.all_gather(vectors, "shard", axis=0).reshape(shards, -1)[:, :count]
    gain_one = widen(vectors[:, :per_d].reshape(width))
    gain_two = widen(vectors[:, per_d : 2 * per_d].reshape(width))
    channel = vectors[:, 2 * per_d :].reshape(shards, taps + 4, per_r).transpose(1, 0, 2).reshape(taps + 4, low_r)
    channel = widen(mine(channel, half_r, 1))
    taps_half, cbias = channel[:taps], channel[taps]
    rbias, abias, lam = channel[taps + 1], channel[taps + 2], channel[taps + 3]
    rate = DECAY_SCALE * jax.nn.softplus(-lam)
    params = jnp.concatenate([jnp.stack([rbias, abias, rate]), jnp.zeros((5, half_r), F32)])

    def ffn_half(v):
        return lax.dynamic_index_in_dim(v.reshape(v.shape[0], shards, 2, piece_f), side, 2, False).reshape(v.shape[0], half_f)

    def gather_blocks(parts, block):
        rows = [p[:, at : at + block] for p in parts for at in range(0, p.shape[1], block)]
        return lax.all_gather(jnp.concatenate(rows, axis=0), "shard", axis=0)

    def unpack(whole, at, rows, columns):
        block = whole.shape[2]
        cols = [whole[:, at + i * rows : at + (i + 1) * rows].reshape(shards * rows, block) for i in range(columns // block)]
        return jnp.concatenate(cols, axis=1)

    per_f, tiles = 2 * piece_f, 3
    whole = lax.all_gather(
        pack(here_side, [branch_proj, lruin_proj, recur_proj, admit_proj], out_proj, 512), "shard", axis=0
    )
    ffn_blocks = gather_blocks(
        [ffn_half(ffn_gate), ffn_half(ffn_up), mine(ffn_down, piece_f, 0)], half_f // tiles
    )
    cot_pair = with_pair(cotangent)
    values = widen(with_pair(tokens))
    scale_one = lax.rsqrt(jnp.mean(values * values, axis=-1, keepdims=True) + EPS)
    normed = (values * scale_one * gain_one).astype(BF16)
    normed_t = flip(normed)
    tock(normed_t, cot_pair)
    whole, = tick(whole)
    at = low_r // 512 * per_d
    w1 = unpack(whole, 0, per_d, low_r)
    w2 = unpack(whole, at, per_r, low_r)
    w3 = unpack(whole, at + low_r // 512 * per_r, per_r, width)
    pre = matmul(normed, w1)
    lru_pre = pre[:, half_r:].reshape(2, length, half_r)
    conv = cbias
    for k in range(taps):
        conv = conv + taps_half[k] * shifted(lru_pre, k)
    admitted = conv.reshape(2 * length, half_r).astype(BF16)
    admitted_all = natural(admitted, swap_rows(admitted))
    gates = matmul(admitted_all, w2)
    mixed, before = recurrence_forward(pre, gates, admitted, params, length)
    tock(mixed)
    admitted_all, = tick(admitted_all)
    admitted_t = flip(admitted_all)
    tock(admitted_t)
    mixed_other, = tick(swap(mixed[length:]))
    mixed_own = natural(mixed[:length], mixed_other)
    middle = widen(tokens) + matmul(mixed_own, w3)
    scale_two = lax.rsqrt(jnp.mean(middle * middle, axis=-1, keepdims=True) + EPS)
    normed_two = (middle * scale_two * gain_two).astype(BF16)
    tock(normed_two)
    mixed_late, mixed_far = tick(mixed[length:], swap(mixed[:length]))
    mixed_t = flip(jnp.concatenate([mixed_own, natural(mixed_late, mixed_far)], axis=0))
    tock(mixed_t)
    normed_two = jnp.concatenate([normed_two, *tick(swap(normed_two))], axis=0)
    tock(normed_two)
    ffn_blocks, = tick(ffn_blocks)

    ffn = dict(rows=per_d, tiles=tiles)
    hidden, hidden_t, act, slope = hidden_pass(normed_two, ffn_blocks, **ffn)
    tock(hidden, hidden_t)
    down_a = Scatter(hidden_t, cot_pair, columns=width // 2)
    down_b = Scatter(hidden_t, cot_pair, columns=width // 2, skip=1)
    act, = tick(act)
    gate_cot, up_cot, near, far = ffn_back(cot_pair, ffn_blocks, act, slope, piece=piece_f, **ffn)
    tock(near, far)
    far = swap(far)
    down_a.home()
    down_b.home()
    normed_two, = tick(normed_two)
    normed_two_t = flip(normed_two)
    tock(normed_two_t)
    gate_s = Scatter(normed_two_t, gate_cot)
    near, far = tick(near, far)
    middle_cot, middle_low = norm_back(near, far, cotangent, middle, gain_two)
    tock(middle_cot, middle_low)
    middle_other = swap(middle_low)
    gate_s.home()
    down_a.two()
    up_s = Scatter(normed_two_t, up_cot)
    middle_low, middle_other = tick(middle_low, middle_other)
    branch_low, gates_cot, direct, sums, near, far = chain_back(
        here_side, middle_low, middle_other, whole, at, per_r, pre, gates, admitted, before, params
    )
    tock(near, far)
    far = swap(far)
    down_b.two()
    down_a.fold()
    up_s.home()
    down_b.fold()
    near, far = tick(near, far)
    pre_cot, conv_sums, near, far = conv_back(direct, near, far, pre, branch_low, channel, whole, per_d, width)
    tock(near, far, pre_cot)
    far = swap(far)
    down_a.settle()
    down_b.settle()
    gate_s.two()
    near, far = tick(near, far)
    tokens_grad, _ = norm_back(near, far, middle_cot, tokens, gain_one)
    tock(tokens_grad)
    gates_s = Scatter(admitted_t, gates_cot, [2, 1] + list(range(3, bits)))
    ffndown_grad = join_rows(here_side, down_a.both(), down_b.both())
    tock(ffndown_grad)
    sums = jnp.sum(sums.reshape(3, ROWS, half_r), axis=1)
    small = jnp.concatenate(
        [conv_sums[: taps + 1], sums[:2], sums[2:] * (DECAY_SCALE * jax.nn.sigmoid(-lam))]
    )
    small = natural(small, jnp.zeros_like(small))
    small_s = SmallScatter(small.reshape(taps + 4, shards, per_r).transpose(1, 0, 2))
    small_s.start(0)
    hidden_late, = tick(hidden)
    near, far = down_pass(hidden_late, ffn_blocks, width, piece=piece_f, **ffn)
    tock(near, far)
    far = swap(far)
    small_s.take()
    gates_s.home()
    pre_s = Scatter(normed_t, pre_cot)
    gate_s.fold()
    near, far = tick(near, far)
    block_out = (middle + near + widen(far)).astype(BF16)
    tock(block_out)
    small_s.start(1)
    up_s.two()
    pre_s.home()
    out_s = Scatter(mixed_t, jnp.concatenate([middle_low, middle_other], axis=0), columns=width // 2, skip=-1)
    gate_s.settle()
    up_s.fold()
    ffngate_grad = weave(here_side, *gate_s.both(), piece_f)
    tock(ffngate_grad)
    small_s.take()
    for bit in range(2, bits - 1):
        small_s.start(bit)
        small_s.take()
    out_s.home()
    gates_s.two()
    small_s.start(bits - 1)
    up_s.settle()
    pre_s.two()
    ffnup_grad = weave(here_side, *up_s.both(), piece_f)
    tock(ffnup_grad)
    small_s.take()
    out_s.two()
    small_s.start(bits)
    ffngain_grad = jnp.sum(ffngate_grad * widen(ffn_gate) + ffnup_grad * widen(ffn_up), axis=1) / widen(ffn_gain)
    pre_s.fold()
    gates_s.fold()
    out_s.fold()
    pre_s.settle()
    small_s.take()
    small = small_s.v.reshape(taps + 4, per_r)
    gates_s.settle()
    branch_grad, lruin_grad = join_columns(here_side, *pre_s.both(), 2)
    tock(branch_grad)
    out_s.settle()
    recur_grad, admit_grad = join_columns(here_side, *gates_s.both(), 2)
    tock(recur_grad)
    outproj_grad, = join_columns(here_side, *out_s.both(), 1)
    mixgain_grad = jnp.sum(branch_grad * widen(branch_proj) + lruin_grad * widen(lruin_proj), axis=1) / widen(mix_gain)
    return (
        block_out, tokens_grad, mixgain_grad, branch_grad, lruin_grad, small[:taps], small[taps], recur_grad,
        small[taps + 1], admit_grad, small[taps + 2], small[taps + 3], outproj_grad, ffngain_grad, ffngate_grad,
        ffnup_grad, ffndown_grad,
    )


def solution(mesh):
    groups, shards = mesh.shape["rep"], mesh.shape["shard"]
    whole = P(("rep", "shard"), None)
    row, vec, col = P("shard", None), P("shard"), P(None, "shard")
    in_specs = (whole, whole, vec, row, row, col, vec, row, vec, row, vec, vec, row, vec, row, row, row)
    out_specs = (whole, whole, vec, row, row, col, vec, row, vec, row, vec, vec, row, vec, row, row, row)
    return jax.shard_map(
        functools.partial(body, groups, shards), mesh=mesh, in_specs=in_specs, out_specs=out_specs, check_vma=False
    )
```

```python
import functools
import math

import jax
import jax.numpy as jnp
from jax import lax
from jax.experimental import pallas as pl
from jax.experimental.pallas import tpu as pltpu
from jax.sharding import PartitionSpec as P

EPS = 1e-06
DECAY_SCALE = 8.0
ROOT_FLOOR = 0.001
GELU_K = math.sqrt(2.0 / math.pi)
GELU_C = 0.044715
ROWS = 16
VMEM = 44 << 20
LESS = 24 << 20
STEPS = (
    "hidden", "ffn_in", "turn", "away_u", "away_d", "norm_two", "home_u", "home_d", "mixer", "away_r", "two_u",
    "two_d", "home_r", "away_g", "conv_in", "fold_u", "fold_d", "home_g", "away_b", "away_o", "two_r", "home_b",
    "home_o", "small", "settle_u", "two_g", "fold_r", "join_u", "settle_d", "two_o", "fold_g", "join_d", "down",
    "two_b", "settle_r", "settle_g", "fold_o", "result", "fold_b", "join_r", "settle_o", "norm_one", "small_end",
    "settle_b", "join_g", "join_o", "join_b",
)
HINT = pl.CostEstimate(flops=100000000000, bytes_accessed=1024, transcendentals=0)
BF16 = jnp.bfloat16
F32 = jnp.float32


def sent(shape):
    return pltpu.HBM(shape, BF16)


def matmul(left, right):
    return jnp.dot(left, right, preferred_element_type=F32)


def rows_product(left, right):
    return lax.dot_general(left, right, (((0,), (0,)), ((), ())), preferred_element_type=F32)


def cols_product(left, right):
    return lax.dot_general(left, right, (((1,), (1,)), ((), ())), preferred_element_type=F32)


def widen(value):
    return value.astype(F32)


def gelu(v):
    return 0.5 * v * (1.0 + jnp.tanh(GELU_K * (v + GELU_C * v * v * v)))


def gelu_slope(v):
    t = jnp.tanh(GELU_K * (v + GELU_C * v * v * v))
    return 0.5 * (1.0 + t) + 0.5 * v * (1.0 - t * t) * GELU_K * (1.0 + 3.0 * GELU_C * v * v)


def forward_kernel(pre_ref, gates_r_ref, gates_i_ref, admitted_ref, params_ref, mixed_ref, before_ref):
    width = pre_ref.shape[1]
    rbias, abias, rate = params_ref[0:1, :], params_ref[1:2, :], params_ref[2:3, :]
    row = lax.broadcasted_iota(jnp.int32, (ROWS, width), 0)

    def step(i, carry):
        at = pl.ds(pl.multiple_of(i * ROWS, ROWS), ROWS)
        gate_r = jax.nn.sigmoid(gates_r_ref[at, :] + rbias)
        gate_i = jax.nn.sigmoid(gates_i_ref[at, :] + abias)
        a = jnp.exp(-(gate_r * rate))
        b = jnp.sqrt(jnp.maximum(1.0 - a * a, ROOT_FLOOR)) * gate_i * widen(admitted_ref[at, :])
        for d in (1, 2, 4, 8):
            keep = row >= d
            b = b + a * jnp.where(keep, pltpu.roll(b, d, 0), 0.0)
            a = a * jnp.where(keep, pltpu.roll(a, d, 0), 1.0)
        state = b + a * carry
        before_ref[at, :] = jnp.where(row >= 1, pltpu.roll(state, 1, 0), carry)
        mixed_ref[at, :] = (state * gelu(pre_ref[at, :])).astype(BF16)
        return jnp.broadcast_to(state[ROWS - 1 : ROWS, :], (ROWS, width))

    lax.fori_loop(0, pre_ref.shape[0] // ROWS, step, jnp.zeros((ROWS, width), F32))


def chain_kernel(
    side_ref, own_ref, other_ref, out_a_ref, out_b_ref, out_c_ref, recur_w_ref, admit_w_ref, pre_ref, gates_r_ref, gates_i_ref, admitted_ref,
    before_ref, params_ref, branch_ref, gates_cot_ref, direct_ref, sums_ref, near_ref, far_ref, cot_ref, sum_ref,
):
    length = own_ref.shape[0]
    width = pre_ref.shape[1]
    out_w = jnp.concatenate([joined(out_a_ref), joined(out_b_ref), joined(out_c_ref)], axis=1)
    cot_ref[:length, :] = cols_product(own_ref[...], out_w)
    cot_ref[length:, :] = cols_product(other_ref[...], out_w)
    rbias, abias, rate = params_ref[0:1, :], params_ref[1:2, :], params_ref[2:3, :]
    row = lax.broadcasted_iota(jnp.int32, (ROWS, width), 0)
    blocks = length // ROWS
    zero = jnp.zeros((ROWS, width), F32)

    def step(first, i, state):
        carry, sum_r, sum_i, sum_d = state
        at = pl.ds(pl.multiple_of(first + (blocks - 1 - i) * ROWS, ROWS), ROWS)
        gate_r = jax.nn.sigmoid(gates_r_ref[at, :] + rbias)
        gate_i = jax.nn.sigmoid(gates_i_ref[at, :] + abias)
        admitted = widen(admitted_ref[at, :])
        a = jnp.exp(-(gate_r * rate))
        rest = 1.0 - a * a
        root = jnp.sqrt(jnp.maximum(rest, ROOT_FLOOR))
        before = before_ref[at, :]
        state_now = a * before + root * gate_i * admitted
        pre = pre_ref[at, :]
        cot = cot_ref[at, :]
        branch_ref[at, :] = (cot * state_now * gelu_slope(pre)).astype(BF16)
        own = cot * gelu(pre)
        f = a
        e = a * own
        for d in (1, 2, 4, 8):
            keep = row < ROWS - d
            e = e + f * jnp.where(keep, pltpu.roll(e, ROWS - d, 0), 0.0)
            f = f * jnp.where(keep, pltpu.roll(f, ROWS - d, 0), 1.0)
        e = e + f * carry
        g = own + jnp.where(row < ROWS - 1, pltpu.roll(e, ROWS - 1, 0), carry)
        direct_ref[at, :] = g * root * gate_i
        share = jnp.where(rest > ROOT_FLOOR, 1.0, jnp.where(rest == ROOT_FLOOR, 0.5, 0.0))
        d_log = a * (g * before - g * gate_i * admitted * (share * a / root))
        recur = -(d_log * rate) * gate_r * (1.0 - gate_r)
        admit = g * root * admitted * gate_i * (1.0 - gate_i)
        gates_cot_ref[0, at, :] = recur.astype(BF16)
        gates_cot_ref[1, at, :] = admit.astype(BF16)
        carry = jnp.broadcast_to(e[0:1, :], (ROWS, width))
        return carry, sum_r + recur, sum_i + admit, sum_d + d_log * gate_r

    sums = (zero, zero, zero)
    for first in (0, length):
        _, *sums = lax.fori_loop(0, blocks, functools.partial(step, first), (zero, *sums))
    for i in range(3):
        sums_ref[i * ROWS : (i + 1) * ROWS, :] = sums[i]
    depth = sum_ref.shape[1]
    part = cols_product(gates_cot_ref[0], joined(recur_w_ref)) + cols_product(gates_cot_ref[1], joined(admit_w_ref))

    @pl.when(pl.program_id(0) == 0)
    def _():
        sum_ref[...] = part

    @pl.when(pl.program_id(0) > 0)
    def _():
        sum_ref[...] += part

    half = depth // 2
    for side in range(2):
        @pl.when((pl.program_id(0) == pl.num_programs(0) - 1) & (side_ref[0] == side))
        def _(side=side):
            near_ref[...] = sum_ref[:, side * half : (side + 1) * half]
            away = slice((1 - side) * half, (2 - side) * half)
            far_ref[:length, :] = sum_ref[length:, away].astype(BF16)
            far_ref[length:, :] = sum_ref[:length, away].astype(BF16)


def chain_back(side, own, other, whole, at, rows, pre, gates, admitted, before, params):
    length, depth = own.shape
    tokens, width = admitted.shape
    shards, _, tile = whole.shape
    n = width // tile
    at = at // rows
    low = jax.ShapeDtypeStruct((tokens, width), BF16)
    full = pl.BlockSpec((length, depth), lambda j, s: (0, 0))
    near = pl.BlockSpec((tokens, tile), lambda j, s: (0, j))
    fixed = pl.BlockSpec((tokens, width), lambda j, s: (0, 0))
    return pl.pallas_call(
        chain_kernel,
        grid_spec=pltpu.PrefetchScalarGridSpec(
            num_scalar_prefetch=1,
            grid=(n,),
            in_specs=[
                full, full,
                *[
                    pl.BlockSpec((tile // rows, rows, tile), lambda j, s, k=k: (s[0] * n + j, at + 2 * n + k, 0))
                    for k in range(3)
                ],
                pl.BlockSpec((shards, rows, tile), lambda j, s: (0, at + j, 0)),
                pl.BlockSpec((shards, rows, tile), lambda j, s: (0, at + n + j, 0)),
                near, near,
                pl.BlockSpec((tokens, tile), lambda j, s: (0, j + n)),
                near, near,
                pl.BlockSpec((8, tile), lambda j, s: (0, j)),
            ],
            out_specs=[
                near, pl.BlockSpec((2, tokens, tile), lambda j, s: (0, 0, j)), near,
                pl.BlockSpec((3 * ROWS, tile), lambda j, s: (0, j)), fixed, fixed,
            ],
            scratch_shapes=[pltpu.VMEM((tokens, tile), F32), pltpu.VMEM((tokens, 2 * width), F32)],
        ),
        out_shape=[
            low, jax.ShapeDtypeStruct((2, tokens, width), BF16), jax.ShapeDtypeStruct((tokens, width), F32),
            jax.ShapeDtypeStruct((3 * ROWS, width), F32), jax.ShapeDtypeStruct((tokens, width), F32), sent((tokens, width)),
        ],
        compiler_params=pltpu.CompilerParams(vmem_limit_bytes=VMEM),
        cost_estimate=HINT,
        name="chain_back",
    )(side, own, other, *[whole] * 5, pre, gates, gates, admitted, before, params)


def conv_kernel(
    direct_ref, near_in_ref, far_in_ref, lru_ref, branch_ref, taps_ref, branch_w_ref, lruin_w_ref,
    pre_cot_ref, sums_ref, near_ref, far_ref, sum_ref,
):
    tokens, width = direct_ref.shape
    length = tokens // 2
    cot = direct_ref[...] + near_in_ref[...] + widen(far_in_ref[...])
    lru = lru_ref[...]
    token = lax.broadcasted_iota(jnp.int32, (tokens, width), 0)
    token = jnp.where(token >= length, token - length, token)
    total = jnp.zeros_like(cot)
    count = 4
    for k in range(count):
        later = cot if k == 0 else jnp.where(token < length - k, pltpu.roll(cot, tokens - k, 0), 0.0)
        total = total + taps_ref[k : k + 1, :] * later
        sums_ref[k : k + 1, :] = jnp.sum(later * lru, axis=0, keepdims=True)
    sums_ref[count : count + 1, :] = jnp.sum(cot, axis=0, keepdims=True)
    low = total.astype(BF16)
    pre_cot_ref[0] = branch_ref[...]
    pre_cot_ref[1] = low
    part = cols_product(branch_ref[...], joined(branch_w_ref)) + cols_product(low, joined(lruin_w_ref))

    @pl.when(pl.program_id(0) == 0)
    def _():
        sum_ref[...] = part

    @pl.when(pl.program_id(0) > 0)
    def _():
        sum_ref[...] += part

    @pl.when(pl.program_id(0) == pl.num_programs(0) - 1)
    def _():
        near_ref[...] = sum_ref[:length, :]
        far_ref[...] = sum_ref[length:, :].astype(BF16)


def conv_back(direct, near, far, pre, branch, taps, whole, rows, depth):
    tokens, width = direct.shape
    shards, _, tile = whole.shape
    n = width // tile
    one = pl.BlockSpec((tokens, tile), lambda j: (0, j))
    half = pl.BlockSpec((tokens // 2, depth), lambda j: (0, 0))
    return pl.pallas_call(
        conv_kernel,
        grid=(n,),
        in_specs=[
            one, one, one, pl.BlockSpec((tokens, tile), lambda j: (0, j + n)), one,
            pl.BlockSpec((8, tile), lambda j: (0, j)),
            pl.BlockSpec((shards, rows, tile), lambda j: (0, j, 0)),
            pl.BlockSpec((shards, rows, tile), lambda j: (0, n + j, 0)),
        ],
        out_specs=[
            pl.BlockSpec((2, tokens, tile), lambda j: (0, 0, j)), pl.BlockSpec((8, tile), lambda j: (0, j)), half, half,
        ],
        out_shape=[
            jax.ShapeDtypeStruct((2, tokens, width), BF16), jax.ShapeDtypeStruct((8, width), F32),
            jax.ShapeDtypeStruct((tokens // 2, depth), F32), sent((tokens // 2, depth)),
        ],
        scratch_shapes=[pltpu.VMEM((tokens, depth), F32)],
        compiler_params=pltpu.CompilerParams(vmem_limit_bytes=VMEM),
        cost_estimate=HINT,
        name="conv_back",
    )(direct, near, far, pre, branch, taps, whole, whole)


def norm_kernel(near_ref, far_ref, base_ref, v_ref, gain_ref, out_ref, low_ref):
    v = widen(v_ref[...])
    scale = lax.rsqrt(jnp.mean(v * v, axis=-1, keepdims=True) + EPS)
    g = (near_ref[...] + widen(far_ref[...])) * gain_ref[0:1, :]
    out = widen(base_ref[...]) + scale * (g - v * (scale * scale * jnp.mean(g * v, axis=-1, keepdims=True)))
    out_ref[...] = out
    low_ref[...] = out.astype(BF16)


def norm_back(near, far, base, v, gain):
    rows, width = near.shape
    tile = rows // 4
    one = pl.BlockSpec((tile, width), lambda j: (j, 0))
    return pl.pallas_call(
        norm_kernel,
        grid=(rows // tile,),
        in_specs=[one, one, one, one, pl.BlockSpec((8, width), lambda j: (0, 0))],
        out_specs=[one, one],
        out_shape=[jax.ShapeDtypeStruct((rows, width), F32), sent((rows, width))],
        compiler_params=pltpu.CompilerParams(vmem_limit_bytes=LESS),
        cost_estimate=HINT,
        name="norm_back",
    )(near, far, base, v, jnp.broadcast_to(gain, (8, width)))


def flip_kernel(x_ref, out_ref):
    out_ref[...] = widen(x_ref[...]).T.astype(BF16)


def flip(x):
    tokens, n = x.shape
    tile = 256
    return pl.pallas_call(
        flip_kernel,
        grid=(n // tile,),
        in_specs=[pl.BlockSpec((tokens, tile), lambda j: (0, j))],
        out_specs=pl.BlockSpec((tile, tokens), lambda j: (j, 0)),
        out_shape=jax.ShapeDtypeStruct((n, tokens), BF16),
        compiler_params=pltpu.CompilerParams(vmem_limit_bytes=LESS),
        cost_estimate=HINT,
        name="flip",
    )(x)


def pack_kernel(block, side_ref, *refs):
    out_ref, at = refs[-1], 0
    for ref in refs[:-1]:
        rows, n = ref.shape
        for first in range(0, n, block):
            out_ref[at : at + rows, :] = ref[:, first : first + block]
            at += rows


def pack(side, halves, full, block):
    specs = [pl.BlockSpec((p.shape[0], p.shape[1] // 2), lambda j, s: (0, s[0])) for p in halves]
    specs.append(pl.BlockSpec(full.shape, lambda j, s: (0, 0)))
    size = sum(p.shape[0] * p.shape[1] // 2 for p in halves) + full.size
    return pl.pallas_call(
        functools.partial(pack_kernel, block),
        grid_spec=pltpu.PrefetchScalarGridSpec(
            num_scalar_prefetch=1, grid=(1,), in_specs=specs,
            out_specs=pl.BlockSpec((size // block, block), lambda j, s: (0, 0)),
        ),
        out_shape=jax.ShapeDtypeStruct((size // block, block), BF16),
        compiler_params=pltpu.CompilerParams(vmem_limit_bytes=LESS),
        cost_estimate=HINT,
        name="pack",
    )(side, *halves, full)


def columns_kernel(parts, side_ref, own_ref, got_ref, *out_refs):
    n = out_refs[0].shape[1]
    mine = pl.program_id(0) == side_ref[0]

    @pl.when(mine)
    def _():
        for i in range(parts):
            out_refs[i][...] = own_ref[:, i * n : (i + 1) * n]

    @pl.when(jnp.logical_not(mine))
    def _():
        for i in range(parts):
            out_refs[i][...] = widen(got_ref[:, i * n : (i + 1) * n])


def join_columns(side, own, got, parts):
    rows, n = own.shape[0], own.shape[1] // parts
    full = pl.BlockSpec(own.shape, lambda h, s: (0, 0))
    return pl.pallas_call(
        functools.partial(columns_kernel, parts),
        grid_spec=pltpu.PrefetchScalarGridSpec(
            num_scalar_prefetch=1, grid=(2,), in_specs=[full, full],
            out_specs=[pl.BlockSpec((rows, n), lambda h, s: (0, h))] * parts,
        ),
        out_shape=[jax.ShapeDtypeStruct((rows, 2 * n), F32)] * parts,
        compiler_params=pltpu.CompilerParams(vmem_limit_bytes=LESS),
        cost_estimate=HINT,
        name="join_columns",
    )(side, own, got)


def rows_kernel(side_ref, own_ref, got_ref, out_ref):
    mine = pl.program_id(0) == side_ref[0]

    @pl.when(mine)
    def _():
        out_ref[...] = own_ref[...]

    @pl.when(jnp.logical_not(mine))
    def _():
        out_ref[...] = widen(got_ref[...])


def join_rows(side, own, got):
    rows, n = own.shape
    full = pl.BlockSpec((rows, n), lambda h, s: (0, 0))
    return pl.pallas_call(
        rows_kernel,
        grid_spec=pltpu.PrefetchScalarGridSpec(
            num_scalar_prefetch=1, grid=(2,), in_specs=[full] * 2,
            out_specs=pl.BlockSpec((rows, n), lambda h, s: (h, 0)),
        ),
        out_shape=jax.ShapeDtypeStruct((2 * rows, n), F32),
        compiler_params=pltpu.CompilerParams(vmem_limit_bytes=LESS),
        cost_estimate=HINT,
        name="join_rows",
    )(side, own, got)


def weave_kernel(piece, side_ref, own_ref, got_ref, out_ref):
    for side in range(2):
        @pl.when(side_ref[0] == side)
        def _(side=side):
            parts = []
            for at in range(0, own_ref.shape[1], piece):
                own = own_ref[:, at : at + piece]
                got = widen(got_ref[:, at : at + piece])
                parts += [got, own] if side else [own, got]
            out_ref[...] = jnp.concatenate(parts, axis=1)


def weave(side, own, got, piece):
    rows, n = own.shape
    return pl.pallas_call(
        functools.partial(weave_kernel, piece),
        grid_spec=pltpu.PrefetchScalarGridSpec(
            num_scalar_prefetch=1, grid=(1,),
            in_specs=[pl.BlockSpec((rows, n), lambda h, s: (0, 0))] * 2,
            out_specs=pl.BlockSpec((rows, 2 * n), lambda h, s: (0, 0)),
        ),
        out_shape=jax.ShapeDtypeStruct((rows, 2 * n), F32),
        compiler_params=pltpu.CompilerParams(vmem_limit_bytes=LESS),
        cost_estimate=HINT,
        name="weave",
    )(side, own, got)


def recurrence_forward(pre, gates, admitted, params, length):
    tokens, width = admitted.shape
    tile = math.gcd(width, 512)
    n = width // tile
    near = pl.BlockSpec((length, tile), lambda s, j: (s, j))
    far = pl.BlockSpec((length, tile), lambda s, j: (s, j + n))
    vector = pl.BlockSpec((8, tile), lambda s, j: (0, j))
    return pl.pallas_call(
        forward_kernel,
        grid=(tokens // length, n),
        in_specs=[near, near, far, near, vector],
        out_specs=[near, near],
        out_shape=[
            jax.ShapeDtypeStruct((tokens, width), BF16),
            jax.ShapeDtypeStruct((tokens, width), F32),
        ],
        cost_estimate=pl.CostEstimate(flops=60 * tokens * width, bytes_accessed=20 * tokens * width, transcendentals=6 * tokens * width),
        name="recurrence_forward",
    )(pre, gates, gates, admitted, params)


def hidden_kernel(x_ref, gate_ref, up_ref, hidden_ref, flipped_ref, act_ref, slope_ref):
    x = x_ref[...]
    gate = matmul(x, joined(gate_ref))
    up = matmul(x, joined(up_ref))
    t = jnp.tanh(GELU_K * (gate + GELU_C * gate * gate * gate))
    act = 0.5 * gate * (1.0 + t)
    slope = 0.5 * (1.0 + t) + 0.5 * gate * (1.0 - t * t) * GELU_K * (1.0 + 3.0 * GELU_C * gate * gate)
    hidden = act * up
    hidden_ref[...] = hidden.astype(BF16)
    flipped_ref[...] = hidden.T.astype(BF16)
    act_ref[...] = act
    slope_ref[...] = up * slope


def hidden_pass(x, blocks, rows, tiles):
    tokens, depth = x.shape
    shards, _, tile = blocks.shape
    n = tiles * tile
    wide = pl.BlockSpec((tokens, tile), lambda j: (0, j))
    return pl.pallas_call(
        hidden_kernel,
        grid=(tiles,),
        in_specs=[
            pl.BlockSpec((tokens, depth), lambda j: (0, 0)),
            pl.BlockSpec((shards, rows, tile), lambda j: (0, j, 0)),
            pl.BlockSpec((shards, rows, tile), lambda j: (0, j + tiles, 0)),
        ],
        out_specs=[wide, pl.BlockSpec((tile, tokens), lambda j: (j, 0)), wide, wide],
        out_shape=[
            jax.ShapeDtypeStruct((tokens, n), BF16), jax.ShapeDtypeStruct((n, tokens), BF16),
            jax.ShapeDtypeStruct((tokens, n), F32), jax.ShapeDtypeStruct((tokens, n), F32),
        ],
        compiler_params=pltpu.CompilerParams(vmem_limit_bytes=VMEM),
        cost_estimate=HINT,
        name="hidden_pass",
    )(x, blocks, blocks)


def halves(sum_ref, part, near_ref, far_ref):
    @pl.when(pl.program_id(0) == 0)
    def _():
        sum_ref[...] = part

    @pl.when(pl.program_id(0) > 0)
    def _():
        sum_ref[...] += part

    @pl.when(pl.program_id(0) == pl.num_programs(0) - 1)
    def _():
        half = near_ref.shape[0]
        near_ref[...] = sum_ref[:half, :]
        far_ref[...] = sum_ref[half:, :].astype(BF16)


def take_tile(down_a_ref, down_b_ref, down_ref):
    rows, n = down_ref.shape[0], down_a_ref.shape[2]
    for j in range(shape_rows(down_a_ref) // rows):
        @pl.when(pl.program_id(0) == j)
        def _(j=j):
            down_ref[:, :n] = joined(down_a_ref)[j * rows : (j + 1) * rows]
            down_ref[:, n:] = joined(down_b_ref)[j * rows : (j + 1) * rows]


def shape_rows(ref):
    return ref.shape[0] * ref.shape[1]


def ffn_back_kernel(
    cot_ref, gate_ref, up_ref, down_a_ref, down_b_ref, act_ref, slope_ref,
    gate_cot_ref, up_cot_ref, near_ref, far_ref, sum_ref, down_ref,
):
    take_tile(down_a_ref, down_b_ref, down_ref)
    cot = cols_product(cot_ref[...], down_ref[...])
    gate_cot = (cot * slope_ref[...]).astype(BF16)
    up_cot = (cot * act_ref[...]).astype(BF16)
    gate_cot_ref[...] = gate_cot
    up_cot_ref[...] = up_cot
    halves(sum_ref, cols_product(gate_cot, joined(gate_ref)) + cols_product(up_cot, joined(up_ref)), near_ref, far_ref)


def down_specs(blocks, rows, tiles, piece):
    shards, _, tile = blocks.shape
    at = 2 * tiles * rows // piece
    return [pl.BlockSpec((shards, piece, tile), lambda j, k=k: (0, at + k, 0), pipeline_mode=pl.Buffered(1)) for k in range(2)]


def ffn_back(cot, blocks, act, slope, rows, tiles, piece):
    tokens, depth = cot.shape
    shards, _, tile = blocks.shape
    low = jax.ShapeDtypeStruct((tokens, tiles * tile), BF16)
    wide = pl.BlockSpec((tokens, tile), lambda j: (0, j))
    half = pl.BlockSpec((tokens // 2, depth), lambda j: (0, 0))
    return pl.pallas_call(
        ffn_back_kernel,
        grid=(tiles,),
        in_specs=[
            pl.BlockSpec((tokens, depth), lambda j: (0, 0)),
            pl.BlockSpec((shards, rows, tile), lambda j: (0, j, 0)),
            pl.BlockSpec((shards, rows, tile), lambda j: (0, j + tiles, 0)),
            *down_specs(blocks, rows, tiles, piece),
            wide, wide,
        ],
        out_specs=[wide, wide, half, half],
        out_shape=[
            low, low,
            jax.ShapeDtypeStruct((tokens // 2, depth), F32), sent((tokens // 2, depth)),
        ],
        scratch_shapes=[pltpu.VMEM((tokens, depth), F32), pltpu.VMEM((tile, depth), BF16)],
        compiler_params=pltpu.CompilerParams(vmem_limit_bytes=VMEM),
        cost_estimate=HINT,
        name="ffn_back",
    )(cot, blocks, blocks, blocks, blocks, act, slope)


def down_kernel(hidden_ref, down_a_ref, down_b_ref, near_ref, far_ref, sum_ref, down_ref):
    take_tile(down_a_ref, down_b_ref, down_ref)
    halves(sum_ref, matmul(hidden_ref[...], down_ref[...]), near_ref, far_ref)


def down_pass(hidden, blocks, depth, rows, tiles, piece):
    tokens, n = hidden.shape
    half = pl.BlockSpec((tokens // 2, depth), lambda j: (0, 0))
    return pl.pallas_call(
        down_kernel,
        grid=(tiles,),
        in_specs=[pl.BlockSpec((tokens, n // tiles), lambda j: (0, j)), *down_specs(blocks, rows, tiles, piece)],
        out_specs=[half, half],
        out_shape=[
            jax.ShapeDtypeStruct((tokens // 2, depth), F32), sent((tokens // 2, depth)),
        ],
        scratch_shapes=[pltpu.VMEM((tokens, depth), F32), pltpu.VMEM((n // tiles, depth), BF16)],
        compiler_params=pltpu.CompilerParams(vmem_limit_bytes=VMEM),
        cost_estimate=HINT,
        name="down_pass",
    )(hidden, blocks, blocks)


def joined(ref):
    v = ref[...]
    if v.shape[1] % 16:
        return widen(v).reshape(-1, v.shape[2]).astype(BF16)
    return v.reshape(-1, v.shape[2])


def away_kernel(at_ref, left_ref, right_ref, out_ref):
    out_ref[...] = matmul(joined(left_ref), right_ref[...]).reshape(out_ref.shape).astype(out_ref.dtype)


def home_kernel(bit, at_ref, left_ref, right_ref, got_ref, keep_ref, send_ref, sum_ref):
    v = matmul(joined(left_ref), right_ref[...]).reshape(got_ref.shape) + widen(got_ref[...])
    sum_ref[...] = v.reshape(sum_ref.shape)
    keep_ref[...] = sum_ref[:, at_ref[bit]]
    send_ref[...] = sum_ref[:, 1 - at_ref[bit]].astype(send_ref.dtype)


def column_tile(n, choices=(1024, 768, 512, 256, 128)):
    return max(t for t in choices if n % t == 0)


def tiling(right, columns, skip):
    parts, _, n = right.shape
    tile = column_tile(columns or n)
    each = n // tile

    def index(j, at):
        at_tile = j + (at[0] if skip < 0 else skip)
        return at_tile // each, 0, at_tile % each

    return tile, columns or parts * n, index


def grad_away(left, right, at, columns=0, skip=0):
    owners, _, rows, tokens = left.shape
    tile, n, index = tiling(right, columns, skip)
    return pl.pallas_call(
        away_kernel,
        grid_spec=pltpu.PrefetchScalarGridSpec(
            num_scalar_prefetch=1,
            grid=(n // tile,),
            in_specs=[
                pl.BlockSpec((owners, None, rows, tokens), lambda j, at: (0, 1 - at[1], 0, 0)),
                pl.BlockSpec((None, tokens, tile), index),
            ],
            out_specs=pl.BlockSpec((owners, rows, tile), lambda j, at: (0, 0, j)),
        ),
        out_shape=sent((owners, rows, n)),
        compiler_params=pltpu.CompilerParams(vmem_limit_bytes=LESS),
        cost_estimate=HINT,
        name="grad_away",
    )(at, left, right)


def grad_home(left, right, got, at, bit, low, columns=0, skip=0):
    owners, _, rows, tokens = left.shape
    tile, n, index = tiling(right, columns, skip)
    high = owners // (2 * low)
    half = pl.BlockSpec((high, low, rows, tile), lambda j, at: (0, 0, 0, j))
    return pl.pallas_call(
        functools.partial(home_kernel, bit),
        grid_spec=pltpu.PrefetchScalarGridSpec(
            num_scalar_prefetch=1,
            grid=(n // tile,),
            in_specs=[
                pl.BlockSpec((owners, None, rows, tokens), lambda j, at: (0, at[1], 0, 0)),
                pl.BlockSpec((None, tokens, tile), index),
                pl.BlockSpec((owners, rows, tile), lambda j, at: (0, 0, j)),
            ],
            out_specs=[half, half],
            scratch_shapes=[pltpu.VMEM((high, 2, low, rows, tile), F32)],
        ),
        out_shape=[
            jax.ShapeDtypeStruct((high, low, rows, n), F32), sent((high, low, rows, n)),
        ],
        compiler_params=pltpu.CompilerParams(vmem_limit_bytes=LESS),
        cost_estimate=HINT,
        name="grad_home",
    )(at, left, right, got)


def fold_kernel(bit, at_ref, own_ref, got_ref, keep_ref, send_ref):
    mine, other = at_ref[bit], 1 - at_ref[bit]
    keep_ref[...] = own_ref[:, mine] + widen(got_ref[:, mine])
    send_ref[...] = (own_ref[:, other] + widen(got_ref[:, other])).astype(BF16)


def fold(own, got, at, bit, low):
    rows, n = own.shape[2:]
    high = own.shape[0] * own.shape[1] // (2 * low)
    tile = column_tile(n, (1024, 768, 512, 256, 128))
    both = pl.BlockSpec((high, 2, low, rows, tile), lambda j, at: (0, 0, 0, 0, j))
    half = pl.BlockSpec((high, low, rows, tile), lambda j, at: (0, 0, 0, j))
    shape = (high, 2, low, rows, n)
    return pl.pallas_call(
        functools.partial(fold_kernel, bit),
        grid_spec=pltpu.PrefetchScalarGridSpec(
            num_scalar_prefetch=1, grid=(n // tile,), in_specs=[both, both], out_specs=[half, half]
        ),
        out_shape=[
            jax.ShapeDtypeStruct((high, low, rows, n), F32), sent((high, low, rows, n)),
        ],
        compiler_params=pltpu.CompilerParams(vmem_limit_bytes=LESS),
        cost_estimate=HINT,
        name="fold",
    )(at, own.reshape(shape), got.reshape(shape))


def settle_kernel(own_ref, got_ref, out_ref, low_ref):
    v = own_ref[...] + widen(got_ref[...])
    out_ref[...] = v
    low_ref[...] = v.astype(BF16)


def settle(own, got):
    rows, n = own.shape
    tile = column_tile(n, (1024, 768, 512, 256, 128))
    one = pl.BlockSpec((rows, tile), lambda j: (0, j))
    return pl.pallas_call(
        settle_kernel,
        grid=(n // tile,),
        in_specs=[one, one],
        out_specs=[one, one],
        out_shape=[jax.ShapeDtypeStruct((rows, n), F32), sent((rows, n))],
        compiler_params=pltpu.CompilerParams(vmem_limit_bytes=LESS),
        cost_estimate=HINT,
        name="settle",
    )(own, got)


def shifted(values, offset):
    if offset == 0:
        return values
    if offset > 0:
        return jnp.pad(values, ((0, 0), (offset, 0), (0, 0)))[:, : values.shape[1]]
    return jnp.pad(values, ((0, 0), (0, -offset), (0, 0)))[:, -offset:]


def body(
    groups, shards,
    tokens, cotangent, mix_gain, branch_proj, lruin_proj, conv_kernel, conv_bias, recur_proj, recur_bias,
    admit_proj, admit_bias, decay_param, out_proj, ffn_gain, ffn_gate, ffn_up, ffn_down,
):
    cores, bits = 2, shards.bit_length() - 1
    side = lax.axis_index("rep") % 2
    here = lax.axis_index("shard")
    taps = conv_kernel.shape[0]
    length, width = tokens.shape
    low_r = branch_proj.shape[1]
    half_r = low_r // 2
    half_f = ffn_gate.shape[1] // 2
    piece_f = half_f // shards

    def swap(v):
        return lax.ppermute(v, "rep", [(i, i ^ 1) for i in range(groups)])

    def swap_rows(v):
        v = swap(v)
        return jnp.concatenate([v[length:], v[:length]], axis=0)

    def mine(v, size, axis):
        return lax.dynamic_slice_in_dim(v, side * size, size, axis)

    def theirs(v, size, axis):
        return lax.dynamic_slice_in_dim(v, (1 - side) * size, size, axis)

    def natural(own, other):
        first = jnp.where(side == 0, own, other)
        second = jnp.where(side == 0, other, own)
        return jnp.concatenate([first, second], axis=-1)

    def with_pair(own):
        return jnp.concatenate([own, swap(own)], axis=0)

    clock = []

    def tick(*xs):
        return lax.optimization_barrier(tuple(xs) + tuple(clock))[: len(xs)]

    def tock(*ys):
        clock[:] = ys

    place = jnp.stack([side] + [(here >> i) & 1 for i in range(bits)]).astype(jnp.int32)
    here_side = place[:1]

    def cross(v, bit):
        return lax.ppermute(v, "shard", [(i, i ^ (1 << bit)) for i in range(shards)])

    class Scatter:
        def __init__(self, left, right, order=None, columns=0, skip=0):
            self.right, = tick(right if right.ndim == 3 else right[None])
            self.left = left.reshape(shards // cores, cores, left.shape[0] // shards, left.shape[1])
            self.order = list(order or range(1, bits))
            self.span = dict(columns=columns, skip=skip)
            send = grad_away(self.left, self.right, place, **self.span)
            tock(send)
            self.got = cross(send, 0)

        def next(self):
            bit, rest = self.order[0], self.order[1:]
            self.order = rest
            return bit, 2 ** sum(other < bit for other in rest)

        def home(self):
            right, got = tick(self.right, self.got)
            bit, low = self.next()
            self.v, send = grad_home(self.left, right, got, place, bit + 1, low, **self.span)
            tock(self.v, send)
            self.got = cross(send, bit)

        def fold(self):
            v, got = tick(self.v, self.got)
            bit, low = self.next()
            self.v, send = fold(v, got, place, bit + 1, low)
            tock(self.v, send)
            self.got = cross(send, bit)

        def two(self):
            while len(self.order) > 1:
                self.fold()

        def settle(self):
            v, got = tick(self.v, self.got)
            v, send = settle(v.reshape(v.shape[2:]), got.reshape(got.shape[2:]))
            tock(v, send)
            if groups > 2:
                total = v
                for k in range(1, groups // 2):
                    total = total + lax.ppermute(v, "rep", [(i, (i + 2 * k) % groups) for i in range(groups)])
                v, send = total, total.astype(BF16)
            self.v, self.got = v, swap(send)

        def both(self):
            return tick(self.v, self.got)

    per_d, per_r = mix_gain.shape[0], conv_bias.shape[0]
    vectors = jnp.concatenate(
        [mix_gain, ffn_gain, conv_kernel.reshape(-1), conv_bias, recur_bias, admit_bias, decay_param]
    )
    count = vectors.shape[0]
    vectors = jnp.pad(vectors, (0, -count % 128)).reshape(-1, 128)
    vectors = lax.all_gather(vectors, "shard", axis=0).reshape(shards, -1)[:, :count]
    gain_one = widen(vectors[:, :per_d].reshape(width))
    gain_two = widen(vectors[:, per_d : 2 * per_d].reshape(width))
    channel = vectors[:, 2 * per_d :].reshape(shards, taps + 4, per_r).transpose(1, 0, 2).reshape(taps + 4, low_r)
    channel = widen(mine(channel, half_r, 1))
    taps_half, cbias = channel[:taps], channel[taps]
    rbias, abias, lam = channel[taps + 1], channel[taps + 2], channel[taps + 3]
    rate = DECAY_SCALE * jax.nn.softplus(-lam)
    params = jnp.concatenate([jnp.stack([rbias, abias, rate]), jnp.zeros((5, half_r), F32)])

    def ffn_half(v):
        return lax.dynamic_index_in_dim(v.reshape(v.shape[0], shards, 2, piece_f), side, 2, False).reshape(v.shape[0], half_f)

    def gather_blocks(parts, block):
        rows = [p[:, at : at + block] for p in parts for at in range(0, p.shape[1], block)]
        return lax.all_gather(jnp.concatenate(rows, axis=0), "shard", axis=0)

    def unpack(whole, at, rows, columns):
        block = whole.shape[2]
        cols = [whole[:, at + i * rows : at + (i + 1) * rows].reshape(shards * rows, block) for i in range(columns // block)]
        return jnp.concatenate(cols, axis=1)

    per_f, tiles = 2 * piece_f, 3
    whole = lax.all_gather(
        pack(here_side, [branch_proj, lruin_proj, recur_proj, admit_proj], out_proj, 512), "shard", axis=0
    )
    ffn_blocks = gather_blocks(
        [ffn_half(ffn_gate), ffn_half(ffn_up), mine(ffn_down, piece_f, 0)], half_f // tiles
    )
    cot_pair = with_pair(cotangent)
    values = widen(with_pair(tokens))
    scale_one = lax.rsqrt(jnp.mean(values * values, axis=-1, keepdims=True) + EPS)
    normed = (values * scale_one * gain_one).astype(BF16)
    normed_t = flip(normed)
    tock(normed_t, cot_pair)
    whole, = tick(whole)
    at = low_r // 512 * per_d
    w1 = unpack(whole, 0, per_d, low_r)
    w2 = unpack(whole, at, per_r, low_r)
    w3 = unpack(whole, at + low_r // 512 * per_r, per_r, width)
    pre = matmul(normed, w1)
    lru_pre = pre[:, half_r:].reshape(2, length, half_r)
    conv = cbias
    for k in range(taps):
        conv = conv + taps_half[k] * shifted(lru_pre, k)
    admitted = conv.reshape(2 * length, half_r).astype(BF16)
    admitted_all = natural(admitted, swap_rows(admitted))
    gates = matmul(admitted_all, w2)
    mixed, before = recurrence_forward(pre, gates, admitted, params, length)
    tock(mixed)
    admitted_all, = tick(admitted_all)
    admitted_t = flip(admitted_all)
    tock(admitted_t)
    mixed_other, = tick(swap(mixed[length:]))
    mixed_own = natural(mixed[:length], mixed_other)
    middle = widen(tokens) + matmul(mixed_own, w3)
    scale_two = lax.rsqrt(jnp.mean(middle * middle, axis=-1, keepdims=True) + EPS)
    normed_two = (middle * scale_two * gain_two).astype(BF16)
    tock(normed_two)
    mixed_late, mixed_far = tick(mixed[length:], swap(mixed[:length]))
    mixed_t = flip(jnp.concatenate([mixed_own, natural(mixed_late, mixed_far)], axis=0))
    tock(mixed_t)
    normed_two = jnp.concatenate([normed_two, *tick(swap(normed_two))], axis=0)
    tock(normed_two)
    ffn_blocks, = tick(ffn_blocks)

    ffn = dict(rows=per_d, tiles=tiles)
    have, grads, steps = {}, {}, {}

    def step(run):
        steps[run.__name__] = run
        return run

    @step
    def hidden():
        x, = tick(normed_two)
        have["hidden"], have["hidden_t"], have["act"], have["slope"] = hidden_pass(x, ffn_blocks, **ffn)
        tock(have["hidden"], have["hidden_t"])

    @step
    def ffn_in():
        act, = tick(have["act"])
        have["gate_cot"], have["up_cot"], near, far = ffn_back(
            cot_pair, ffn_blocks, act, have["slope"], piece=piece_f, **ffn
        )
        tock(near, far)
        have["ffn"] = near, swap(far)

    @step
    def turn():
        x, = tick(normed_two)
        have["normed_two_t"] = flip(x)
        tock(have["normed_two_t"])

    @step
    def norm_two():
        near, far = tick(*have["ffn"])
        have["middle_cot"], low = norm_back(near, far, cotangent, middle, gain_two)
        tock(have["middle_cot"], low)
        have["middle_low"] = low, swap(low)

    @step
    def mixer():
        low, other = tick(*have["middle_low"])
        have["branch_low"], have["gates_cot"], have["direct"], have["sums"], near, far = chain_back(
            here_side, low, other, whole, at, per_r, pre, gates, admitted, before, params
        )
        have["out_cot"] = jnp.concatenate([low, other], axis=0)
        tock(near, far)
        have["admitted"] = near, swap(far)

    @step
    def conv_in():
        direct, near, far = tick(have["direct"], *have["admitted"])
        have["pre_cot"], have["conv_sums"], near, far = conv_back(
            direct, near, far, pre, have["branch_low"], channel, whole, per_d, width
        )
        tock(near, far, have["pre_cot"])
        have["normed"] = near, swap(far)

    @step
    def norm_one():
        near, far = tick(*have["normed"])
        have["tokens_grad"], _ = norm_back(near, far, have["middle_cot"], tokens, gain_one)
        tock(have["tokens_grad"])

    @step
    def down():
        x, = tick(have["hidden"])
        near, far = down_pass(x, ffn_blocks, width, piece=piece_f, **ffn)
        tock(near, far)
        have["down"] = near, swap(far)

    @step
    def result():
        near, far = tick(*have["down"])
        have["block_out"] = (middle + near + widen(far)).astype(BF16)
        tock(have["block_out"])

    @step
    def small():
        conv_sums, sums = tick(have["conv_sums"], have["sums"])
        sums = jnp.sum(sums.reshape(3, ROWS, half_r), axis=1)
        v = jnp.concatenate([conv_sums[: taps + 1], sums[:2], sums[2:] * (DECAY_SCALE * jax.nn.sigmoid(-lam))])
        v = natural(v, jnp.zeros_like(v))
        tock(v)
        have["small"] = lax.psum(v, ("rep", "shard"))

    @step
    def small_end():
        v, = tick(have["small"])
        have["small"] = lax.dynamic_slice_in_dim(v, here * per_r, per_r, 1)
        tock(have["small"])

    def late(name, left, right, order=None, **span):
        def away():
            grads[name] = Scatter(left(), right(), order, **span)

        steps["away_" + name] = away
        for stage in ("home", "two", "fold", "settle"):
            steps[stage + "_" + name] = lambda stage=stage: getattr(grads[name], stage)()

    z_first = [2, 1] + list(range(3, bits))
    late("d", lambda: have["hidden_t"], lambda: cot_pair)
    late("g", lambda: have["normed_two_t"], lambda: have["gate_cot"])
    late("u", lambda: have["normed_two_t"], lambda: have["up_cot"], z_first)
    late("r", lambda: admitted_t, lambda: have["gates_cot"])
    late("b", lambda: normed_t, lambda: have["pre_cot"])
    late("o", lambda: mixed_t, lambda: have["out_cot"], columns=width // 2, skip=-1)

    @step
    def join_d():
        v, got = grads["d"].both()
        have["d"] = join_rows(here_side, v, got)
        tock(have["d"])

    @step
    def join_g():
        have["g"] = weave(here_side, *grads["g"].both(), piece_f)
        tock(have["g"])

    @step
    def join_u():
        have["u"] = weave(here_side, *grads["u"].both(), piece_f)
        tock(have["u"])

    @step
    def join_r():
        have["r"] = join_columns(here_side, *grads["r"].both(), 2)
        tock(*have["r"])

    @step
    def join_b():
        have["b"] = join_columns(here_side, *grads["b"].both(), 2)
        tock(*have["b"])

    @step
    def join_o():
        have["o"], = join_columns(here_side, *grads["o"].both(), 1)
        tock(have["o"])

    for name in STEPS:
        steps[name]()
    small_grad, (branch_grad, lruin_grad) = have["small"], have["b"]
    ffngain_grad = jnp.sum(have["g"] * widen(ffn_gate) + have["u"] * widen(ffn_up), axis=1) / widen(ffn_gain)
    mixgain_grad = jnp.sum(branch_grad * widen(branch_proj) + lruin_grad * widen(lruin_proj), axis=1) / widen(mix_gain)
    return (
        have["block_out"], have["tokens_grad"], mixgain_grad, branch_grad, lruin_grad, small_grad[:taps],
        small_grad[taps], have["r"][0], small_grad[taps + 1], have["r"][1], small_grad[taps + 2],
        small_grad[taps + 3], have["o"], ffngain_grad, have["g"], have["u"], have["d"],
    )


def solution(mesh):
    groups, shards = mesh.shape["rep"], mesh.shape["shard"]
    whole = P(("rep", "shard"), None)
    row, vec, col = P("shard", None), P("shard"), P(None, "shard")
    in_specs = (whole, whole, vec, row, row, col, vec, row, vec, row, vec, vec, row, vec, row, row, row)
    out_specs = (whole, whole, vec, row, row, col, vec, row, vec, row, vec, vec, row, vec, row, row, row)
    return jax.shard_map(
        functools.partial(body, groups, shards), mesh=mesh, in_specs=in_specs, out_specs=out_specs, check_vma=False
    )
```

```python
import functools
import math

import jax
import jax.numpy as jnp
from jax import lax
from jax.experimental import pallas as pl
from jax.experimental.pallas import tpu as pltpu
from jax.sharding import PartitionSpec as P

EPS = 1e-06
DECAY_SCALE = 8.0
ROOT_FLOOR = 0.001
GELU_K = math.sqrt(2.0 / math.pi)
GELU_C = 0.044715
ROWS = 16
FACTORS = 7
VMEM = 44 << 20
LESS = 24 << 20
STEPS = (
    "hidden", "ffn_in", "turn", "away_u", "away_d", "norm_two", "home_u", "home_d", "away_g", "mixer", "away_r",
    "two_u", "two_d", "home_g", "home_r", "conv_in", "fold_u", "fold_d", "away_b", "small", "settle_u", "down",
    "home_b", "norm_one", "two_g", "two_r", "join_u", "away_o", "two_b", "fold_g", "settle_d", "home_o", "fold_r",
    "settle_g", "join_d", "two_o", "fold_b", "join_g", "settle_r", "small_end", "fold_o", "settle_b", "result",
    "join_r", "settle_o", "join_b", "join_o",
)
HINT = pl.CostEstimate(flops=100000000000, bytes_accessed=1024, transcendentals=0)
BF16 = jnp.bfloat16
F32 = jnp.float32
KEEP = BF16


def sent(shape):
    return pltpu.HBM(shape, BF16)


def matmul(left, right):
    return jnp.dot(left, right, preferred_element_type=F32)


def rows_product(left, right):
    return lax.dot_general(left, right, (((0,), (0,)), ((), ())), preferred_element_type=F32)


def cols_product(left, right):
    return lax.dot_general(left, right, (((1,), (1,)), ((), ())), preferred_element_type=F32)


def widen(value):
    return value.astype(F32)


def gelu(v):
    return 0.5 * v * (1.0 + jnp.tanh(GELU_K * (v + GELU_C * v * v * v)))


def gelu_slope(v):
    t = jnp.tanh(GELU_K * (v + GELU_C * v * v * v))
    return 0.5 * (1.0 + t) + 0.5 * v * (1.0 - t * t) * GELU_K * (1.0 + 3.0 * GELU_C * v * v)


def forward_kernel(pre_ref, gates_r_ref, gates_i_ref, admitted_ref, params_ref, mixed_ref, *factor_refs):
    width = pre_ref.shape[1]
    rbias, abias, rate = params_ref[0:1, :], params_ref[1:2, :], params_ref[2:3, :]
    row = lax.broadcasted_iota(jnp.int32, (ROWS, width), 0)

    def step(i, carry):
        at = pl.ds(pl.multiple_of(i * ROWS, ROWS), ROWS)
        gate_r = jax.nn.sigmoid(gates_r_ref[at, :] + rbias)
        gate_i = jax.nn.sigmoid(gates_i_ref[at, :] + abias)
        admitted = widen(admitted_ref[at, :])
        decay = jnp.exp(-(gate_r * rate))
        rest = 1.0 - decay * decay
        root = jnp.sqrt(jnp.maximum(rest, ROOT_FLOOR))
        through = root * gate_i
        a, b = decay, through * admitted
        for d in (1, 2, 4, 8):
            keep = row >= d
            b = b + a * jnp.where(keep, pltpu.roll(b, d, 0), 0.0)
            a = a * jnp.where(keep, pltpu.roll(a, d, 0), 1.0)
        state = b + a * carry
        before = jnp.where(row >= 1, pltpu.roll(state, 1, 0), carry)
        pre = pre_ref[at, :]
        t = jnp.tanh(GELU_K * (pre + GELU_C * pre * pre * pre))
        act = 0.5 * pre * (1.0 + t)
        slope = 0.5 * (1.0 + t) + 0.5 * pre * (1.0 - t * t) * GELU_K * (1.0 + 3.0 * GELU_C * pre * pre)
        mixed_ref[at, :] = (state * act).astype(BF16)
        share = jnp.where(rest > ROOT_FLOOR, 1.0, jnp.where(rest == ROOT_FLOOR, 0.5, 0.0))
        log = decay * (before - gate_i * admitted * (share * decay / root))
        factors = (
            decay, act, state * slope, through, through * admitted * (1.0 - gate_i),
            -(log * rate) * gate_r * (1.0 - gate_r), log * gate_r,
        )
        for ref, factor in zip(factor_refs, factors, strict=True):
            ref[at, :] = factor
        return jnp.broadcast_to(state[ROWS - 1 : ROWS, :], (ROWS, width))

    lax.fori_loop(0, pre_ref.shape[0] // ROWS, step, jnp.zeros((ROWS, width), F32))


def chain_kernel(
    side_ref, own_ref, other_ref, out_a_ref, out_b_ref, out_c_ref, recur_w_ref, admit_w_ref, decay_ref, act_ref,
    branch_f_ref, direct_f_ref, admit_f_ref, recur_f_ref, rate_f_ref,
    branch_ref, gates_cot_ref, direct_ref, sums_ref, near_ref, far_ref, cot_ref, sum_ref,
):
    length = own_ref.shape[0]
    width = act_ref.shape[1]
    out_w = jnp.concatenate([joined(out_a_ref), joined(out_b_ref), joined(out_c_ref)], axis=1)
    cot_ref[:length, :] = cols_product(own_ref[...], out_w)
    cot_ref[length:, :] = cols_product(other_ref[...], out_w)
    row = lax.broadcasted_iota(jnp.int32, (ROWS, width), 0)
    blocks = length // ROWS
    zero = jnp.zeros((ROWS, width), F32)

    def step(first, i, state):
        carry, sum_r, sum_i, sum_d = state
        at = pl.ds(pl.multiple_of(first + (blocks - 1 - i) * ROWS, ROWS), ROWS)
        cot = cot_ref[at, :]
        branch_ref[at, :] = (cot * branch_f_ref[at, :]).astype(BF16)
        own = cot * act_ref[at, :]
        f = decay_ref[at, :]
        e = f * own
        for d in (1, 2, 4, 8):
            keep = row < ROWS - d
            e = e + f * jnp.where(keep, pltpu.roll(e, ROWS - d, 0), 0.0)
            f = f * jnp.where(keep, pltpu.roll(f, ROWS - d, 0), 1.0)
        e = e + f * carry
        g = own + jnp.where(row < ROWS - 1, pltpu.roll(e, ROWS - 1, 0), carry)
        direct_ref[at, :] = g * direct_f_ref[at, :]
        recur = g * recur_f_ref[at, :]
        admit = g * admit_f_ref[at, :]
        gates_cot_ref[0, at, :] = recur.astype(BF16)
        gates_cot_ref[1, at, :] = admit.astype(BF16)
        carry = jnp.broadcast_to(e[0:1, :], (ROWS, width))
        return carry, sum_r + recur, sum_i + admit, sum_d + g * rate_f_ref[at, :]

    sums = (zero, zero, zero)
    for first in (0, length):
        _, *sums = lax.fori_loop(0, blocks, functools.partial(step, first), (zero, *sums))
    for i in range(3):
        sums_ref[i * ROWS : (i + 1) * ROWS, :] = sums[i]
    depth = sum_ref.shape[1]
    part = cols_product(gates_cot_ref[0], joined(recur_w_ref)) + cols_product(gates_cot_ref[1], joined(admit_w_ref))

    @pl.when(pl.program_id(0) == 0)
    def _():
        sum_ref[...] = part

    @pl.when(pl.program_id(0) > 0)
    def _():
        sum_ref[...] += part

    half = depth // 2
    for side in range(2):
        @pl.when((pl.program_id(0) == pl.num_programs(0) - 1) & (side_ref[0] == side))
        def _(side=side):
            near_ref[...] = sum_ref[:, side * half : (side + 1) * half]
            away = slice((1 - side) * half, (2 - side) * half)
            far_ref[:length, :] = sum_ref[length:, away].astype(BF16)
            far_ref[length:, :] = sum_ref[:length, away].astype(BF16)


def chain_back(side, own, other, whole, at, rows, factors):
    length, depth = own.shape
    tokens, width = factors[0].shape
    shards, _, tile = whole.shape
    n = width // tile
    at = at // rows
    low = jax.ShapeDtypeStruct((tokens, width), BF16)
    full = pl.BlockSpec((length, depth), lambda j, s: (0, 0))
    near = pl.BlockSpec((tokens, tile), lambda j, s: (0, j))
    fixed = pl.BlockSpec((tokens, width), lambda j, s: (0, 0))
    return pl.pallas_call(
        chain_kernel,
        grid_spec=pltpu.PrefetchScalarGridSpec(
            num_scalar_prefetch=1,
            grid=(n,),
            in_specs=[
                full, full,
                *[
                    pl.BlockSpec((tile // rows, rows, tile), lambda j, s, k=k: (s[0] * n + j, at + 2 * n + k, 0))
                    for k in range(3)
                ],
                pl.BlockSpec((shards, rows, tile), lambda j, s: (0, at + j, 0)),
                pl.BlockSpec((shards, rows, tile), lambda j, s: (0, at + n + j, 0)),
                *[near] * FACTORS,
            ],
            out_specs=[
                near, pl.BlockSpec((2, tokens, tile), lambda j, s: (0, 0, j)), near,
                pl.BlockSpec((3 * ROWS, tile), lambda j, s: (0, j)), fixed, fixed,
            ],
            scratch_shapes=[pltpu.VMEM((tokens, tile), F32), pltpu.VMEM((tokens, 2 * width), F32)],
        ),
        out_shape=[
            low, jax.ShapeDtypeStruct((2, tokens, width), BF16), jax.ShapeDtypeStruct((tokens, width), F32),
            jax.ShapeDtypeStruct((3 * ROWS, width), F32), jax.ShapeDtypeStruct((tokens, width), F32), sent((tokens, width)),
        ],
        compiler_params=pltpu.CompilerParams(vmem_limit_bytes=VMEM),
        cost_estimate=HINT,
        name="chain_back",
    )(side, own, other, *[whole] * 5, *factors)


def conv_kernel(
    direct_ref, near_in_ref, far_in_ref, lru_ref, branch_ref, taps_ref, branch_w_ref, lruin_w_ref,
    pre_cot_ref, sums_ref, near_ref, far_ref, sum_ref,
):
    tokens, width = direct_ref.shape
    length = tokens // 2
    cot = direct_ref[...] + near_in_ref[...] + widen(far_in_ref[...])
    lru = lru_ref[...]
    token = lax.broadcasted_iota(jnp.int32, (tokens, width), 0)
    token = jnp.where(token >= length, token - length, token)
    total = jnp.zeros_like(cot)
    count = 4
    for k in range(count):
        later = cot if k == 0 else jnp.where(token < length - k, pltpu.roll(cot, tokens - k, 0), 0.0)
        total = total + taps_ref[k : k + 1, :] * later
        sums_ref[k : k + 1, :] = jnp.sum(later * lru, axis=0, keepdims=True)
    sums_ref[count : count + 1, :] = jnp.sum(cot, axis=0, keepdims=True)
    low = total.astype(BF16)
    pre_cot_ref[0] = branch_ref[...]
    pre_cot_ref[1] = low
    part = cols_product(branch_ref[...], joined(branch_w_ref)) + cols_product(low, joined(lruin_w_ref))

    @pl.when(pl.program_id(0) == 0)
    def _():
        sum_ref[...] = part

    @pl.when(pl.program_id(0) > 0)
    def _():
        sum_ref[...] += part

    @pl.when(pl.program_id(0) == pl.num_programs(0) - 1)
    def _():
        near_ref[...] = sum_ref[:length, :]
        far_ref[...] = sum_ref[length:, :].astype(BF16)


def conv_back(direct, near, far, pre, branch, taps, whole, rows, depth):
    tokens, width = direct.shape
    shards, _, tile = whole.shape
    n = width // tile
    one = pl.BlockSpec((tokens, tile), lambda j: (0, j))
    half = pl.BlockSpec((tokens // 2, depth), lambda j: (0, 0))
    return pl.pallas_call(
        conv_kernel,
        grid=(n,),
        in_specs=[
            one, one, one, pl.BlockSpec((tokens, tile), lambda j: (0, j + n)), one,
            pl.BlockSpec((8, tile), lambda j: (0, j)),
            pl.BlockSpec((shards, rows, tile), lambda j: (0, j, 0)),
            pl.BlockSpec((shards, rows, tile), lambda j: (0, n + j, 0)),
        ],
        out_specs=[
            pl.BlockSpec((2, tokens, tile), lambda j: (0, 0, j)), pl.BlockSpec((8, tile), lambda j: (0, j)), half, half,
        ],
        out_shape=[
            jax.ShapeDtypeStruct((2, tokens, width), BF16), jax.ShapeDtypeStruct((8, width), F32),
            jax.ShapeDtypeStruct((tokens // 2, depth), F32), sent((tokens // 2, depth)),
        ],
        scratch_shapes=[pltpu.VMEM((tokens, depth), F32)],
        compiler_params=pltpu.CompilerParams(vmem_limit_bytes=VMEM),
        cost_estimate=HINT,
        name="conv_back",
    )(direct, near, far, pre, branch, taps, whole, whole)


def norm_kernel(near_ref, far_ref, base_ref, v_ref, gain_ref, out_ref, low_ref):
    v = widen(v_ref[...])
    scale = lax.rsqrt(jnp.mean(v * v, axis=-1, keepdims=True) + EPS)
    g = (near_ref[...] + widen(far_ref[...])) * gain_ref[0:1, :]
    out = widen(base_ref[...]) + scale * (g - v * (scale * scale * jnp.mean(g * v, axis=-1, keepdims=True)))
    out_ref[...] = out
    low_ref[...] = out.astype(BF16)


def norm_back(near, far, base, v, gain):
    rows, width = near.shape
    tile = rows // 4
    one = pl.BlockSpec((tile, width), lambda j: (j, 0))
    return pl.pallas_call(
        norm_kernel,
        grid=(rows // tile,),
        in_specs=[one, one, one, one, pl.BlockSpec((8, width), lambda j: (0, 0))],
        out_specs=[one, one],
        out_shape=[jax.ShapeDtypeStruct((rows, width), F32), sent((rows, width))],
        compiler_params=pltpu.CompilerParams(vmem_limit_bytes=LESS),
        cost_estimate=HINT,
        name="norm_back",
    )(near, far, base, v, jnp.broadcast_to(gain, (8, width)))


def flip_kernel(x_ref, out_ref):
    out_ref[...] = widen(x_ref[...]).T.astype(BF16)


def flip(x):
    tokens, n = x.shape
    tile = 256
    return pl.pallas_call(
        flip_kernel,
        grid=(n // tile,),
        in_specs=[pl.BlockSpec((tokens, tile), lambda j: (0, j))],
        out_specs=pl.BlockSpec((tile, tokens), lambda j: (j, 0)),
        out_shape=jax.ShapeDtypeStruct((n, tokens), BF16),
        compiler_params=pltpu.CompilerParams(vmem_limit_bytes=LESS),
        cost_estimate=HINT,
        name="flip",
    )(x)


def pack_kernel(block, side_ref, *refs):
    out_ref, at = refs[-1], 0
    for ref in refs[:-1]:
        rows, n = ref.shape
        for first in range(0, n, block):
            out_ref[at : at + rows, :] = ref[:, first : first + block]
            at += rows


def pack(side, halves, full, block):
    specs = [pl.BlockSpec((p.shape[0], p.shape[1] // 2), lambda j, s: (0, s[0])) for p in halves]
    specs.append(pl.BlockSpec(full.shape, lambda j, s: (0, 0)))
    size = sum(p.shape[0] * p.shape[1] // 2 for p in halves) + full.size
    return pl.pallas_call(
        functools.partial(pack_kernel, block),
        grid_spec=pltpu.PrefetchScalarGridSpec(
            num_scalar_prefetch=1, grid=(1,), in_specs=specs,
            out_specs=pl.BlockSpec((size // block, block), lambda j, s: (0, 0)),
        ),
        out_shape=jax.ShapeDtypeStruct((size // block, block), BF16),
        compiler_params=pltpu.CompilerParams(vmem_limit_bytes=LESS),
        cost_estimate=HINT,
        name="pack",
    )(side, *halves, full)


def columns_kernel(parts, side_ref, own_ref, got_ref, *out_refs):
    n = out_refs[0].shape[1]
    mine = pl.program_id(0) == side_ref[0]

    @pl.when(mine)
    def _():
        for i in range(parts):
            out_refs[i][...] = own_ref[:, i * n : (i + 1) * n]

    @pl.when(jnp.logical_not(mine))
    def _():
        for i in range(parts):
            out_refs[i][...] = widen(got_ref[:, i * n : (i + 1) * n])


def join_columns(side, own, got, parts):
    rows, n = own.shape[0], own.shape[1] // parts
    full = pl.BlockSpec(own.shape, lambda h, s: (0, 0))
    return pl.pallas_call(
        functools.partial(columns_kernel, parts),
        grid_spec=pltpu.PrefetchScalarGridSpec(
            num_scalar_prefetch=1, grid=(2,), in_specs=[full, full],
            out_specs=[pl.BlockSpec((rows, n), lambda h, s: (0, h))] * parts,
        ),
        out_shape=[jax.ShapeDtypeStruct((rows, 2 * n), F32)] * parts,
        compiler_params=pltpu.CompilerParams(vmem_limit_bytes=LESS),
        cost_estimate=HINT,
        name="join_columns",
    )(side, own, got)


def rows_kernel(side_ref, own_ref, got_ref, out_ref):
    mine = pl.program_id(0) == side_ref[0]

    @pl.when(mine)
    def _():
        out_ref[...] = own_ref[...]

    @pl.when(jnp.logical_not(mine))
    def _():
        out_ref[...] = widen(got_ref[...])


def join_rows(side, own, got):
    rows, n = own.shape
    full = pl.BlockSpec((rows, n), lambda h, s: (0, 0))
    return pl.pallas_call(
        rows_kernel,
        grid_spec=pltpu.PrefetchScalarGridSpec(
            num_scalar_prefetch=1, grid=(2,), in_specs=[full] * 2,
            out_specs=pl.BlockSpec((rows, n), lambda h, s: (h, 0)),
        ),
        out_shape=jax.ShapeDtypeStruct((2 * rows, n), F32),
        compiler_params=pltpu.CompilerParams(vmem_limit_bytes=LESS),
        cost_estimate=HINT,
        name="join_rows",
    )(side, own, got)


def weave_kernel(piece, side_ref, own_ref, got_ref, out_ref):
    for side in range(2):
        @pl.when(side_ref[0] == side)
        def _(side=side):
            parts = []
            for at in range(0, own_ref.shape[1], piece):
                own = own_ref[:, at : at + piece]
                got = widen(got_ref[:, at : at + piece])
                parts += [got, own] if side else [own, got]
            out_ref[...] = jnp.concatenate(parts, axis=1)


def weave(side, own, got, piece):
    rows, n = own.shape
    return pl.pallas_call(
        functools.partial(weave_kernel, piece),
        grid_spec=pltpu.PrefetchScalarGridSpec(
            num_scalar_prefetch=1, grid=(1,),
            in_specs=[pl.BlockSpec((rows, n), lambda h, s: (0, 0))] * 2,
            out_specs=pl.BlockSpec((rows, 2 * n), lambda h, s: (0, 0)),
        ),
        out_shape=jax.ShapeDtypeStruct((rows, 2 * n), F32),
        compiler_params=pltpu.CompilerParams(vmem_limit_bytes=LESS),
        cost_estimate=HINT,
        name="weave",
    )(side, own, got)


def recurrence_forward(pre, gates, admitted, params, length):
    tokens, width = admitted.shape
    tile = math.gcd(width, 512)
    n = width // tile
    near = pl.BlockSpec((length, tile), lambda s, j: (s, j))
    far = pl.BlockSpec((length, tile), lambda s, j: (s, j + n))
    vector = pl.BlockSpec((8, tile), lambda s, j: (0, j))
    return pl.pallas_call(
        forward_kernel,
        grid=(tokens // length, n),
        in_specs=[near, near, far, near, vector],
        out_specs=[near] * (1 + FACTORS),
        out_shape=[jax.ShapeDtypeStruct((tokens, width), BF16)] + [jax.ShapeDtypeStruct((tokens, width), F32)] * FACTORS,
        cost_estimate=pl.CostEstimate(flops=60 * tokens * width, bytes_accessed=20 * tokens * width, transcendentals=6 * tokens * width),
        name="recurrence_forward",
    )(pre, gates, gates, admitted, params)


def hidden_kernel(x_ref, gate_ref, up_ref, hidden_ref, flipped_ref, act_ref, slope_ref):
    x = x_ref[...]
    gate = matmul(x, joined(gate_ref))
    up = matmul(x, joined(up_ref))
    t = jnp.tanh(GELU_K * (gate + GELU_C * gate * gate * gate))
    act = 0.5 * gate * (1.0 + t)
    slope = 0.5 * (1.0 + t) + 0.5 * gate * (1.0 - t * t) * GELU_K * (1.0 + 3.0 * GELU_C * gate * gate)
    hidden = act * up
    hidden_ref[...] = hidden.astype(BF16)
    flipped_ref[...] = hidden.T.astype(BF16)
    act_ref[...] = act
    slope_ref[...] = up * slope


def hidden_pass(x, blocks, rows, tiles):
    tokens, depth = x.shape
    shards, _, tile = blocks.shape
    n = tiles * tile
    wide = pl.BlockSpec((tokens, tile), lambda j: (0, j))
    return pl.pallas_call(
        hidden_kernel,
        grid=(tiles,),
        in_specs=[
            pl.BlockSpec((tokens, depth), lambda j: (0, 0)),
            pl.BlockSpec((shards, rows, tile), lambda j: (0, j, 0)),
            pl.BlockSpec((shards, rows, tile), lambda j: (0, j + tiles, 0)),
        ],
        out_specs=[wide, pl.BlockSpec((tile, tokens), lambda j: (j, 0)), wide, wide],
        out_shape=[
            jax.ShapeDtypeStruct((tokens, n), BF16), jax.ShapeDtypeStruct((n, tokens), BF16),
            jax.ShapeDtypeStruct((tokens, n), F32), jax.ShapeDtypeStruct((tokens, n), F32),
        ],
        compiler_params=pltpu.CompilerParams(vmem_limit_bytes=VMEM),
        cost_estimate=HINT,
        name="hidden_pass",
    )(x, blocks, blocks)


def halves(sum_ref, part, near_ref, far_ref):
    @pl.when(pl.program_id(0) == 0)
    def _():
        sum_ref[...] = part

    @pl.when(pl.program_id(0) > 0)
    def _():
        sum_ref[...] += part

    @pl.when(pl.program_id(0) == pl.num_programs(0) - 1)
    def _():
        half = near_ref.shape[0]
        near_ref[...] = sum_ref[:half, :]
        far_ref[...] = sum_ref[half:, :].astype(BF16)


def take_tile(down_a_ref, down_b_ref, down_ref):
    rows, n = down_ref.shape[0], down_a_ref.shape[2]
    for j in range(shape_rows(down_a_ref) // rows):
        @pl.when(pl.program_id(0) == j)
        def _(j=j):
            down_ref[:, :n] = joined(down_a_ref)[j * rows : (j + 1) * rows]
            down_ref[:, n:] = joined(down_b_ref)[j * rows : (j + 1) * rows]


def shape_rows(ref):
    return ref.shape[0] * ref.shape[1]


def ffn_back_kernel(
    cot_ref, gate_ref, up_ref, down_a_ref, down_b_ref, act_ref, slope_ref,
    gate_cot_ref, up_cot_ref, near_ref, far_ref, sum_ref, down_ref,
):
    take_tile(down_a_ref, down_b_ref, down_ref)
    cot = cols_product(cot_ref[...], down_ref[...])
    gate_cot = (cot * slope_ref[...]).astype(BF16)
    up_cot = (cot * act_ref[...]).astype(BF16)
    gate_cot_ref[...] = gate_cot
    up_cot_ref[...] = up_cot
    halves(sum_ref, cols_product(gate_cot, joined(gate_ref)) + cols_product(up_cot, joined(up_ref)), near_ref, far_ref)


def down_specs(blocks, rows, tiles, piece):
    shards, _, tile = blocks.shape
    at = 2 * tiles * rows // piece
    return [pl.BlockSpec((shards, piece, tile), lambda j, k=k: (0, at + k, 0), pipeline_mode=pl.Buffered(1)) for k in range(2)]


def ffn_back(cot, blocks, act, slope, rows, tiles, piece):
    tokens, depth = cot.shape
    shards, _, tile = blocks.shape
    low = jax.ShapeDtypeStruct((tokens, tiles * tile), BF16)
    wide = pl.BlockSpec((tokens, tile), lambda j: (0, j))
    half = pl.BlockSpec((tokens // 2, depth), lambda j: (0, 0))
    return pl.pallas_call(
        ffn_back_kernel,
        grid=(tiles,),
        in_specs=[
            pl.BlockSpec((tokens, depth), lambda j: (0, 0)),
            pl.BlockSpec((shards, rows, tile), lambda j: (0, j, 0)),
            pl.BlockSpec((shards, rows, tile), lambda j: (0, j + tiles, 0)),
            *down_specs(blocks, rows, tiles, piece),
            wide, wide,
        ],
        out_specs=[wide, wide, half, half],
        out_shape=[
            low, low,
            jax.ShapeDtypeStruct((tokens // 2, depth), F32), sent((tokens // 2, depth)),
        ],
        scratch_shapes=[pltpu.VMEM((tokens, depth), F32), pltpu.VMEM((tile, depth), BF16)],
        compiler_params=pltpu.CompilerParams(vmem_limit_bytes=VMEM),
        cost_estimate=HINT,
        name="ffn_back",
    )(cot, blocks, blocks, blocks, blocks, act, slope)


def down_kernel(hidden_ref, down_a_ref, down_b_ref, near_ref, far_ref, sum_ref, down_ref):
    take_tile(down_a_ref, down_b_ref, down_ref)
    halves(sum_ref, matmul(hidden_ref[...], down_ref[...]), near_ref, far_ref)


def down_pass(hidden, blocks, depth, rows, tiles, piece):
    tokens, n = hidden.shape
    half = pl.BlockSpec((tokens // 2, depth), lambda j: (0, 0))
    return pl.pallas_call(
        down_kernel,
        grid=(tiles,),
        in_specs=[pl.BlockSpec((tokens, n // tiles), lambda j: (0, j)), *down_specs(blocks, rows, tiles, piece)],
        out_specs=[half, half],
        out_shape=[
            jax.ShapeDtypeStruct((tokens // 2, depth), F32), sent((tokens // 2, depth)),
        ],
        scratch_shapes=[pltpu.VMEM((tokens, depth), F32), pltpu.VMEM((n // tiles, depth), BF16)],
        compiler_params=pltpu.CompilerParams(vmem_limit_bytes=VMEM),
        cost_estimate=HINT,
        name="down_pass",
    )(hidden, blocks, blocks)


def joined(ref):
    v = ref[...]
    if v.shape[1] % 16:
        return widen(v).reshape(-1, v.shape[2]).astype(BF16)
    return v.reshape(-1, v.shape[2])


def away_kernel(at_ref, left_ref, right_ref, out_ref):
    out_ref[...] = matmul(joined(left_ref), right_ref[...]).reshape(out_ref.shape).astype(out_ref.dtype)


def home_kernel(bit, at_ref, left_ref, right_ref, got_ref, keep_ref, send_ref, sum_ref):
    v = matmul(joined(left_ref), right_ref[...]).reshape(got_ref.shape) + widen(got_ref[...])
    sum_ref[...] = v.reshape(sum_ref.shape)
    keep_ref[...] = sum_ref[:, at_ref[bit]].astype(keep_ref.dtype)
    send_ref[...] = sum_ref[:, 1 - at_ref[bit]].astype(send_ref.dtype)


def column_tile(n, choices=(1024, 768, 512, 256, 128)):
    return max(t for t in choices if n % t == 0)


def tiling(right, columns, skip):
    parts, _, n = right.shape
    tile = column_tile(columns or n)
    each = n // tile

    def index(j, at):
        at_tile = j + (at[0] if skip < 0 else skip)
        return at_tile // each, 0, at_tile % each

    return tile, columns or parts * n, index


def grad_away(left, right, at, columns=0, skip=0):
    owners, _, rows, tokens = left.shape
    tile, n, index = tiling(right, columns, skip)
    return pl.pallas_call(
        away_kernel,
        grid_spec=pltpu.PrefetchScalarGridSpec(
            num_scalar_prefetch=1,
            grid=(n // tile,),
            in_specs=[
                pl.BlockSpec((owners, None, rows, tokens), lambda j, at: (0, 1 - at[1], 0, 0)),
                pl.BlockSpec((None, tokens, tile), index),
            ],
            out_specs=pl.BlockSpec((owners, rows, tile), lambda j, at: (0, 0, j)),
        ),
        out_shape=sent((owners, rows, n)),
        compiler_params=pltpu.CompilerParams(vmem_limit_bytes=LESS),
        cost_estimate=HINT,
        name="grad_away",
    )(at, left, right)


def grad_home(left, right, got, at, bit, low, columns=0, skip=0):
    owners, _, rows, tokens = left.shape
    tile, n, index = tiling(right, columns, skip)
    high = owners // (2 * low)
    half = pl.BlockSpec((high, low, rows, tile), lambda j, at: (0, 0, 0, j))
    return pl.pallas_call(
        functools.partial(home_kernel, bit),
        grid_spec=pltpu.PrefetchScalarGridSpec(
            num_scalar_prefetch=1,
            grid=(n // tile,),
            in_specs=[
                pl.BlockSpec((owners, None, rows, tokens), lambda j, at: (0, at[1], 0, 0)),
                pl.BlockSpec((None, tokens, tile), index),
                pl.BlockSpec((owners, rows, tile), lambda j, at: (0, 0, j)),
            ],
            out_specs=[half, half],
            scratch_shapes=[pltpu.VMEM((high, 2, low, rows, tile), F32)],
        ),
        out_shape=[
            jax.ShapeDtypeStruct((high, low, rows, n), KEEP), sent((high, low, rows, n)),
        ],
        compiler_params=pltpu.CompilerParams(vmem_limit_bytes=LESS),
        cost_estimate=HINT,
        name="grad_home",
    )(at, left, right, got)


def fold_kernel(bit, at_ref, own_ref, got_ref, keep_ref, send_ref):
    mine, other = at_ref[bit], 1 - at_ref[bit]
    keep_ref[...] = (widen(own_ref[:, mine]) + widen(got_ref[:, mine])).astype(keep_ref.dtype)
    send_ref[...] = (widen(own_ref[:, other]) + widen(got_ref[:, other])).astype(BF16)


def fold(own, got, at, bit, low):
    rows, n = own.shape[2:]
    high = own.shape[0] * own.shape[1] // (2 * low)
    tile = column_tile(n, (1024, 768, 512, 256, 128))
    both = pl.BlockSpec((high, 2, low, rows, tile), lambda j, at: (0, 0, 0, 0, j))
    half = pl.BlockSpec((high, low, rows, tile), lambda j, at: (0, 0, 0, j))
    shape = (high, 2, low, rows, n)
    return pl.pallas_call(
        functools.partial(fold_kernel, bit),
        grid_spec=pltpu.PrefetchScalarGridSpec(
            num_scalar_prefetch=1, grid=(n // tile,), in_specs=[both, both], out_specs=[half, half]
        ),
        out_shape=[
            jax.ShapeDtypeStruct((high, low, rows, n), KEEP), sent((high, low, rows, n)),
        ],
        compiler_params=pltpu.CompilerParams(vmem_limit_bytes=LESS),
        cost_estimate=HINT,
        name="fold",
    )(at, own.reshape(shape), got.reshape(shape))


def settle_kernel(own_ref, got_ref, out_ref, low_ref):
    v = widen(own_ref[...]) + widen(got_ref[...])
    out_ref[...] = v
    low_ref[...] = v.astype(BF16)


def settle(own, got):
    rows, n = own.shape
    tile = column_tile(n, (1024, 768, 512, 256, 128))
    one = pl.BlockSpec((rows, tile), lambda j: (0, j))
    return pl.pallas_call(
        settle_kernel,
        grid=(n // tile,),
        in_specs=[one, one],
        out_specs=[one, one],
        out_shape=[jax.ShapeDtypeStruct((rows, n), F32), sent((rows, n))],
        compiler_params=pltpu.CompilerParams(vmem_limit_bytes=LESS),
        cost_estimate=HINT,
        name="settle",
    )(own, got)


def shifted(values, offset):
    if offset == 0:
        return values
    if offset > 0:
        return jnp.pad(values, ((0, 0), (offset, 0), (0, 0)))[:, : values.shape[1]]
    return jnp.pad(values, ((0, 0), (0, -offset), (0, 0)))[:, -offset:]


def body(
    groups, shards,
    tokens, cotangent, mix_gain, branch_proj, lruin_proj, conv_kernel, conv_bias, recur_proj, recur_bias,
    admit_proj, admit_bias, decay_param, out_proj, ffn_gain, ffn_gate, ffn_up, ffn_down,
):
    cores, bits = 2, shards.bit_length() - 1
    side = lax.axis_index("rep") % 2
    here = lax.axis_index("shard")
    taps = conv_kernel.shape[0]
    length, width = tokens.shape
    low_r = branch_proj.shape[1]
    half_r = low_r // 2
    half_f = ffn_gate.shape[1] // 2
    piece_f = half_f // shards

    def swap(v):
        return lax.ppermute(v, "rep", [(i, i ^ 1) for i in range(groups)])

    def swap_rows(v):
        v = swap(v)
        return jnp.concatenate([v[length:], v[:length]], axis=0)

    def mine(v, size, axis):
        return lax.dynamic_slice_in_dim(v, side * size, size, axis)

    def theirs(v, size, axis):
        return lax.dynamic_slice_in_dim(v, (1 - side) * size, size, axis)

    def natural(own, other):
        first = jnp.where(side == 0, own, other)
        second = jnp.where(side == 0, other, own)
        return jnp.concatenate([first, second], axis=-1)

    def with_pair(own):
        return jnp.concatenate([own, swap(own)], axis=0)

    clock = []

    def tick(*xs):
        return lax.optimization_barrier(tuple(xs) + tuple(clock))[: len(xs)]

    def tock(*ys):
        clock[:] = ys

    place = jnp.stack([side] + [(here >> i) & 1 for i in range(bits)]).astype(jnp.int32)
    here_side = place[:1]

    def cross(v, bit):
        return lax.ppermute(v, "shard", [(i, i ^ (1 << bit)) for i in range(shards)])

    class Scatter:
        def __init__(self, left, right, order=None, columns=0, skip=0):
            self.right, = tick(right if right.ndim == 3 else right[None])
            self.left = left.reshape(shards // cores, cores, left.shape[0] // shards, left.shape[1])
            self.order = list(order or range(1, bits))
            self.span = dict(columns=columns, skip=skip)
            send = grad_away(self.left, self.right, place, **self.span)
            tock(send)
            self.got = cross(send, 0)

        def next(self):
            bit, rest = self.order[0], self.order[1:]
            self.order = rest
            return bit, 2 ** sum(other < bit for other in rest)

        def home(self):
            right, got = tick(self.right, self.got)
            bit, low = self.next()
            self.v, send = grad_home(self.left, right, got, place, bit + 1, low, **self.span)
            tock(self.v, send)
            self.got = cross(send, bit)

        def fold(self):
            v, got = tick(self.v, self.got)
            bit, low = self.next()
            self.v, send = fold(v, got, place, bit + 1, low)
            tock(self.v, send)
            self.got = cross(send, bit)

        def two(self):
            while len(self.order) > 1:
                self.fold()

        def settle(self):
            v, got = tick(self.v, self.got)
            v, send = settle(v.reshape(v.shape[2:]), got.reshape(got.shape[2:]))
            tock(v, send)
            if groups > 2:
                total = v
                for k in range(1, groups // 2):
                    total = total + lax.ppermute(v, "rep", [(i, (i + 2 * k) % groups) for i in range(groups)])
                v, send = total, total.astype(BF16)
            self.v, self.got = v, swap(send)

        def both(self):
            return tick(self.v, self.got)

    per_d, per_r = mix_gain.shape[0], conv_bias.shape[0]
    vectors = jnp.concatenate(
        [mix_gain, ffn_gain, conv_kernel.reshape(-1), conv_bias, recur_bias, admit_bias, decay_param]
    )
    count = vectors.shape[0]
    vectors = jnp.pad(vectors, (0, -count % 128)).reshape(-1, 128)
    vectors = lax.all_gather(vectors, "shard", axis=0).reshape(shards, -1)[:, :count]
    gain_one = widen(vectors[:, :per_d].reshape(width))
    gain_two = widen(vectors[:, per_d : 2 * per_d].reshape(width))
    channel = vectors[:, 2 * per_d :].reshape(shards, taps + 4, per_r).transpose(1, 0, 2).reshape(taps + 4, low_r)
    channel = widen(mine(channel, half_r, 1))
    taps_half, cbias = channel[:taps], channel[taps]
    rbias, abias, lam = channel[taps + 1], channel[taps + 2], channel[taps + 3]
    rate = DECAY_SCALE * jax.nn.softplus(-lam)
    params = jnp.concatenate([jnp.stack([rbias, abias, rate]), jnp.zeros((5, half_r), F32)])

    def ffn_half(v):
        return lax.dynamic_index_in_dim(v.reshape(v.shape[0], shards, 2, piece_f), side, 2, False).reshape(v.shape[0], half_f)

    def gather_blocks(parts, block):
        rows = [p[:, at : at + block] for p in parts for at in range(0, p.shape[1], block)]
        return lax.all_gather(jnp.concatenate(rows, axis=0), "shard", axis=0)

    def unpack(whole, at, rows, columns):
        block = whole.shape[2]
        cols = [whole[:, at + i * rows : at + (i + 1) * rows].reshape(shards * rows, block) for i in range(columns // block)]
        return jnp.concatenate(cols, axis=1)

    per_f, tiles = 2 * piece_f, 3
    whole = lax.all_gather(
        pack(here_side, [branch_proj, lruin_proj, recur_proj, admit_proj], out_proj, 512), "shard", axis=0
    )
    ffn_blocks = gather_blocks(
        [ffn_half(ffn_gate), ffn_half(ffn_up), mine(ffn_down, piece_f, 0)], half_f // tiles
    )
    cot_pair = with_pair(cotangent)
    values = widen(with_pair(tokens))
    scale_one = lax.rsqrt(jnp.mean(values * values, axis=-1, keepdims=True) + EPS)
    normed = (values * scale_one * gain_one).astype(BF16)
    normed_t = flip(normed)
    tock(normed_t, cot_pair)
    whole, = tick(whole)
    at = low_r // 512 * per_d
    w1 = unpack(whole, 0, per_d, low_r)
    w2 = unpack(whole, at, per_r, low_r)
    w3 = unpack(whole, at + low_r // 512 * per_r, per_r, width)
    pre = matmul(normed, w1)
    lru_pre = pre[:, half_r:].reshape(2, length, half_r)
    conv = cbias
    for k in range(taps):
        conv = conv + taps_half[k] * shifted(lru_pre, k)
    admitted = conv.reshape(2 * length, half_r).astype(BF16)
    admitted_all = natural(admitted, swap_rows(admitted))
    gates = matmul(admitted_all, w2)
    mixed, *factors = recurrence_forward(pre, gates, admitted, params, length)
    tock(mixed)
    admitted_all, = tick(admitted_all)
    admitted_t = flip(admitted_all)
    tock(admitted_t)
    mixed_other, = tick(swap(mixed[length:]))
    mixed_own = natural(mixed[:length], mixed_other)
    middle = widen(tokens) + matmul(mixed_own, w3)
    scale_two = lax.rsqrt(jnp.mean(middle * middle, axis=-1, keepdims=True) + EPS)
    normed_two = (middle * scale_two * gain_two).astype(BF16)
    tock(normed_two)
    mixed_late, mixed_far = tick(mixed[length:], swap(mixed[:length]))
    mixed_t = flip(jnp.concatenate([mixed_own, natural(mixed_late, mixed_far)], axis=0))
    tock(mixed_t)
    normed_two = jnp.concatenate([normed_two, *tick(swap(normed_two))], axis=0)
    tock(normed_two)
    ffn_blocks, = tick(ffn_blocks)

    ffn = dict(rows=per_d, tiles=tiles)
    have, grads, steps = {}, {}, {}

    def step(run):
        steps[run.__name__] = run
        return run

    @step
    def hidden():
        x, = tick(normed_two)
        have["hidden"], have["hidden_t"], have["act"], have["slope"] = hidden_pass(x, ffn_blocks, **ffn)
        tock(have["hidden"], have["hidden_t"])

    @step
    def ffn_in():
        act, = tick(have["act"])
        have["gate_cot"], have["up_cot"], near, far = ffn_back(
            cot_pair, ffn_blocks, act, have["slope"], piece=piece_f, **ffn
        )
        tock(near, far)
        have["ffn"] = near, swap(far)

    @step
    def turn():
        x, = tick(normed_two)
        have["normed_two_t"] = flip(x)
        tock(have["normed_two_t"])

    @step
    def norm_two():
        near, far = tick(*have["ffn"])
        have["middle_cot"], low = norm_back(near, far, cotangent, middle, gain_two)
        tock(have["middle_cot"], low)
        have["middle_low"] = low, swap(low)

    @step
    def mixer():
        low, other = tick(*have["middle_low"])
        have["branch_low"], have["gates_cot"], have["direct"], have["sums"], near, far = chain_back(
            here_side, low, other, whole, at, per_r, factors
        )
        have["out_cot"] = jnp.concatenate([low, other], axis=0)
        tock(near, far)
        have["admitted"] = near, swap(far)

    @step
    def conv_in():
        direct, near, far = tick(have["direct"], *have["admitted"])
        have["pre_cot"], have["conv_sums"], near, far = conv_back(
            direct, near, far, pre, have["branch_low"], channel, whole, per_d, width
        )
        tock(near, far, have["pre_cot"])
        have["normed"] = near, swap(far)

    @step
    def norm_one():
        near, far = tick(*have["normed"])
        have["tokens_grad"], _ = norm_back(near, far, have["middle_cot"], tokens, gain_one)
        tock(have["tokens_grad"])

    @step
    def down():
        x, = tick(have["hidden"])
        near, far = down_pass(x, ffn_blocks, width, piece=piece_f, **ffn)
        tock(near, far)
        have["down"] = near, swap(far)

    @step
    def result():
        near, far = tick(*have["down"])
        have["block_out"] = (middle + near + widen(far)).astype(BF16)
        tock(have["block_out"])

    @step
    def small():
        conv_sums, sums = tick(have["conv_sums"], have["sums"])
        sums = jnp.sum(sums.reshape(3, ROWS, half_r), axis=1)
        v = jnp.concatenate([conv_sums[: taps + 1], sums[:2], sums[2:] * (DECAY_SCALE * jax.nn.sigmoid(-lam))])
        v = natural(v, jnp.zeros_like(v))
        tock(v)
        have["small"] = lax.psum(v, ("rep", "shard"))

    @step
    def small_end():
        v, = tick(have["small"])
        have["small"] = lax.dynamic_slice_in_dim(v, here * per_r, per_r, 1)
        tock(have["small"])

    def late(name, left, right, order=None, **span):
        def away():
            grads[name] = Scatter(left(), right(), order, **span)

        steps["away_" + name] = away
        for stage in ("home", "two", "fold", "settle"):
            steps[stage + "_" + name] = lambda stage=stage: getattr(grads[name], stage)()

    z_first = [2, 1] + list(range(3, bits))
    late("d", lambda: have["hidden_t"], lambda: cot_pair)
    late("g", lambda: have["normed_two_t"], lambda: have["gate_cot"])
    late("u", lambda: have["normed_two_t"], lambda: have["up_cot"], z_first)
    late("r", lambda: admitted_t, lambda: have["gates_cot"], z_first)
    late("b", lambda: normed_t, lambda: have["pre_cot"])
    late("o", lambda: mixed_t, lambda: have["out_cot"], columns=width // 2, skip=-1)

    @step
    def join_d():
        v, got = grads["d"].both()
        have["d"] = join_rows(here_side, v, got)
        tock(have["d"])

    @step
    def join_g():
        have["g"] = weave(here_side, *grads["g"].both(), piece_f)
        tock(have["g"])

    @step
    def join_u():
        have["u"] = weave(here_side, *grads["u"].both(), piece_f)
        tock(have["u"])

    @step
    def join_r():
        have["r"] = join_columns(here_side, *grads["r"].both(), 2)
        tock(*have["r"])

    @step
    def join_b():
        have["b"] = join_columns(here_side, *grads["b"].both(), 2)
        tock(*have["b"])

    @step
    def join_o():
        have["o"], = join_columns(here_side, *grads["o"].both(), 1)
        tock(have["o"])

    for name in STEPS:
        steps[name]()
    small_grad, (branch_grad, lruin_grad) = have["small"], have["b"]
    ffngain_grad = jnp.sum(have["g"] * widen(ffn_gate) + have["u"] * widen(ffn_up), axis=1) / widen(ffn_gain)
    mixgain_grad = jnp.sum(branch_grad * widen(branch_proj) + lruin_grad * widen(lruin_proj), axis=1) / widen(mix_gain)
    return (
        have["block_out"], have["tokens_grad"], mixgain_grad, branch_grad, lruin_grad, small_grad[:taps],
        small_grad[taps], have["r"][0], small_grad[taps + 1], have["r"][1], small_grad[taps + 2],
        small_grad[taps + 3], have["o"], ffngain_grad, have["g"], have["u"], have["d"],
    )


def solution(mesh):
    groups, shards = mesh.shape["rep"], mesh.shape["shard"]
    whole = P(("rep", "shard"), None)
    row, vec, col = P("shard", None), P("shard"), P(None, "shard")
    in_specs = (whole, whole, vec, row, row, col, vec, row, vec, row, vec, vec, row, vec, row, row, row)
    out_specs = (whole, whole, vec, row, row, col, vec, row, vec, row, vec, vec, row, vec, row, row, row)
    return jax.shard_map(
        functools.partial(body, groups, shards), mesh=mesh, in_specs=in_specs, out_specs=out_specs, check_vma=False
    )
```

```python
import functools
import math

import jax
import jax.numpy as jnp
from jax import lax
from jax.experimental import pallas as pl
from jax.experimental.pallas import tpu as pltpu
from jax.sharding import PartitionSpec as P

EPS = 1e-06
DECAY_SCALE = 8.0
ROOT_FLOOR = 0.001
GELU_K = math.sqrt(2.0 / math.pi)
GELU_C = 0.044715
ROWS = 16
FACTORS = 7
VMEM = 44 << 20
LESS = 24 << 20
MORE = 50 << 20
PARTS = 2
STEPS = (
    "turn", "ffn_in", "away_u", "away_d", "norm_two", "home_u", "home_d", "away_g", "mixer", "away_r", "two_u",
    "two_d", "home_g", "home_r", "conv_in", "fold_u", "fold_d", "away_b", "small", "settle_u", "down", "home_b",
    "norm_one", "two_g", "two_r", "join_u", "two_b", "away_o", "fold_g", "settle_d", "home_o", "fold_r", "settle_g",
    "join_d", "two_o", "fold_b", "join_g", "settle_r", "fold_o", "result", "small_end", "settle_b", "join_r",
    "settle_o", "join_b", "join_o",
)
HINT = pl.CostEstimate(flops=100000000000, bytes_accessed=1024, transcendentals=0)
BF16 = jnp.bfloat16
F32 = jnp.float32
KEEP = BF16


def sent(shape):
    return pltpu.HBM(shape, BF16)


def matmul(left, right):
    return jnp.dot(left, right, preferred_element_type=F32)


def rows_product(left, right):
    return lax.dot_general(left, right, (((0,), (0,)), ((), ())), preferred_element_type=F32)


def cols_product(left, right):
    return lax.dot_general(left, right, (((1,), (1,)), ((), ())), preferred_element_type=F32)


def widen(value):
    return value.astype(F32)


def gelu(v):
    return 0.5 * v * (1.0 + jnp.tanh(GELU_K * (v + GELU_C * v * v * v)))


def gelu_slope(v):
    t = jnp.tanh(GELU_K * (v + GELU_C * v * v * v))
    return 0.5 * (1.0 + t) + 0.5 * v * (1.0 - t * t) * GELU_K * (1.0 + 3.0 * GELU_C * v * v)


def forward_kernel(pre_ref, gates_r_ref, gates_i_ref, admitted_ref, params_ref, mixed_ref, *factor_refs):
    width = pre_ref.shape[1]
    rbias, abias, rate = params_ref[0:1, :], params_ref[1:2, :], params_ref[2:3, :]
    row = lax.broadcasted_iota(jnp.int32, (ROWS, width), 0)

    def step(i, carry):
        at = pl.ds(pl.multiple_of(i * ROWS, ROWS), ROWS)
        gate_r = jax.nn.sigmoid(gates_r_ref[at, :] + rbias)
        gate_i = jax.nn.sigmoid(gates_i_ref[at, :] + abias)
        admitted = widen(admitted_ref[at, :])
        decay = jnp.exp(-(gate_r * rate))
        rest = 1.0 - decay * decay
        root = jnp.sqrt(jnp.maximum(rest, ROOT_FLOOR))
        through = root * gate_i
        a, b = decay, through * admitted
        for d in (1, 2, 4, 8):
            keep = row >= d
            b = b + a * jnp.where(keep, pltpu.roll(b, d, 0), 0.0)
            a = a * jnp.where(keep, pltpu.roll(a, d, 0), 1.0)
        state = b + a * carry
        before = jnp.where(row >= 1, pltpu.roll(state, 1, 0), carry)
        pre = pre_ref[at, :]
        t = jnp.tanh(GELU_K * (pre + GELU_C * pre * pre * pre))
        act = 0.5 * pre * (1.0 + t)
        slope = 0.5 * (1.0 + t) + 0.5 * pre * (1.0 - t * t) * GELU_K * (1.0 + 3.0 * GELU_C * pre * pre)
        mixed_ref[at, :] = (state * act).astype(BF16)
        share = jnp.where(rest > ROOT_FLOOR, 1.0, jnp.where(rest == ROOT_FLOOR, 0.5, 0.0))
        log = decay * (before - gate_i * admitted * (share * decay / root))
        factors = (
            decay, act, state * slope, through, through * admitted * (1.0 - gate_i),
            -(log * rate) * gate_r * (1.0 - gate_r), log * gate_r,
        )
        for ref, factor in zip(factor_refs, factors, strict=True):
            ref[at, :] = factor
        return jnp.broadcast_to(state[ROWS - 1 : ROWS, :], (ROWS, width))

    lax.fori_loop(0, pre_ref.shape[0] // ROWS, step, jnp.zeros((ROWS, width), F32))


def chain_kernel(
    side_ref, own_ref, other_ref, out_a_ref, out_b_ref, out_c_ref, recur_w_ref, admit_w_ref, decay_ref, act_ref,
    branch_f_ref, direct_f_ref, admit_f_ref, recur_f_ref, rate_f_ref,
    branch_ref, gates_cot_ref, direct_ref, sums_ref, near_ref, far_ref, cot_ref, sum_ref,
):
    length = own_ref.shape[0]
    width = act_ref.shape[1]
    out_w = jnp.concatenate([joined(out_a_ref), joined(out_b_ref), joined(out_c_ref)], axis=1)
    cot_ref[:length, :] = cols_product(own_ref[...], out_w)
    cot_ref[length:, :] = cols_product(other_ref[...], out_w)
    row = lax.broadcasted_iota(jnp.int32, (ROWS, width), 0)
    blocks = length // ROWS
    zero = jnp.zeros((ROWS, width), F32)

    def step(first, i, state):
        carry, sum_r, sum_i, sum_d = state
        at = pl.ds(pl.multiple_of(first + (blocks - 1 - i) * ROWS, ROWS), ROWS)
        cot = cot_ref[at, :]
        branch_ref[at, :] = (cot * branch_f_ref[at, :]).astype(BF16)
        own = cot * act_ref[at, :]
        f = decay_ref[at, :]
        e = f * own
        for d in (1, 2, 4, 8):
            keep = row < ROWS - d
            e = e + f * jnp.where(keep, pltpu.roll(e, ROWS - d, 0), 0.0)
            f = f * jnp.where(keep, pltpu.roll(f, ROWS - d, 0), 1.0)
        e = e + f * carry
        g = own + jnp.where(row < ROWS - 1, pltpu.roll(e, ROWS - 1, 0), carry)
        direct_ref[at, :] = g * direct_f_ref[at, :]
        recur = g * recur_f_ref[at, :]
        admit = g * admit_f_ref[at, :]
        gates_cot_ref[0, at, :] = recur.astype(BF16)
        gates_cot_ref[1, at, :] = admit.astype(BF16)
        carry = jnp.broadcast_to(e[0:1, :], (ROWS, width))
        return carry, sum_r + recur, sum_i + admit, sum_d + g * rate_f_ref[at, :]

    sums = (zero, zero, zero)
    for first in (0, length):
        _, *sums = lax.fori_loop(0, blocks, functools.partial(step, first), (zero, *sums))
    for i in range(3):
        sums_ref[i * ROWS : (i + 1) * ROWS, :] = sums[i]
    depth = sum_ref.shape[1]
    part = cols_product(gates_cot_ref[0], joined(recur_w_ref)) + cols_product(gates_cot_ref[1], joined(admit_w_ref))

    @pl.when(pl.program_id(0) == 0)
    def _():
        sum_ref[...] = part

    @pl.when(pl.program_id(0) > 0)
    def _():
        sum_ref[...] += part

    half = depth // 2
    for side in range(2):
        @pl.when((pl.program_id(0) == pl.num_programs(0) - 1) & (side_ref[0] == side))
        def _(side=side):
            near_ref[...] = sum_ref[:, side * half : (side + 1) * half]
            away = slice((1 - side) * half, (2 - side) * half)
            far_ref[:length, :] = sum_ref[length:, away].astype(BF16)
            far_ref[length:, :] = sum_ref[:length, away].astype(BF16)


def chain_back(side, own, other, whole, at, rows, factors):
    length, depth = own.shape
    tokens, width = factors[0].shape
    shards, _, tile = whole.shape
    n = width // tile
    at = at // rows
    low = jax.ShapeDtypeStruct((tokens, width), BF16)
    full = pl.BlockSpec((length, depth), lambda j, s: (0, 0))
    near = pl.BlockSpec((tokens, tile), lambda j, s: (0, j))
    fixed = pl.BlockSpec((tokens, width), lambda j, s: (0, 0))
    return pl.pallas_call(
        chain_kernel,
        grid_spec=pltpu.PrefetchScalarGridSpec(
            num_scalar_prefetch=1,
            grid=(n,),
            in_specs=[
                full, full,
                *[
                    pl.BlockSpec((tile // rows, rows, tile), lambda j, s, k=k: (s[0] * n + j, at + 2 * n + k, 0))
                    for k in range(3)
                ],
                pl.BlockSpec((shards, rows, tile), lambda j, s: (0, at + j, 0)),
                pl.BlockSpec((shards, rows, tile), lambda j, s: (0, at + n + j, 0)),
                *[near] * FACTORS,
            ],
            out_specs=[
                near, pl.BlockSpec((2, tokens, tile), lambda j, s: (0, 0, j)), near,
                pl.BlockSpec((3 * ROWS, tile), lambda j, s: (0, j)), fixed, fixed,
            ],
            scratch_shapes=[pltpu.VMEM((tokens, tile), F32), pltpu.VMEM((tokens, 2 * width), F32)],
        ),
        out_shape=[
            low, jax.ShapeDtypeStruct((2, tokens, width), BF16), jax.ShapeDtypeStruct((tokens, width), F32),
            jax.ShapeDtypeStruct((3 * ROWS, width), F32), jax.ShapeDtypeStruct((tokens, width), F32), sent((tokens, width)),
        ],
        compiler_params=pltpu.CompilerParams(vmem_limit_bytes=VMEM),
        cost_estimate=HINT,
        name="chain_back",
    )(side, own, other, *[whole] * 5, *factors)


def conv_kernel(
    direct_ref, near_in_ref, far_in_ref, lru_ref, branch_ref, taps_ref, branch_w_ref, lruin_w_ref,
    pre_cot_ref, sums_ref, near_ref, far_ref, sum_ref,
):
    tokens, width = direct_ref.shape
    length = tokens // 2
    cot = direct_ref[...] + near_in_ref[...] + widen(far_in_ref[...])
    lru = lru_ref[...]
    token = lax.broadcasted_iota(jnp.int32, (tokens, width), 0)
    token = jnp.where(token >= length, token - length, token)
    total = jnp.zeros_like(cot)
    count = 4
    for k in range(count):
        later = cot if k == 0 else jnp.where(token < length - k, pltpu.roll(cot, tokens - k, 0), 0.0)
        total = total + taps_ref[k : k + 1, :] * later
        sums_ref[k : k + 1, :] = jnp.sum(later * lru, axis=0, keepdims=True)
    sums_ref[count : count + 1, :] = jnp.sum(cot, axis=0, keepdims=True)
    low = total.astype(BF16)
    pre_cot_ref[0] = branch_ref[...]
    pre_cot_ref[1] = low
    part = cols_product(branch_ref[...], joined(branch_w_ref)) + cols_product(low, joined(lruin_w_ref))

    @pl.when(pl.program_id(0) == 0)
    def _():
        sum_ref[...] = part

    @pl.when(pl.program_id(0) > 0)
    def _():
        sum_ref[...] += part

    @pl.when(pl.program_id(0) == pl.num_programs(0) - 1)
    def _():
        near_ref[...] = sum_ref[:length, :]
        far_ref[...] = sum_ref[length:, :].astype(BF16)


def conv_back(direct, near, far, pre, branch, taps, whole, rows, depth):
    tokens, width = direct.shape
    shards, _, tile = whole.shape
    n = width // tile
    one = pl.BlockSpec((tokens, tile), lambda j: (0, j))
    half = pl.BlockSpec((tokens // 2, depth), lambda j: (0, 0))
    return pl.pallas_call(
        conv_kernel,
        grid=(n,),
        in_specs=[
            one, one, one, pl.BlockSpec((tokens, tile), lambda j: (0, j + n)), one,
            pl.BlockSpec((8, tile), lambda j: (0, j)),
            pl.BlockSpec((shards, rows, tile), lambda j: (0, j, 0)),
            pl.BlockSpec((shards, rows, tile), lambda j: (0, n + j, 0)),
        ],
        out_specs=[
            pl.BlockSpec((2, tokens, tile), lambda j: (0, 0, j)), pl.BlockSpec((8, tile), lambda j: (0, j)), half, half,
        ],
        out_shape=[
            jax.ShapeDtypeStruct((2, tokens, width), BF16), jax.ShapeDtypeStruct((8, width), F32),
            jax.ShapeDtypeStruct((tokens // 2, depth), F32), sent((tokens // 2, depth)),
        ],
        scratch_shapes=[pltpu.VMEM((tokens, depth), F32)],
        compiler_params=pltpu.CompilerParams(vmem_limit_bytes=VMEM),
        cost_estimate=HINT,
        name="conv_back",
    )(direct, near, far, pre, branch, taps, whole, whole)


def norm_kernel(near_ref, far_ref, base_ref, v_ref, gain_ref, out_ref, low_ref):
    v = widen(v_ref[...])
    scale = lax.rsqrt(jnp.mean(v * v, axis=-1, keepdims=True) + EPS)
    g = (near_ref[...] + widen(far_ref[...])) * gain_ref[0:1, :]
    out = widen(base_ref[...]) + scale * (g - v * (scale * scale * jnp.mean(g * v, axis=-1, keepdims=True)))
    out_ref[...] = out
    low_ref[...] = out.astype(BF16)


def norm_back(near, far, base, v, gain):
    rows, width = near.shape
    tile = rows // 4
    one = pl.BlockSpec((tile, width), lambda j: (j, 0))
    return pl.pallas_call(
        norm_kernel,
        grid=(rows // tile,),
        in_specs=[one, one, one, one, pl.BlockSpec((8, width), lambda j: (0, 0))],
        out_specs=[one, one],
        out_shape=[jax.ShapeDtypeStruct((rows, width), F32), sent((rows, width))],
        compiler_params=pltpu.CompilerParams(vmem_limit_bytes=LESS),
        cost_estimate=HINT,
        name="norm_back",
    )(near, far, base, v, jnp.broadcast_to(gain, (8, width)))


def flip_kernel(x_ref, out_ref):
    out_ref[...] = widen(x_ref[...]).T.astype(BF16)


def flip(x):
    tokens, n = x.shape
    tile = 256
    return pl.pallas_call(
        flip_kernel,
        grid=(n // tile,),
        in_specs=[pl.BlockSpec((tokens, tile), lambda j: (0, j))],
        out_specs=pl.BlockSpec((tile, tokens), lambda j: (j, 0)),
        out_shape=jax.ShapeDtypeStruct((n, tokens), BF16),
        compiler_params=pltpu.CompilerParams(vmem_limit_bytes=LESS),
        cost_estimate=HINT,
        name="flip",
    )(x)


def pack_kernel(block, side_ref, *refs):
    out_ref, at = refs[-1], 0
    for ref in refs[:-1]:
        rows, n = ref.shape
        for first in range(0, n, block):
            out_ref[at : at + rows, :] = ref[:, first : first + block]
            at += rows


def pack(side, halves, full, block):
    specs = [pl.BlockSpec((p.shape[0], p.shape[1] // 2), lambda j, s: (0, s[0])) for p in halves]
    specs.append(pl.BlockSpec(full.shape, lambda j, s: (0, 0)))
    size = sum(p.shape[0] * p.shape[1] // 2 for p in halves) + full.size
    return pl.pallas_call(
        functools.partial(pack_kernel, block),
        grid_spec=pltpu.PrefetchScalarGridSpec(
            num_scalar_prefetch=1, grid=(1,), in_specs=specs,
            out_specs=pl.BlockSpec((size // block, block), lambda j, s: (0, 0)),
        ),
        out_shape=jax.ShapeDtypeStruct((size // block, block), BF16),
        compiler_params=pltpu.CompilerParams(vmem_limit_bytes=LESS),
        cost_estimate=HINT,
        name="pack",
    )(side, *[pltpu.with_memory_space_constraint(p, pltpu.HBM) for p in (*halves, full)])


def columns_kernel(parts, side_ref, own_ref, got_ref, *out_refs):
    n = out_refs[0].shape[1]
    mine = pl.program_id(0) == side_ref[0]

    @pl.when(mine)
    def _():
        for i in range(parts):
            out_refs[i][...] = own_ref[:, i * n : (i + 1) * n]

    @pl.when(jnp.logical_not(mine))
    def _():
        for i in range(parts):
            out_refs[i][...] = widen(got_ref[:, i * n : (i + 1) * n])


def join_columns(side, own, got, parts):
    rows, n = own.shape[0], own.shape[1] // parts
    full = pl.BlockSpec(own.shape, lambda h, s: (0, 0))
    return pl.pallas_call(
        functools.partial(columns_kernel, parts),
        grid_spec=pltpu.PrefetchScalarGridSpec(
            num_scalar_prefetch=1, grid=(2,), in_specs=[full, full],
            out_specs=[pl.BlockSpec((rows, n), lambda h, s: (0, h))] * parts,
        ),
        out_shape=[jax.ShapeDtypeStruct((rows, 2 * n), F32)] * parts,
        compiler_params=pltpu.CompilerParams(vmem_limit_bytes=LESS),
        cost_estimate=HINT,
        name="join_columns",
    )(side, own, got)


def rows_kernel(side_ref, own_ref, got_ref, out_ref):
    mine = pl.program_id(0) == side_ref[0]

    @pl.when(mine)
    def _():
        out_ref[...] = own_ref[...]

    @pl.when(jnp.logical_not(mine))
    def _():
        out_ref[...] = widen(got_ref[...])


def join_rows(side, own, got):
    rows, n = own.shape
    full = pl.BlockSpec((rows, n), lambda h, s: (0, 0))
    return pl.pallas_call(
        rows_kernel,
        grid_spec=pltpu.PrefetchScalarGridSpec(
            num_scalar_prefetch=1, grid=(2,), in_specs=[full] * 2,
            out_specs=pl.BlockSpec((rows, n), lambda h, s: (h, 0)),
        ),
        out_shape=jax.ShapeDtypeStruct((2 * rows, n), F32),
        compiler_params=pltpu.CompilerParams(vmem_limit_bytes=LESS),
        cost_estimate=HINT,
        name="join_rows",
    )(side, own, got)


def weave_kernel(piece, side_ref, own_ref, got_ref, out_ref):
    for side in range(2):
        @pl.when(side_ref[0] == side)
        def _(side=side):
            parts = []
            for at in range(0, own_ref.shape[1], piece):
                own = own_ref[:, at : at + piece]
                got = widen(got_ref[:, at : at + piece])
                parts += [got, own] if side else [own, got]
            out_ref[...] = jnp.concatenate(parts, axis=1)


def weave(side, own, got, piece):
    rows, n = own.shape
    return pl.pallas_call(
        functools.partial(weave_kernel, piece),
        grid_spec=pltpu.PrefetchScalarGridSpec(
            num_scalar_prefetch=1, grid=(1,),
            in_specs=[pl.BlockSpec((rows, n), lambda h, s: (0, 0))] * 2,
            out_specs=pl.BlockSpec((rows, 2 * n), lambda h, s: (0, 0)),
        ),
        out_shape=jax.ShapeDtypeStruct((rows, 2 * n), F32),
        compiler_params=pltpu.CompilerParams(vmem_limit_bytes=LESS),
        cost_estimate=HINT,
        name="weave",
    )(side, own, got)


def recurrence_forward(pre, gates, admitted, params, length):
    tokens, width = admitted.shape
    tile = math.gcd(width, 512)
    n = width // tile
    near = pl.BlockSpec((length, tile), lambda s, j: (s, j))
    far = pl.BlockSpec((length, tile), lambda s, j: (s, j + n))
    vector = pl.BlockSpec((8, tile), lambda s, j: (0, j))
    return pl.pallas_call(
        forward_kernel,
        grid=(tokens // length, n),
        in_specs=[near, near, far, near, vector],
        out_specs=[near] * (1 + FACTORS),
        out_shape=[jax.ShapeDtypeStruct((tokens, width), BF16)] + [jax.ShapeDtypeStruct((tokens, width), F32)] * FACTORS,
        cost_estimate=pl.CostEstimate(flops=60 * tokens * width, bytes_accessed=20 * tokens * width, transcendentals=6 * tokens * width),
        name="recurrence_forward",
    )(pre, gates, gates, admitted, params)


def take_tile(down_a_ref, down_b_ref, down_ref):
    rows, n = down_ref.shape[0], down_a_ref.shape[2]
    for j in range(shape_rows(down_a_ref) // rows):
        @pl.when(pl.program_id(0) == j)
        def _(j=j):
            down_ref[:, :n] = joined(down_a_ref)[j * rows : (j + 1) * rows]
            down_ref[:, n:] = joined(down_b_ref)[j * rows : (j + 1) * rows]


def shape_rows(ref):
    return ref.shape[0] * ref.shape[1]


def ffn_kernel(
    x_ref, cot_ref, gate_ref, up_ref, down_a_ref, down_b_ref,
    hidden_ref, flipped_ref, gate_cot_ref, up_cot_ref, near_ref, far_ref, sum_ref, down_ref,
):
    take_tile(down_a_ref, down_b_ref, down_ref)
    gate_w, up_w, down_w = joined(gate_ref), joined(up_ref), down_ref[...]
    tokens = x_ref.shape[0]
    for first in range(0, tokens, tokens // PARTS):
        rows = slice(first, first + tokens // PARTS)
        x = x_ref[rows, :]
        gate = matmul(x, gate_w)
        up = matmul(x, up_w)
        cot = cols_product(cot_ref[rows, :], down_w)
        t = jnp.tanh(GELU_K * (gate + GELU_C * gate * gate * gate))
        act = 0.5 * gate * (1.0 + t)
        slope = 0.5 * (1.0 + t) + 0.5 * gate * (1.0 - t * t) * GELU_K * (1.0 + 3.0 * GELU_C * gate * gate)
        hidden = act * up
        hidden_ref[rows, :] = hidden.astype(BF16)
        flipped_ref[:, rows] = hidden.T.astype(BF16)
        gate_cot = (cot * up * slope).astype(BF16)
        up_cot = (cot * act).astype(BF16)
        gate_cot_ref[rows, :] = gate_cot
        up_cot_ref[rows, :] = up_cot
        part = cols_product(gate_cot, gate_w) + cols_product(up_cot, up_w)

        @pl.when(pl.program_id(0) == 0)
        def _(part=part, rows=rows):
            sum_ref[rows, :] = part

        @pl.when(pl.program_id(0) > 0)
        def _(part=part, rows=rows):
            sum_ref[rows, :] += part

    @pl.when(pl.program_id(0) == pl.num_programs(0) - 1)
    def _():
        half = near_ref.shape[0]
        near_ref[...] = sum_ref[:half, :]
        far_ref[...] = sum_ref[half:, :].astype(BF16)


def down_specs(blocks, rows, tiles, piece):
    shards, _, tile = blocks.shape
    at = 2 * tiles * rows // piece
    return [pl.BlockSpec((shards, piece, tile), lambda j, k=k: (0, at + k, 0), pipeline_mode=pl.Buffered(1)) for k in range(2)]


def ffn_pass(x, cot, blocks, rows, tiles, piece):
    tokens, depth = x.shape
    shards, _, tile = blocks.shape
    n = tiles * tile
    low = jax.ShapeDtypeStruct((tokens, n), BF16)
    fixed = pl.BlockSpec((tokens, depth), lambda j: (0, 0))
    wide = pl.BlockSpec((tokens, tile), lambda j: (0, j))
    half = pl.BlockSpec((tokens // 2, depth), lambda j: (0, 0))
    return pl.pallas_call(
        ffn_kernel,
        grid=(tiles,),
        in_specs=[
            fixed, fixed,
            pl.BlockSpec((shards, rows, tile), lambda j: (0, j, 0)),
            pl.BlockSpec((shards, rows, tile), lambda j: (0, j + tiles, 0)),
            *down_specs(blocks, rows, tiles, piece),
        ],
        out_specs=[wide, pl.BlockSpec((tile, tokens), lambda j: (j, 0)), wide, wide, half, half],
        out_shape=[
            low, jax.ShapeDtypeStruct((n, tokens), BF16), low, low,
            jax.ShapeDtypeStruct((tokens // 2, depth), F32), sent((tokens // 2, depth)),
        ],
        scratch_shapes=[pltpu.VMEM((tokens, depth), F32), pltpu.VMEM((tile, depth), BF16)],
        compiler_params=pltpu.CompilerParams(vmem_limit_bytes=MORE),
        cost_estimate=HINT,
        name="ffn_pass",
    )(x, cot, blocks, blocks, blocks, blocks)


def down_kernel(hidden_ref, down_a_ref, down_b_ref, near_ref, far_ref, sum_ref):
    hidden = hidden_ref[...]
    n = down_a_ref.shape[2]
    first = pl.program_id(0) == 0
    for k, ref in enumerate((down_a_ref, down_b_ref)):
        at = slice(k * n, (k + 1) * n)
        part = matmul(hidden, joined(ref))

        @pl.when(first)
        def _(part=part, at=at):
            sum_ref[:, at] = part

        @pl.when(jnp.logical_not(first))
        def _(part=part, at=at):
            sum_ref[:, at] += part

    @pl.when(pl.program_id(0) == pl.num_programs(0) - 1)
    def _():
        half = near_ref.shape[0]
        near_ref[...] = sum_ref[:half, :]
        far_ref[...] = sum_ref[half:, :].astype(BF16)


def down_pass(hidden, blocks, depth, rows, tiles, piece):
    tokens, n = hidden.shape
    shards, _, tile = blocks.shape
    at = 2 * tiles * rows // piece
    half = pl.BlockSpec((tokens // 2, depth), lambda j: (0, 0))
    return pl.pallas_call(
        down_kernel,
        grid=(2,),
        in_specs=[
            pl.BlockSpec((tokens, n // 2), lambda j: (0, j)),
            *[pl.BlockSpec((shards // 2, piece, tile), lambda j, k=k: (j, at + k, 0)) for k in range(2)],
        ],
        out_specs=[half, half],
        out_shape=[jax.ShapeDtypeStruct((tokens // 2, depth), F32), sent((tokens // 2, depth))],
        scratch_shapes=[pltpu.VMEM((tokens, depth), F32)],
        compiler_params=pltpu.CompilerParams(vmem_limit_bytes=VMEM),
        cost_estimate=HINT,
        name="down_pass",
    )(hidden, blocks, blocks)


def joined(ref):
    v = ref[...]
    if v.shape[1] % 16:
        return widen(v).reshape(-1, v.shape[2]).astype(BF16)
    return v.reshape(-1, v.shape[2])


def away_kernel(at_ref, left_ref, right_ref, out_ref):
    out_ref[...] = matmul(joined(left_ref), right_ref[...]).reshape(out_ref.shape).astype(out_ref.dtype)


def home_kernel(bit, at_ref, left_ref, right_ref, got_ref, keep_ref, send_ref, sum_ref):
    v = matmul(joined(left_ref), right_ref[...]).reshape(got_ref.shape) + widen(got_ref[...])
    sum_ref[...] = v.reshape(sum_ref.shape)
    keep_ref[...] = sum_ref[:, at_ref[bit]].astype(keep_ref.dtype)
    send_ref[...] = sum_ref[:, 1 - at_ref[bit]].astype(send_ref.dtype)


def column_tile(n, choices=(1024, 768, 512, 256, 128)):
    return max(t for t in choices if n % t == 0)


def tiling(right, columns, skip):
    parts, _, n = right.shape
    tile = column_tile(columns or n)
    each = n // tile

    def index(j, at):
        at_tile = j + (at[0] if skip < 0 else skip)
        return at_tile // each, 0, at_tile % each

    return tile, columns or parts * n, index


def grad_away(left, right, at, columns=0, skip=0):
    owners, _, rows, tokens = left.shape
    tile, n, index = tiling(right, columns, skip)
    return pl.pallas_call(
        away_kernel,
        grid_spec=pltpu.PrefetchScalarGridSpec(
            num_scalar_prefetch=1,
            grid=(n // tile,),
            in_specs=[
                pl.BlockSpec((owners, None, rows, tokens), lambda j, at: (0, 1 - at[1], 0, 0)),
                pl.BlockSpec((None, tokens, tile), index),
            ],
            out_specs=pl.BlockSpec((owners, rows, tile), lambda j, at: (0, 0, j)),
        ),
        out_shape=sent((owners, rows, n)),
        compiler_params=pltpu.CompilerParams(vmem_limit_bytes=LESS),
        cost_estimate=HINT,
        name="grad_away",
    )(at, left, right)


def grad_home(left, right, got, at, bit, low, columns=0, skip=0):
    owners, _, rows, tokens = left.shape
    tile, n, index = tiling(right, columns, skip)
    high = owners // (2 * low)
    half = pl.BlockSpec((high, low, rows, tile), lambda j, at: (0, 0, 0, j))
    return pl.pallas_call(
        functools.partial(home_kernel, bit),
        grid_spec=pltpu.PrefetchScalarGridSpec(
            num_scalar_prefetch=1,
            grid=(n // tile,),
            in_specs=[
                pl.BlockSpec((owners, None, rows, tokens), lambda j, at: (0, at[1], 0, 0)),
                pl.BlockSpec((None, tokens, tile), index),
                pl.BlockSpec((owners, rows, tile), lambda j, at: (0, 0, j)),
            ],
            out_specs=[half, half],
            scratch_shapes=[pltpu.VMEM((high, 2, low, rows, tile), F32)],
        ),
        out_shape=[
            jax.ShapeDtypeStruct((high, low, rows, n), KEEP), sent((high, low, rows, n)),
        ],
        compiler_params=pltpu.CompilerParams(vmem_limit_bytes=LESS),
        cost_estimate=HINT,
        name="grad_home",
    )(at, left, right, got)


def fold_kernel(bit, at_ref, own_ref, got_ref, keep_ref, send_ref):
    mine, other = at_ref[bit], 1 - at_ref[bit]
    keep_ref[...] = (widen(own_ref[:, mine]) + widen(got_ref[:, mine])).astype(keep_ref.dtype)
    send_ref[...] = (widen(own_ref[:, other]) + widen(got_ref[:, other])).astype(BF16)


def fold(own, got, at, bit, low):
    rows, n = own.shape[2:]
    high = own.shape[0] * own.shape[1] // (2 * low)
    tile = column_tile(n, (2304, 2048, 1536, 1024, 768, 512, 256, 128))
    both = pl.BlockSpec((high, 2, low, rows, tile), lambda j, at: (0, 0, 0, 0, j))
    half = pl.BlockSpec((high, low, rows, tile), lambda j, at: (0, 0, 0, j))
    shape = (high, 2, low, rows, n)
    return pl.pallas_call(
        functools.partial(fold_kernel, bit),
        grid_spec=pltpu.PrefetchScalarGridSpec(
            num_scalar_prefetch=1, grid=(n // tile,), in_specs=[both, both], out_specs=[half, half]
        ),
        out_shape=[
            jax.ShapeDtypeStruct((high, low, rows, n), KEEP), sent((high, low, rows, n)),
        ],
        compiler_params=pltpu.CompilerParams(vmem_limit_bytes=LESS),
        cost_estimate=HINT,
        name="fold",
    )(at, own.reshape(shape), got.reshape(shape))


def settle_kernel(own_ref, got_ref, out_ref, low_ref):
    v = widen(own_ref[...]) + widen(got_ref[...])
    out_ref[...] = v
    low_ref[...] = v.astype(BF16)


def settle(own, got):
    rows, n = own.shape
    tile = column_tile(n, (2304, 2048, 1536, 1024, 768, 512, 256, 128))
    one = pl.BlockSpec((rows, tile), lambda j: (0, j))
    return pl.pallas_call(
        settle_kernel,
        grid=(n // tile,),
        in_specs=[one, one],
        out_specs=[one, one],
        out_shape=[jax.ShapeDtypeStruct((rows, n), F32), sent((rows, n))],
        compiler_params=pltpu.CompilerParams(vmem_limit_bytes=LESS),
        cost_estimate=HINT,
        name="settle",
    )(own, got)


def shifted(values, offset):
    if offset == 0:
        return values
    if offset > 0:
        return jnp.pad(values, ((0, 0), (offset, 0), (0, 0)))[:, : values.shape[1]]
    return jnp.pad(values, ((0, 0), (0, -offset), (0, 0)))[:, -offset:]


def body(
    groups, shards,
    tokens, cotangent, mix_gain, branch_proj, lruin_proj, conv_kernel, conv_bias, recur_proj, recur_bias,
    admit_proj, admit_bias, decay_param, out_proj, ffn_gain, ffn_gate, ffn_up, ffn_down,
):
    cores, bits = 2, shards.bit_length() - 1
    side = lax.axis_index("rep") % 2
    here = lax.axis_index("shard")
    taps = conv_kernel.shape[0]
    length, width = tokens.shape
    low_r = branch_proj.shape[1]
    half_r = low_r // 2
    half_f = ffn_gate.shape[1] // 2
    piece_f = half_f // shards

    def swap(v):
        return lax.ppermute(v, "rep", [(i, i ^ 1) for i in range(groups)])

    def swap_rows(v):
        v = swap(v)
        return jnp.concatenate([v[length:], v[:length]], axis=0)

    def mine(v, size, axis):
        return lax.dynamic_slice_in_dim(v, side * size, size, axis)

    def theirs(v, size, axis):
        return lax.dynamic_slice_in_dim(v, (1 - side) * size, size, axis)

    def natural(own, other):
        first = jnp.where(side == 0, own, other)
        second = jnp.where(side == 0, other, own)
        return jnp.concatenate([first, second], axis=-1)

    def with_pair(own):
        return jnp.concatenate([own, swap(own)], axis=0)

    clock = []

    def tick(*xs):
        return lax.optimization_barrier(tuple(xs) + tuple(clock))[: len(xs)]

    def tock(*ys):
        clock[:] = ys

    place = jnp.stack([side] + [(here >> i) & 1 for i in range(bits)]).astype(jnp.int32)
    here_side = place[:1]

    def cross(v, bit):
        return lax.ppermute(v, "shard", [(i, i ^ (1 << bit)) for i in range(shards)])

    class Scatter:
        def __init__(self, left, right, order=None, columns=0, skip=0):
            self.right, = tick(right if right.ndim == 3 else right[None])
            self.left = left.reshape(shards // cores, cores, left.shape[0] // shards, left.shape[1])
            self.order = list(order or range(1, bits))
            self.span = dict(columns=columns, skip=skip)
            send = grad_away(self.left, self.right, place, **self.span)
            tock(send)
            self.got = cross(send, 0)

        def next(self):
            bit, rest = self.order[0], self.order[1:]
            self.order = rest
            return bit, 2 ** sum(other < bit for other in rest)

        def home(self):
            right, got = tick(self.right, self.got)
            bit, low = self.next()
            self.v, send = grad_home(self.left, right, got, place, bit + 1, low, **self.span)
            tock(self.v, send)
            self.got = cross(send, bit)

        def fold(self):
            v, got = tick(self.v, self.got)
            bit, low = self.next()
            self.v, send = fold(v, got, place, bit + 1, low)
            tock(self.v, send)
            self.got = cross(send, bit)

        def two(self):
            while len(self.order) > 1:
                self.fold()

        def settle(self):
            v, got = tick(self.v, self.got)
            v, send = settle(v.reshape(v.shape[2:]), got.reshape(got.shape[2:]))
            tock(v, send)
            if groups > 2:
                total = v
                for k in range(1, groups // 2):
                    total = total + lax.ppermute(v, "rep", [(i, (i + 2 * k) % groups) for i in range(groups)])
                v, send = total, total.astype(BF16)
            self.v, self.got = v, swap(send)

        def both(self):
            return tick(self.v, self.got)

    per_d, per_r = mix_gain.shape[0], conv_bias.shape[0]
    vectors = jnp.concatenate(
        [mix_gain, ffn_gain, conv_kernel.reshape(-1), conv_bias, recur_bias, admit_bias, decay_param]
    )
    count = vectors.shape[0]
    vectors = jnp.pad(vectors, (0, -count % 128)).reshape(-1, 128)
    vectors = lax.all_gather(vectors, "shard", axis=0).reshape(shards, -1)[:, :count]
    gain_one = widen(vectors[:, :per_d].reshape(width))
    gain_two = widen(vectors[:, per_d : 2 * per_d].reshape(width))
    channel = vectors[:, 2 * per_d :].reshape(shards, taps + 4, per_r).transpose(1, 0, 2).reshape(taps + 4, low_r)
    channel = widen(mine(channel, half_r, 1))
    taps_half, cbias = channel[:taps], channel[taps]
    rbias, abias, lam = channel[taps + 1], channel[taps + 2], channel[taps + 3]
    rate = DECAY_SCALE * jax.nn.softplus(-lam)
    params = jnp.concatenate([jnp.stack([rbias, abias, rate]), jnp.zeros((5, half_r), F32)])

    def ffn_half(v):
        return lax.dynamic_index_in_dim(v.reshape(v.shape[0], shards, 2, piece_f), side, 2, False).reshape(v.shape[0], half_f)

    def gather_blocks(parts, block):
        rows = [p[:, at : at + block] for p in parts for at in range(0, p.shape[1], block)]
        return lax.all_gather(jnp.concatenate(rows, axis=0), "shard", axis=0)

    def unpack(whole, at, rows, columns):
        block = whole.shape[2]
        cols = [whole[:, at + i * rows : at + (i + 1) * rows].reshape(shards * rows, block) for i in range(columns // block)]
        return jnp.concatenate(cols, axis=1)

    per_f, tiles = 2 * piece_f, 3
    whole = lax.all_gather(
        pack(here_side, [branch_proj, lruin_proj, recur_proj, admit_proj], out_proj, 512), "shard", axis=0
    )
    ffn_blocks = gather_blocks(
        [ffn_half(ffn_gate), ffn_half(ffn_up), mine(ffn_down, piece_f, 0)], half_f // tiles
    )
    cot_pair = with_pair(cotangent)
    values = widen(with_pair(tokens))
    scale_one = lax.rsqrt(jnp.mean(values * values, axis=-1, keepdims=True) + EPS)
    normed = (values * scale_one * gain_one).astype(BF16)
    normed_t = flip(normed)
    tock(normed_t, cot_pair)
    whole, = tick(whole)
    at = low_r // 512 * per_d
    w1 = unpack(whole, 0, per_d, low_r)
    w2 = unpack(whole, at, per_r, low_r)
    w3 = unpack(whole, at + low_r // 512 * per_r, per_r, width)
    pre = matmul(normed, w1)
    lru_pre = pre[:, half_r:].reshape(2, length, half_r)
    conv = cbias
    for k in range(taps):
        conv = conv + taps_half[k] * shifted(lru_pre, k)
    admitted = conv.reshape(2 * length, half_r).astype(BF16)
    admitted_all = natural(admitted, swap_rows(admitted))
    gates = matmul(admitted_all, w2)
    mixed, *factors = recurrence_forward(pre, gates, admitted, params, length)
    tock(mixed)
    admitted_all, = tick(admitted_all)
    admitted_t = flip(admitted_all)
    tock(admitted_t)
    mixed_other, = tick(swap(mixed[length:]))
    mixed_own = natural(mixed[:length], mixed_other)
    middle = widen(tokens) + matmul(mixed_own, w3)
    scale_two = lax.rsqrt(jnp.mean(middle * middle, axis=-1, keepdims=True) + EPS)
    normed_two = (middle * scale_two * gain_two).astype(BF16)
    tock(normed_two)
    mixed_late, mixed_far = tick(mixed[length:], swap(mixed[:length]))
    mixed_t = flip(jnp.concatenate([mixed_own, natural(mixed_late, mixed_far)], axis=0))
    tock(mixed_t)
    normed_two = jnp.concatenate([normed_two, *tick(swap(normed_two))], axis=0)
    tock(normed_two)
    ffn_blocks, = tick(ffn_blocks)

    ffn = dict(rows=per_d, tiles=tiles)
    have, grads, steps = {}, {}, {}

    def step(run):
        steps[run.__name__] = run
        return run

    @step
    def ffn_in():
        x, = tick(normed_two)
        have["hidden"], have["hidden_t"], have["gate_cot"], have["up_cot"], near, far = ffn_pass(
            x, cot_pair, ffn_blocks, piece=piece_f, **ffn
        )
        tock(near, far)
        have["ffn"] = near, swap(far)

    @step
    def turn():
        x, = tick(normed_two)
        have["normed_two_t"] = flip(x)
        tock(have["normed_two_t"])

    @step
    def norm_two():
        near, far = tick(*have["ffn"])
        have["middle_cot"], low = norm_back(near, far, cotangent, middle, gain_two)
        tock(have["middle_cot"], low)
        have["middle_low"] = low, swap(low)

    @step
    def mixer():
        low, other = tick(*have["middle_low"])
        have["branch_low"], have["gates_cot"], have["direct"], have["sums"], near, far = chain_back(
            here_side, low, other, whole, at, per_r, factors
        )
        have["out_cot"] = jnp.concatenate([low, other], axis=0)
        tock(near, far)
        have["admitted"] = near, swap(far)

    @step
    def conv_in():
        direct, near, far = tick(have["direct"], *have["admitted"])
        have["pre_cot"], have["conv_sums"], near, far = conv_back(
            direct, near, far, pre, have["branch_low"], channel, whole, per_d, width
        )
        tock(near, far, have["pre_cot"])
        have["normed"] = near, swap(far)

    @step
    def norm_one():
        near, far = tick(*have["normed"])
        have["tokens_grad"], _ = norm_back(near, far, have["middle_cot"], tokens, gain_one)
        tock(have["tokens_grad"])

    @step
    def down():
        x, = tick(have["hidden"])
        near, far = down_pass(x, ffn_blocks, width, piece=piece_f, **ffn)
        tock(near, far)
        have["down"] = near, swap(far)

    @step
    def result():
        near, far = tick(*have["down"])
        have["block_out"] = (middle + near + widen(far)).astype(BF16)
        tock(have["block_out"])

    @step
    def small():
        conv_sums, sums = tick(have["conv_sums"], have["sums"])
        sums = jnp.sum(sums.reshape(3, ROWS, half_r), axis=1)
        v = jnp.concatenate([conv_sums[: taps + 1], sums[:2], sums[2:] * (DECAY_SCALE * jax.nn.sigmoid(-lam))])
        v = natural(v, jnp.zeros_like(v))
        tock(v)
        have["small"] = lax.psum(v, ("rep", "shard"))

    @step
    def small_end():
        v, = tick(have["small"])
        have["small"] = lax.dynamic_slice_in_dim(v, here * per_r, per_r, 1)
        tock(have["small"])

    def late(name, left, right, order=None, **span):
        def away():
            grads[name] = Scatter(left(), right(), order, **span)

        steps["away_" + name] = away
        for stage in ("home", "two", "fold", "settle"):
            steps[stage + "_" + name] = lambda stage=stage: getattr(grads[name], stage)()

    z_first = [2, 1] + list(range(3, bits))
    late("d", lambda: have["hidden_t"], lambda: cot_pair)
    late("g", lambda: have["normed_two_t"], lambda: have["gate_cot"])
    late("u", lambda: have["normed_two_t"], lambda: have["up_cot"], z_first)
    late("r", lambda: admitted_t, lambda: have["gates_cot"], z_first)
    late("b", lambda: normed_t, lambda: have["pre_cot"])
    late("o", lambda: mixed_t, lambda: have["out_cot"], columns=width // 2, skip=-1)

    @step
    def join_d():
        v, got = grads["d"].both()
        have["d"] = join_rows(here_side, v, got)
        tock(have["d"])

    @step
    def join_g():
        have["g"] = weave(here_side, *grads["g"].both(), piece_f)
        tock(have["g"])

    @step
    def join_u():
        have["u"] = weave(here_side, *grads["u"].both(), piece_f)
        tock(have["u"])

    @step
    def join_r():
        have["r"] = join_columns(here_side, *grads["r"].both(), 2)
        tock(*have["r"])

    @step
    def join_b():
        have["b"] = join_columns(here_side, *grads["b"].both(), 2)
        tock(*have["b"])

    @step
    def join_o():
        have["o"], = join_columns(here_side, *grads["o"].both(), 1)
        tock(have["o"])

    for name in STEPS:
        steps[name]()
    small_grad, (branch_grad, lruin_grad) = have["small"], have["b"]
    ffngain_grad = jnp.sum(have["g"] * widen(ffn_gate) + have["u"] * widen(ffn_up), axis=1) / widen(ffn_gain)
    mixgain_grad = jnp.sum(branch_grad * widen(branch_proj) + lruin_grad * widen(lruin_proj), axis=1) / widen(mix_gain)
    return (
        have["block_out"], have["tokens_grad"], mixgain_grad, branch_grad, lruin_grad, small_grad[:taps],
        small_grad[taps], have["r"][0], small_grad[taps + 1], have["r"][1], small_grad[taps + 2],
        small_grad[taps + 3], have["o"], ffngain_grad, have["g"], have["u"], have["d"],
    )


def solution(mesh):
    groups, shards = mesh.shape["rep"], mesh.shape["shard"]
    whole = P(("rep", "shard"), None)
    row, vec, col = P("shard", None), P("shard"), P(None, "shard")
    in_specs = (whole, whole, vec, row, row, col, vec, row, vec, row, vec, vec, row, vec, row, row, row)
    out_specs = (whole, whole, vec, row, row, col, vec, row, vec, row, vec, vec, row, vec, row, row, row)
    return jax.shard_map(
        functools.partial(body, groups, shards), mesh=mesh, in_specs=in_specs, out_specs=out_specs, check_vma=False
    )
```

```python
import functools
import math

import jax
import jax.numpy as jnp
from jax import lax
from jax.experimental import pallas as pl
from jax.experimental.pallas import tpu as pltpu
from jax.sharding import PartitionSpec as P

EPS = 1e-06
DECAY_SCALE = 8.0
ROOT_FLOOR = 0.001
GELU_K = math.sqrt(2.0 / math.pi)
GELU_C = 0.044715
ROWS = 16
FACTORS = 7
VMEM = 44 << 20
LESS = 24 << 20
MORE = 50 << 20
PARTS = 2
STEPS = (
    "turn", "ffn_in", "away_d", "away_u", "norm_two", "home_u", "home_d", "away_g", "mixer", "away_r", "two_u",
    "two_d", "home_g", "home_r", "fold_u", "conv_in", "fold_d", "away_b", "small", "settle_u", "down", "home_b",
    "norm_one", "two_g", "two_r", "join_u", "two_b", "away_o", "fold_g", "settle_d", "home_o", "fold_r", "settle_g",
    "join_d", "two_o", "fold_b", "join_g", "settle_r", "fold_o", "result", "settle_b", "small_end", "join_r",
    "settle_o", "join_b", "join_o",
)
HINT = pl.CostEstimate(flops=100000000000, bytes_accessed=1024, transcendentals=0)
BF16 = jnp.bfloat16
F32 = jnp.float32
KEEP = BF16


def sent(shape):
    return pltpu.HBM(shape, BF16)


def matmul(left, right):
    return jnp.dot(left, right, preferred_element_type=F32)


def rows_product(left, right):
    return lax.dot_general(left, right, (((0,), (0,)), ((), ())), preferred_element_type=F32)


def cols_product(left, right):
    return lax.dot_general(left, right, (((1,), (1,)), ((), ())), preferred_element_type=F32)


def widen(value):
    return value.astype(F32)


def gelu(v):
    return 0.5 * v * (1.0 + jnp.tanh(GELU_K * (v + GELU_C * v * v * v)))


def gelu_slope(v):
    t = jnp.tanh(GELU_K * (v + GELU_C * v * v * v))
    return 0.5 * (1.0 + t) + 0.5 * v * (1.0 - t * t) * GELU_K * (1.0 + 3.0 * GELU_C * v * v)


def forward_kernel(pre_ref, gates_r_ref, gates_i_ref, admitted_ref, params_ref, mixed_ref, *factor_refs):
    width = pre_ref.shape[1]
    rbias, abias, rate = params_ref[0:1, :], params_ref[1:2, :], params_ref[2:3, :]
    row = lax.broadcasted_iota(jnp.int32, (ROWS, width), 0)

    def step(i, carry):
        at = pl.ds(pl.multiple_of(i * ROWS, ROWS), ROWS)
        gate_r = jax.nn.sigmoid(gates_r_ref[at, :] + rbias)
        gate_i = jax.nn.sigmoid(gates_i_ref[at, :] + abias)
        admitted = widen(admitted_ref[at, :])
        decay = jnp.exp(-(gate_r * rate))
        rest = 1.0 - decay * decay
        root = jnp.sqrt(jnp.maximum(rest, ROOT_FLOOR))
        through = root * gate_i
        a, b = decay, through * admitted
        for d in (1, 2, 4, 8):
            keep = row >= d
            b = b + a * jnp.where(keep, pltpu.roll(b, d, 0), 0.0)
            a = a * jnp.where(keep, pltpu.roll(a, d, 0), 1.0)
        state = b + a * carry
        before = jnp.where(row >= 1, pltpu.roll(state, 1, 0), carry)
        pre = pre_ref[at, :]
        t = jnp.tanh(GELU_K * (pre + GELU_C * pre * pre * pre))
        act = 0.5 * pre * (1.0 + t)
        slope = 0.5 * (1.0 + t) + 0.5 * pre * (1.0 - t * t) * GELU_K * (1.0 + 3.0 * GELU_C * pre * pre)
        mixed_ref[at, :] = (state * act).astype(BF16)
        share = jnp.where(rest > ROOT_FLOOR, 1.0, jnp.where(rest == ROOT_FLOOR, 0.5, 0.0))
        log = decay * (before - gate_i * admitted * (share * decay / root))
        factors = (
            decay, act, state * slope, through, through * admitted * (1.0 - gate_i),
            -(log * rate) * gate_r * (1.0 - gate_r), log * gate_r,
        )
        for ref, factor in zip(factor_refs, factors, strict=True):
            ref[at, :] = factor
        return jnp.broadcast_to(state[ROWS - 1 : ROWS, :], (ROWS, width))

    lax.fori_loop(0, pre_ref.shape[0] // ROWS, step, jnp.zeros((ROWS, width), F32))


def chain_kernel(
    side_ref, own_ref, other_ref, out_a_ref, out_b_ref, out_c_ref, recur_w_ref, admit_w_ref, decay_ref, act_ref,
    branch_f_ref, direct_f_ref, admit_f_ref, recur_f_ref, rate_f_ref,
    branch_ref, gates_cot_ref, direct_ref, sums_ref, near_ref, far_ref, cot_ref, sum_ref,
):
    length = own_ref.shape[0]
    width = act_ref.shape[1]
    out_w = jnp.concatenate([joined(out_a_ref), joined(out_b_ref), joined(out_c_ref)], axis=1)
    cot_ref[:length, :] = cols_product(own_ref[...], out_w)
    cot_ref[length:, :] = cols_product(other_ref[...], out_w)
    row = lax.broadcasted_iota(jnp.int32, (ROWS, width), 0)
    blocks = length // ROWS
    zero = jnp.zeros((ROWS, width), F32)

    def step(first, i, state):
        carry, sum_r, sum_i, sum_d = state
        at = pl.ds(pl.multiple_of(first + (blocks - 1 - i) * ROWS, ROWS), ROWS)
        cot = cot_ref[at, :]
        branch_ref[at, :] = (cot * branch_f_ref[at, :]).astype(BF16)
        own = cot * act_ref[at, :]
        f = decay_ref[at, :]
        e = f * own
        for d in (1, 2, 4, 8):
            keep = row < ROWS - d
            e = e + f * jnp.where(keep, pltpu.roll(e, ROWS - d, 0), 0.0)
            f = f * jnp.where(keep, pltpu.roll(f, ROWS - d, 0), 1.0)
        e = e + f * carry
        g = own + jnp.where(row < ROWS - 1, pltpu.roll(e, ROWS - 1, 0), carry)
        direct_ref[at, :] = g * direct_f_ref[at, :]
        recur = g * recur_f_ref[at, :]
        admit = g * admit_f_ref[at, :]
        gates_cot_ref[0, at, :] = recur.astype(BF16)
        gates_cot_ref[1, at, :] = admit.astype(BF16)
        carry = jnp.broadcast_to(e[0:1, :], (ROWS, width))
        return carry, sum_r + recur, sum_i + admit, sum_d + g * rate_f_ref[at, :]

    sums = (zero, zero, zero)
    for first in (0, length):
        _, *sums = lax.fori_loop(0, blocks, functools.partial(step, first), (zero, *sums))
    for i in range(3):
        sums_ref[i * ROWS : (i + 1) * ROWS, :] = sums[i]
    depth = sum_ref.shape[1]
    part = cols_product(gates_cot_ref[0], joined(recur_w_ref)) + cols_product(gates_cot_ref[1], joined(admit_w_ref))

    @pl.when(pl.program_id(0) == 0)
    def _():
        sum_ref[...] = part

    @pl.when(pl.program_id(0) > 0)
    def _():
        sum_ref[...] += part

    half = depth // 2
    for side in range(2):
        @pl.when((pl.program_id(0) == pl.num_programs(0) - 1) & (side_ref[0] == side))
        def _(side=side):
            near_ref[...] = sum_ref[:, side * half : (side + 1) * half]
            away = slice((1 - side) * half, (2 - side) * half)
            far_ref[:length, :] = sum_ref[length:, away].astype(BF16)
            far_ref[length:, :] = sum_ref[:length, away].astype(BF16)


def chain_back(side, own, other, whole, at, rows, factors):
    length, depth = own.shape
    tokens, width = factors[0].shape
    shards, _, tile = whole.shape
    n = width // tile
    at = at // rows
    low = jax.ShapeDtypeStruct((tokens, width), BF16)
    full = pl.BlockSpec((length, depth), lambda j, s: (0, 0))
    near = pl.BlockSpec((tokens, tile), lambda j, s: (0, j))
    fixed = pl.BlockSpec((tokens, width), lambda j, s: (0, 0))
    return pl.pallas_call(
        chain_kernel,
        grid_spec=pltpu.PrefetchScalarGridSpec(
            num_scalar_prefetch=1,
            grid=(n,),
            in_specs=[
                full, full,
                *[
                    pl.BlockSpec((tile // rows, rows, tile), lambda j, s, k=k: (s[0] * n + j, at + 2 * n + k, 0))
                    for k in range(3)
                ],
                pl.BlockSpec((shards, rows, tile), lambda j, s: (0, at + j, 0)),
                pl.BlockSpec((shards, rows, tile), lambda j, s: (0, at + n + j, 0)),
                *[near] * FACTORS,
            ],
            out_specs=[
                near, pl.BlockSpec((2, tokens, tile), lambda j, s: (0, 0, j)), near,
                pl.BlockSpec((3 * ROWS, tile), lambda j, s: (0, j)), fixed, fixed,
            ],
            scratch_shapes=[pltpu.VMEM((tokens, tile), F32), pltpu.VMEM((tokens, 2 * width), F32)],
        ),
        out_shape=[
            low, jax.ShapeDtypeStruct((2, tokens, width), BF16), jax.ShapeDtypeStruct((tokens, width), F32),
            jax.ShapeDtypeStruct((3 * ROWS, width), F32), jax.ShapeDtypeStruct((tokens, width), F32), sent((tokens, width)),
        ],
        compiler_params=pltpu.CompilerParams(vmem_limit_bytes=VMEM),
        cost_estimate=HINT,
        name="chain_back",
    )(side, own, other, *[whole] * 5, *factors)


def conv_kernel(
    direct_ref, near_in_ref, far_in_ref, lru_ref, branch_ref, taps_ref, branch_w_ref, lruin_w_ref,
    pre_cot_ref, sums_ref, near_ref, far_ref, sum_ref,
):
    tokens, width = direct_ref.shape
    length = tokens // 2
    cot = direct_ref[...] + near_in_ref[...] + widen(far_in_ref[...])
    lru = lru_ref[...]
    token = lax.broadcasted_iota(jnp.int32, (tokens, width), 0)
    token = jnp.where(token >= length, token - length, token)
    total = jnp.zeros_like(cot)
    count = 4
    for k in range(count):
        later = cot if k == 0 else jnp.where(token < length - k, pltpu.roll(cot, tokens - k, 0), 0.0)
        total = total + taps_ref[k : k + 1, :] * later
        sums_ref[k : k + 1, :] = jnp.sum(later * lru, axis=0, keepdims=True)
    sums_ref[count : count + 1, :] = jnp.sum(cot, axis=0, keepdims=True)
    low = total.astype(BF16)
    pre_cot_ref[0] = branch_ref[...]
    pre_cot_ref[1] = low
    part = cols_product(branch_ref[...], joined(branch_w_ref)) + cols_product(low, joined(lruin_w_ref))

    @pl.when(pl.program_id(0) == 0)
    def _():
        sum_ref[...] = part

    @pl.when(pl.program_id(0) > 0)
    def _():
        sum_ref[...] += part

    @pl.when(pl.program_id(0) == pl.num_programs(0) - 1)
    def _():
        near_ref[...] = sum_ref[:length, :]
        far_ref[...] = sum_ref[length:, :].astype(BF16)


def conv_back(direct, near, far, pre, branch, taps, whole, rows, depth):
    tokens, width = direct.shape
    shards, _, tile = whole.shape
    n = width // tile
    one = pl.BlockSpec((tokens, tile), lambda j: (0, j))
    half = pl.BlockSpec((tokens // 2, depth), lambda j: (0, 0))
    return pl.pallas_call(
        conv_kernel,
        grid=(n,),
        in_specs=[
            one, one, one, pl.BlockSpec((tokens, tile), lambda j: (0, j + n)), one,
            pl.BlockSpec((8, tile), lambda j: (0, j)),
            pl.BlockSpec((shards, rows, tile), lambda j: (0, j, 0)),
            pl.BlockSpec((shards, rows, tile), lambda j: (0, n + j, 0)),
        ],
        out_specs=[
            pl.BlockSpec((2, tokens, tile), lambda j: (0, 0, j)), pl.BlockSpec((8, tile), lambda j: (0, j)), half, half,
        ],
        out_shape=[
            jax.ShapeDtypeStruct((2, tokens, width), BF16), jax.ShapeDtypeStruct((8, width), F32),
            jax.ShapeDtypeStruct((tokens // 2, depth), F32), sent((tokens // 2, depth)),
        ],
        scratch_shapes=[pltpu.VMEM((tokens, depth), F32)],
        compiler_params=pltpu.CompilerParams(vmem_limit_bytes=VMEM),
        cost_estimate=HINT,
        name="conv_back",
    )(direct, near, far, pre, branch, taps, whole, whole)


def norm_kernel(near_ref, far_ref, base_ref, v_ref, gain_ref, out_ref, low_ref):
    v = widen(v_ref[...])
    scale = lax.rsqrt(jnp.mean(v * v, axis=-1, keepdims=True) + EPS)
    g = (near_ref[...] + widen(far_ref[...])) * gain_ref[0:1, :]
    out = widen(base_ref[...]) + scale * (g - v * (scale * scale * jnp.mean(g * v, axis=-1, keepdims=True)))
    out_ref[...] = out
    low_ref[...] = out.astype(BF16)


def norm_back(near, far, base, v, gain):
    rows, width = near.shape
    tile = rows // 4
    one = pl.BlockSpec((tile, width), lambda j: (j, 0))
    return pl.pallas_call(
        norm_kernel,
        grid=(rows // tile,),
        in_specs=[one, one, one, one, pl.BlockSpec((8, width), lambda j: (0, 0))],
        out_specs=[one, one],
        out_shape=[jax.ShapeDtypeStruct((rows, width), F32), sent((rows, width))],
        compiler_params=pltpu.CompilerParams(vmem_limit_bytes=LESS),
        cost_estimate=HINT,
        name="norm_back",
    )(near, far, base, v, jnp.broadcast_to(gain, (8, width)))


def flip_kernel(x_ref, out_ref):
    out_ref[...] = widen(x_ref[...]).T.astype(BF16)


def flip(x):
    tokens, n = x.shape
    tile = 256
    return pl.pallas_call(
        flip_kernel,
        grid=(n // tile,),
        in_specs=[pl.BlockSpec((tokens, tile), lambda j: (0, j))],
        out_specs=pl.BlockSpec((tile, tokens), lambda j: (j, 0)),
        out_shape=jax.ShapeDtypeStruct((n, tokens), BF16),
        compiler_params=pltpu.CompilerParams(vmem_limit_bytes=LESS),
        cost_estimate=HINT,
        name="flip",
    )(x)


def pack_kernel(block, side_ref, *refs):
    out_ref, at = refs[-1], 0
    for ref in refs[:-1]:
        rows, n = ref.shape
        for first in range(0, n, block):
            out_ref[at : at + rows, :] = ref[:, first : first + block]
            at += rows


def pack(side, halves, full, block):
    specs = [pl.BlockSpec((p.shape[0], p.shape[1] // 2), lambda j, s: (0, s[0])) for p in halves]
    specs.append(pl.BlockSpec(full.shape, lambda j, s: (0, 0)))
    size = sum(p.shape[0] * p.shape[1] // 2 for p in halves) + full.size
    return pl.pallas_call(
        functools.partial(pack_kernel, block),
        grid_spec=pltpu.PrefetchScalarGridSpec(
            num_scalar_prefetch=1, grid=(1,), in_specs=specs,
            out_specs=pl.BlockSpec((size // block, block), lambda j, s: (0, 0)),
        ),
        out_shape=jax.ShapeDtypeStruct((size // block, block), BF16),
        compiler_params=pltpu.CompilerParams(vmem_limit_bytes=LESS),
        cost_estimate=HINT,
        name="pack",
    )(side, *[pltpu.with_memory_space_constraint(p, pltpu.HBM) for p in (*halves, full)])


def columns_kernel(parts, side_ref, own_ref, got_ref, *out_refs):
    n = out_refs[0].shape[1]
    mine = pl.program_id(0) == side_ref[0]

    @pl.when(mine)
    def _():
        for i in range(parts):
            out_refs[i][...] = own_ref[:, i * n : (i + 1) * n]

    @pl.when(jnp.logical_not(mine))
    def _():
        for i in range(parts):
            out_refs[i][...] = widen(got_ref[:, i * n : (i + 1) * n])


def join_columns(side, own, got, parts):
    rows, n = own.shape[0], own.shape[1] // parts
    full = pl.BlockSpec(own.shape, lambda h, s: (0, 0))
    return pl.pallas_call(
        functools.partial(columns_kernel, parts),
        grid_spec=pltpu.PrefetchScalarGridSpec(
            num_scalar_prefetch=1, grid=(2,), in_specs=[full, full],
            out_specs=[pl.BlockSpec((rows, n), lambda h, s: (0, h))] * parts,
        ),
        out_shape=[jax.ShapeDtypeStruct((rows, 2 * n), F32)] * parts,
        compiler_params=pltpu.CompilerParams(vmem_limit_bytes=LESS),
        cost_estimate=HINT,
        name="join_columns",
    )(side, own, got)


def rows_kernel(side_ref, own_ref, got_ref, out_ref):
    mine = pl.program_id(0) == side_ref[0]

    @pl.when(mine)
    def _():
        out_ref[...] = own_ref[...]

    @pl.when(jnp.logical_not(mine))
    def _():
        out_ref[...] = widen(got_ref[...])


def join_rows(side, own, got):
    rows, n = own.shape
    full = pl.BlockSpec((rows, n), lambda h, s: (0, 0))
    return pl.pallas_call(
        rows_kernel,
        grid_spec=pltpu.PrefetchScalarGridSpec(
            num_scalar_prefetch=1, grid=(2,), in_specs=[full] * 2,
            out_specs=pl.BlockSpec((rows, n), lambda h, s: (h, 0)),
        ),
        out_shape=jax.ShapeDtypeStruct((2 * rows, n), F32),
        compiler_params=pltpu.CompilerParams(vmem_limit_bytes=LESS),
        cost_estimate=HINT,
        name="join_rows",
    )(side, own, got)


def weave_kernel(piece, side_ref, own_ref, got_ref, out_ref):
    for side in range(2):
        @pl.when(side_ref[0] == side)
        def _(side=side):
            parts = []
            for at in range(0, own_ref.shape[1], piece):
                own = own_ref[:, at : at + piece]
                got = widen(got_ref[:, at : at + piece])
                parts += [got, own] if side else [own, got]
            out_ref[...] = jnp.concatenate(parts, axis=1)


def weave(side, own, got, piece):
    rows, n = own.shape
    return pl.pallas_call(
        functools.partial(weave_kernel, piece),
        grid_spec=pltpu.PrefetchScalarGridSpec(
            num_scalar_prefetch=1, grid=(1,),
            in_specs=[pl.BlockSpec((rows, n), lambda h, s: (0, 0))] * 2,
            out_specs=pl.BlockSpec((rows, 2 * n), lambda h, s: (0, 0)),
        ),
        out_shape=jax.ShapeDtypeStruct((rows, 2 * n), F32),
        compiler_params=pltpu.CompilerParams(vmem_limit_bytes=LESS),
        cost_estimate=HINT,
        name="weave",
    )(side, own, got)


def recurrence_forward(pre, gates, admitted, params, length):
    tokens, width = admitted.shape
    tile = math.gcd(width, 512)
    n = width // tile
    near = pl.BlockSpec((length, tile), lambda s, j: (s, j))
    far = pl.BlockSpec((length, tile), lambda s, j: (s, j + n))
    vector = pl.BlockSpec((8, tile), lambda s, j: (0, j))
    return pl.pallas_call(
        forward_kernel,
        grid=(tokens // length, n),
        in_specs=[near, near, far, near, vector],
        out_specs=[near] * (1 + FACTORS),
        out_shape=[jax.ShapeDtypeStruct((tokens, width), BF16)] + [jax.ShapeDtypeStruct((tokens, width), F32)] * FACTORS,
        cost_estimate=pl.CostEstimate(flops=60 * tokens * width, bytes_accessed=20 * tokens * width, transcendentals=6 * tokens * width),
        name="recurrence_forward",
    )(pre, gates, gates, admitted, params)


def take_tile(down_a_ref, down_b_ref, down_ref):
    rows, n = down_ref.shape[0], down_a_ref.shape[2]
    for j in range(shape_rows(down_a_ref) // rows):
        @pl.when(pl.program_id(0) == j)
        def _(j=j):
            down_ref[:, :n] = joined(down_a_ref)[j * rows : (j + 1) * rows]
            down_ref[:, n:] = joined(down_b_ref)[j * rows : (j + 1) * rows]


def shape_rows(ref):
    return ref.shape[0] * ref.shape[1]


def ffn_kernel(
    x_ref, cot_ref, gate_ref, up_ref, down_a_ref, down_b_ref,
    hidden_ref, flipped_ref, gate_cot_ref, up_cot_ref, near_ref, far_ref, sum_ref, down_ref,
):
    take_tile(down_a_ref, down_b_ref, down_ref)
    gate_w, up_w, down_w = joined(gate_ref), joined(up_ref), down_ref[...]
    tokens = x_ref.shape[0]
    for first in range(0, tokens, tokens // PARTS):
        rows = slice(first, first + tokens // PARTS)
        x = x_ref[rows, :]
        gate = matmul(x, gate_w)
        up = matmul(x, up_w)
        cot = cols_product(cot_ref[rows, :], down_w)
        t = jnp.tanh(GELU_K * (gate + GELU_C * gate * gate * gate))
        act = 0.5 * gate * (1.0 + t)
        slope = 0.5 * (1.0 + t) + 0.5 * gate * (1.0 - t * t) * GELU_K * (1.0 + 3.0 * GELU_C * gate * gate)
        hidden = act * up
        hidden_ref[rows, :] = hidden.astype(BF16)
        flipped_ref[:, rows] = hidden.T.astype(BF16)
        gate_cot = (cot * up * slope).astype(BF16)
        up_cot = (cot * act).astype(BF16)
        gate_cot_ref[rows, :] = gate_cot
        up_cot_ref[rows, :] = up_cot
        part = cols_product(gate_cot, gate_w) + cols_product(up_cot, up_w)

        @pl.when(pl.program_id(0) == 0)
        def _(part=part, rows=rows):
            sum_ref[rows, :] = part

        @pl.when(pl.program_id(0) > 0)
        def _(part=part, rows=rows):
            sum_ref[rows, :] += part

    @pl.when(pl.program_id(0) == pl.num_programs(0) - 1)
    def _():
        half = near_ref.shape[0]
        near_ref[...] = sum_ref[:half, :]
        far_ref[...] = sum_ref[half:, :].astype(BF16)


def down_specs(blocks, rows, tiles, piece):
    shards, _, tile = blocks.shape
    at = 2 * tiles * rows // piece
    return [pl.BlockSpec((shards, piece, tile), lambda j, k=k: (0, at + k, 0), pipeline_mode=pl.Buffered(1)) for k in range(2)]


def ffn_pass(x, cot, blocks, rows, tiles, piece):
    tokens, depth = x.shape
    shards, _, tile = blocks.shape
    n = tiles * tile
    low = jax.ShapeDtypeStruct((tokens, n), BF16)
    fixed = pl.BlockSpec((tokens, depth), lambda j: (0, 0))
    wide = pl.BlockSpec((tokens, tile), lambda j: (0, j))
    half = pl.BlockSpec((tokens // 2, depth), lambda j: (0, 0))
    return pl.pallas_call(
        ffn_kernel,
        grid=(tiles,),
        in_specs=[
            fixed, fixed,
            pl.BlockSpec((shards, rows, tile), lambda j: (0, j, 0)),
            pl.BlockSpec((shards, rows, tile), lambda j: (0, j + tiles, 0)),
            *down_specs(blocks, rows, tiles, piece),
        ],
        out_specs=[wide, pl.BlockSpec((tile, tokens), lambda j: (j, 0)), wide, wide, half, half],
        out_shape=[
            low, jax.ShapeDtypeStruct((n, tokens), BF16), low, low,
            jax.ShapeDtypeStruct((tokens // 2, depth), F32), sent((tokens // 2, depth)),
        ],
        scratch_shapes=[pltpu.VMEM((tokens, depth), F32), pltpu.VMEM((tile, depth), BF16)],
        compiler_params=pltpu.CompilerParams(vmem_limit_bytes=MORE),
        cost_estimate=HINT,
        name="ffn_pass",
    )(x, cot, blocks, blocks, blocks, blocks)


def down_kernel(hidden_ref, down_a_ref, down_b_ref, near_ref, far_ref, sum_ref):
    hidden = hidden_ref[...]
    n = down_a_ref.shape[2]
    first = pl.program_id(0) == 0
    for k, ref in enumerate((down_a_ref, down_b_ref)):
        at = slice(k * n, (k + 1) * n)
        part = matmul(hidden, joined(ref))

        @pl.when(first)
        def _(part=part, at=at):
            sum_ref[:, at] = part

        @pl.when(jnp.logical_not(first))
        def _(part=part, at=at):
            sum_ref[:, at] += part

    @pl.when(pl.program_id(0) == pl.num_programs(0) - 1)
    def _():
        half = near_ref.shape[0]
        near_ref[...] = sum_ref[:half, :]
        far_ref[...] = sum_ref[half:, :].astype(BF16)


def down_pass(hidden, blocks, depth, rows, tiles, piece):
    tokens, n = hidden.shape
    shards, _, tile = blocks.shape
    at = 2 * tiles * rows // piece
    half = pl.BlockSpec((tokens // 2, depth), lambda j: (0, 0))
    return pl.pallas_call(
        down_kernel,
        grid=(2,),
        in_specs=[
            pl.BlockSpec((tokens, n // 2), lambda j: (0, j)),
            *[pl.BlockSpec((shards // 2, piece, tile), lambda j, k=k: (j, at + k, 0)) for k in range(2)],
        ],
        out_specs=[half, half],
        out_shape=[jax.ShapeDtypeStruct((tokens // 2, depth), F32), sent((tokens // 2, depth))],
        scratch_shapes=[pltpu.VMEM((tokens, depth), F32)],
        compiler_params=pltpu.CompilerParams(vmem_limit_bytes=VMEM),
        cost_estimate=HINT,
        name="down_pass",
    )(hidden, blocks, blocks)


def joined(ref):
    v = ref[...]
    if v.shape[1] % 16:
        return widen(v).reshape(-1, v.shape[2]).astype(BF16)
    return v.reshape(-1, v.shape[2])


def away_kernel(at_ref, left_ref, right_ref, out_ref):
    out_ref[...] = matmul(joined(left_ref), right_ref[...]).reshape(out_ref.shape).astype(out_ref.dtype)


def home_kernel(bit, at_ref, left_ref, right_ref, got_ref, keep_ref, send_ref, sum_ref):
    v = matmul(joined(left_ref), right_ref[...]).reshape(got_ref.shape) + widen(got_ref[...])
    sum_ref[...] = v.reshape(sum_ref.shape)
    keep_ref[...] = sum_ref[:, at_ref[bit]].astype(keep_ref.dtype)
    send_ref[...] = sum_ref[:, 1 - at_ref[bit]].astype(send_ref.dtype)


def column_tile(n, choices=(1024, 768, 512, 256, 128)):
    return max(t for t in choices if n % t == 0)


def tiling(right, columns, skip):
    parts, _, n = right.shape
    tile = column_tile(columns or n)
    each = n // tile

    def index(j, at):
        at_tile = j + (at[0] if skip < 0 else skip)
        return at_tile // each, 0, at_tile % each

    return tile, columns or parts * n, index


def grad_away(left, right, at, columns=0, skip=0):
    owners, _, rows, tokens = left.shape
    tile, n, index = tiling(right, columns, skip)
    return pl.pallas_call(
        away_kernel,
        grid_spec=pltpu.PrefetchScalarGridSpec(
            num_scalar_prefetch=1,
            grid=(n // tile,),
            in_specs=[
                pl.BlockSpec((owners, None, rows, tokens), lambda j, at: (0, 1 - at[1], 0, 0)),
                pl.BlockSpec((None, tokens, tile), index),
            ],
            out_specs=pl.BlockSpec((owners, rows, tile), lambda j, at: (0, 0, j)),
        ),
        out_shape=sent((owners, rows, n)),
        compiler_params=pltpu.CompilerParams(vmem_limit_bytes=LESS),
        cost_estimate=HINT,
        name="grad_away",
    )(at, left, right)


def grad_home(left, right, got, at, bit, low, columns=0, skip=0):
    owners, _, rows, tokens = left.shape
    tile, n, index = tiling(right, columns, skip)
    high = owners // (2 * low)
    half = pl.BlockSpec((high, low, rows, tile), lambda j, at: (0, 0, 0, j))
    return pl.pallas_call(
        functools.partial(home_kernel, bit),
        grid_spec=pltpu.PrefetchScalarGridSpec(
            num_scalar_prefetch=1,
            grid=(n // tile,),
            in_specs=[
                pl.BlockSpec((owners, None, rows, tokens), lambda j, at: (0, at[1], 0, 0)),
                pl.BlockSpec((None, tokens, tile), index),
                pl.BlockSpec((owners, rows, tile), lambda j, at: (0, 0, j)),
            ],
            out_specs=[half, half],
            scratch_shapes=[pltpu.VMEM((high, 2, low, rows, tile), F32)],
        ),
        out_shape=[
            jax.ShapeDtypeStruct((high, low, rows, n), KEEP), sent((high, low, rows, n)),
        ],
        compiler_params=pltpu.CompilerParams(vmem_limit_bytes=LESS),
        cost_estimate=HINT,
        name="grad_home",
    )(at, left, right, got)


def fold_kernel(bit, at_ref, own_ref, got_ref, keep_ref, send_ref):
    mine, other = at_ref[bit], 1 - at_ref[bit]
    keep_ref[...] = (widen(own_ref[:, mine]) + widen(got_ref[:, mine])).astype(keep_ref.dtype)
    send_ref[...] = (widen(own_ref[:, other]) + widen(got_ref[:, other])).astype(BF16)


def fold(own, got, at, bit, low):
    rows, n = own.shape[2:]
    high = own.shape[0] * own.shape[1] // (2 * low)
    tile = column_tile(n, (2304, 2048, 1536, 1024, 768, 512, 256, 128))
    both = pl.BlockSpec((high, 2, low, rows, tile), lambda j, at: (0, 0, 0, 0, j))
    half = pl.BlockSpec((high, low, rows, tile), lambda j, at: (0, 0, 0, j))
    shape = (high, 2, low, rows, n)
    return pl.pallas_call(
        functools.partial(fold_kernel, bit),
        grid_spec=pltpu.PrefetchScalarGridSpec(
            num_scalar_prefetch=1, grid=(n // tile,), in_specs=[both, both], out_specs=[half, half]
        ),
        out_shape=[
            jax.ShapeDtypeStruct((high, low, rows, n), KEEP), sent((high, low, rows, n)),
        ],
        compiler_params=pltpu.CompilerParams(vmem_limit_bytes=LESS),
        cost_estimate=HINT,
        name="fold",
    )(at, own.reshape(shape), got.reshape(shape))


def settle_kernel(own_ref, got_ref, out_ref, low_ref):
    v = widen(own_ref[...]) + widen(got_ref[...])
    out_ref[...] = v
    low_ref[...] = v.astype(BF16)


def settle(own, got):
    rows, n = own.shape
    tile = column_tile(n, (2304, 2048, 1536, 1024, 768, 512, 256, 128))
    one = pl.BlockSpec((rows, tile), lambda j: (0, j))
    return pl.pallas_call(
        settle_kernel,
        grid=(n // tile,),
        in_specs=[one, one],
        out_specs=[one, one],
        out_shape=[jax.ShapeDtypeStruct((rows, n), F32), sent((rows, n))],
        compiler_params=pltpu.CompilerParams(vmem_limit_bytes=LESS),
        cost_estimate=HINT,
        name="settle",
    )(own, got)


def shifted(values, offset):
    if offset == 0:
        return values
    if offset > 0:
        return jnp.pad(values, ((0, 0), (offset, 0), (0, 0)))[:, : values.shape[1]]
    return jnp.pad(values, ((0, 0), (0, -offset), (0, 0)))[:, -offset:]


def body(
    groups, shards,
    tokens, cotangent, mix_gain, branch_proj, lruin_proj, conv_kernel, conv_bias, recur_proj, recur_bias,
    admit_proj, admit_bias, decay_param, out_proj, ffn_gain, ffn_gate, ffn_up, ffn_down,
):
    cores, bits = 2, shards.bit_length() - 1
    side = lax.axis_index("rep") % 2
    here = lax.axis_index("shard")
    taps = conv_kernel.shape[0]
    length, width = tokens.shape
    low_r = branch_proj.shape[1]
    half_r = low_r // 2
    half_f = ffn_gate.shape[1] // 2
    piece_f = half_f // shards

    def swap(v):
        return lax.ppermute(v, "rep", [(i, i ^ 1) for i in range(groups)])

    def swap_rows(v):
        v = swap(v)
        return jnp.concatenate([v[length:], v[:length]], axis=0)

    def mine(v, size, axis):
        return lax.dynamic_slice_in_dim(v, side * size, size, axis)

    def theirs(v, size, axis):
        return lax.dynamic_slice_in_dim(v, (1 - side) * size, size, axis)

    def natural(own, other):
        first = jnp.where(side == 0, own, other)
        second = jnp.where(side == 0, other, own)
        return jnp.concatenate([first, second], axis=-1)

    def with_pair(own):
        return jnp.concatenate([own, swap(own)], axis=0)

    clock = []

    def tick(*xs):
        return lax.optimization_barrier(tuple(xs) + tuple(clock))[: len(xs)]

    def tock(*ys):
        clock[:] = ys

    place = jnp.stack([side] + [(here >> i) & 1 for i in range(bits)]).astype(jnp.int32)
    here_side = place[:1]

    def cross(v, bit):
        return lax.ppermute(v, "shard", [(i, i ^ (1 << bit)) for i in range(shards)])

    class Scatter:
        def __init__(self, left, right, order=None, columns=0, skip=0):
            self.right, = tick(right if right.ndim == 3 else right[None])
            self.left = left.reshape(shards // cores, cores, left.shape[0] // shards, left.shape[1])
            self.order = list(order or range(1, bits))
            self.span = dict(columns=columns, skip=skip)
            send = grad_away(self.left, self.right, place, **self.span)
            tock(send)
            self.got = cross(send, 0)

        def next(self):
            bit, rest = self.order[0], self.order[1:]
            self.order = rest
            return bit, 2 ** sum(other < bit for other in rest)

        def home(self):
            right, got = tick(self.right, self.got)
            bit, low = self.next()
            self.v, send = grad_home(self.left, right, got, place, bit + 1, low, **self.span)
            tock(self.v, send)
            self.got = cross(send, bit)

        def fold(self):
            v, got = tick(self.v, self.got)
            bit, low = self.next()
            self.v, send = fold(v, got, place, bit + 1, low)
            tock(self.v, send)
            self.got = cross(send, bit)

        def two(self):
            while len(self.order) > 1:
                self.fold()

        def settle(self):
            v, got = tick(self.v, self.got)
            v, send = settle(v.reshape(v.shape[2:]), got.reshape(got.shape[2:]))
            tock(v, send)
            if groups > 2:
                total = v
                for k in range(1, groups // 2):
                    total = total + lax.ppermute(v, "rep", [(i, (i + 2 * k) % groups) for i in range(groups)])
                v, send = total, total.astype(BF16)
            self.v, self.got = v, swap(send)

        def both(self):
            return tick(self.v, self.got)

    per_d, per_r = mix_gain.shape[0], conv_bias.shape[0]
    vectors = jnp.concatenate(
        [mix_gain, ffn_gain, conv_kernel.reshape(-1), conv_bias, recur_bias, admit_bias, decay_param]
    )
    count = vectors.shape[0]
    vectors = jnp.pad(vectors, (0, -count % 128)).reshape(-1, 128)
    vectors = lax.all_gather(vectors, "shard", axis=0).reshape(shards, -1)[:, :count]
    gain_one = widen(vectors[:, :per_d].reshape(width))
    gain_two = widen(vectors[:, per_d : 2 * per_d].reshape(width))
    channel = vectors[:, 2 * per_d :].reshape(shards, taps + 4, per_r).transpose(1, 0, 2).reshape(taps + 4, low_r)
    channel = widen(mine(channel, half_r, 1))
    taps_half, cbias = channel[:taps], channel[taps]
    rbias, abias, lam = channel[taps + 1], channel[taps + 2], channel[taps + 3]
    rate = DECAY_SCALE * jax.nn.softplus(-lam)
    params = jnp.concatenate([jnp.stack([rbias, abias, rate]), jnp.zeros((5, half_r), F32)])

    def ffn_half(v):
        return lax.dynamic_index_in_dim(v.reshape(v.shape[0], shards, 2, piece_f), side, 2, False).reshape(v.shape[0], half_f)

    def gather_blocks(parts, block):
        rows = [p[:, at : at + block] for p in parts for at in range(0, p.shape[1], block)]
        return lax.all_gather(jnp.concatenate(rows, axis=0), "shard", axis=0)

    def unpack(whole, at, rows, columns):
        block = whole.shape[2]
        cols = [whole[:, at + i * rows : at + (i + 1) * rows].reshape(shards * rows, block) for i in range(columns // block)]
        return jnp.concatenate(cols, axis=1)

    per_f, tiles = 2 * piece_f, 3
    whole = lax.all_gather(
        pack(here_side, [branch_proj, lruin_proj, recur_proj, admit_proj], out_proj, 512), "shard", axis=0
    )
    ffn_blocks = gather_blocks(
        [ffn_half(ffn_gate), ffn_half(ffn_up), mine(ffn_down, piece_f, 0)], half_f // tiles
    )
    cot_pair = with_pair(cotangent)
    values = widen(with_pair(tokens))
    scale_one = lax.rsqrt(jnp.mean(values * values, axis=-1, keepdims=True) + EPS)
    normed = (values * scale_one * gain_one).astype(BF16)
    normed_t = flip(normed)
    tock(normed_t, cot_pair)
    whole, = tick(whole)
    at = low_r // 512 * per_d
    w1 = unpack(whole, 0, per_d, low_r)
    w2 = unpack(whole, at, per_r, low_r)
    w3 = unpack(whole, at + low_r // 512 * per_r, per_r, width)
    pre = matmul(normed, w1)
    lru_pre = pre[:, half_r:].reshape(2, length, half_r)
    conv = cbias
    for k in range(taps):
        conv = conv + taps_half[k] * shifted(lru_pre, k)
    admitted = conv.reshape(2 * length, half_r).astype(BF16)
    admitted_all = natural(admitted, swap_rows(admitted))
    gates = matmul(admitted_all, w2)
    mixed, *factors = recurrence_forward(pre, gates, admitted, params, length)
    tock(mixed)
    admitted_all, = tick(admitted_all)
    admitted_t = flip(admitted_all)
    tock(admitted_t)
    mixed_other, = tick(swap(mixed[length:]))
    mixed_own = natural(mixed[:length], mixed_other)
    middle = widen(tokens) + matmul(mixed_own, w3)
    scale_two = lax.rsqrt(jnp.mean(middle * middle, axis=-1, keepdims=True) + EPS)
    normed_two = (middle * scale_two * gain_two).astype(BF16)
    tock(normed_two)
    mixed_late, mixed_far = tick(mixed[length:], swap(mixed[:length]))
    mixed_t = flip(jnp.concatenate([mixed_own, natural(mixed_late, mixed_far)], axis=0))
    tock(mixed_t)
    normed_two = jnp.concatenate([normed_two, *tick(swap(normed_two))], axis=0)
    tock(normed_two)
    ffn_blocks, = tick(ffn_blocks)

    ffn = dict(rows=per_d, tiles=tiles)
    have, grads, steps = {}, {}, {}

    def step(run):
        steps[run.__name__] = run
        return run

    @step
    def ffn_in():
        x, = tick(normed_two)
        have["hidden"], have["hidden_t"], have["gate_cot"], have["up_cot"], near, far = ffn_pass(
            x, cot_pair, ffn_blocks, piece=piece_f, **ffn
        )
        tock(near, far)
        have["ffn"] = near, swap(far)

    @step
    def turn():
        x, = tick(normed_two)
        have["normed_two_t"] = flip(x)
        tock(have["normed_two_t"])

    @step
    def norm_two():
        near, far = tick(*have["ffn"])
        have["middle_cot"], low = norm_back(near, far, cotangent, middle, gain_two)
        tock(have["middle_cot"], low)
        have["middle_low"] = low, swap(low)

    @step
    def mixer():
        low, other = tick(*have["middle_low"])
        have["branch_low"], have["gates_cot"], have["direct"], have["sums"], near, far = chain_back(
            here_side, low, other, whole, at, per_r, factors
        )
        have["out_cot"] = jnp.concatenate([low, other], axis=0)
        tock(near, far)
        have["admitted"] = near, swap(far)

    @step
    def conv_in():
        direct, near, far = tick(have["direct"], *have["admitted"])
        have["pre_cot"], have["conv_sums"], near, far = conv_back(
            direct, near, far, pre, have["branch_low"], channel, whole, per_d, width
        )
        tock(near, far, have["pre_cot"])
        have["normed"] = near, swap(far)

    @step
    def norm_one():
        near, far = tick(*have["normed"])
        have["tokens_grad"], _ = norm_back(near, far, have["middle_cot"], tokens, gain_one)
        tock(have["tokens_grad"])

    @step
    def down():
        x, = tick(have["hidden"])
        near, far = down_pass(x, ffn_blocks, width, piece=piece_f, **ffn)
        tock(near, far)
        have["down"] = near, swap(far)

    @step
    def result():
        near, far = tick(*have["down"])
        have["block_out"] = (middle + near + widen(far)).astype(BF16)
        tock(have["block_out"])

    @step
    def small():
        conv_sums, sums = tick(have["conv_sums"], have["sums"])
        sums = jnp.sum(sums.reshape(3, ROWS, half_r), axis=1)
        v = jnp.concatenate([conv_sums[: taps + 1], sums[:2], sums[2:] * (DECAY_SCALE * jax.nn.sigmoid(-lam))])
        v = natural(v, jnp.zeros_like(v))
        tock(v)
        have["small"] = lax.psum(v, ("rep", "shard"))

    @step
    def small_end():
        v, = tick(have["small"])
        have["small"] = lax.dynamic_slice_in_dim(v, here * per_r, per_r, 1)
        tock(have["small"])

    def late(name, left, right, order=None, **span):
        def away():
            grads[name] = Scatter(left(), right(), order, **span)

        steps["away_" + name] = away
        for stage in ("home", "two", "fold", "settle"):
            steps[stage + "_" + name] = lambda stage=stage: getattr(grads[name], stage)()

    z_first = [2, 1] + list(range(3, bits))
    late("d", lambda: have["hidden_t"], lambda: cot_pair)
    late("g", lambda: have["normed_two_t"], lambda: have["gate_cot"])
    late("u", lambda: have["normed_two_t"], lambda: have["up_cot"], z_first)
    late("r", lambda: admitted_t, lambda: have["gates_cot"], z_first)
    late("b", lambda: normed_t, lambda: have["pre_cot"])
    late("o", lambda: mixed_t, lambda: have["out_cot"], columns=width // 2, skip=-1)

    @step
    def join_d():
        v, got = grads["d"].both()
        have["d"] = join_rows(here_side, v, got)
        tock(have["d"])

    @step
    def join_g():
        have["g"] = weave(here_side, *grads["g"].both(), piece_f)
        tock(have["g"])

    @step
    def join_u():
        have["u"] = weave(here_side, *grads["u"].both(), piece_f)
        tock(have["u"])

    @step
    def join_r():
        have["r"] = join_columns(here_side, *grads["r"].both(), 2)
        tock(*have["r"])

    @step
    def join_b():
        have["b"] = join_columns(here_side, *grads["b"].both(), 2)
        tock(*have["b"])

    @step
    def join_o():
        have["o"], = join_columns(here_side, *grads["o"].both(), 1)
        tock(have["o"])

    for name in STEPS:
        steps[name]()
    small_grad, (branch_grad, lruin_grad) = have["small"], have["b"]
    ffngain_grad = jnp.sum(have["g"] * widen(ffn_gate) + have["u"] * widen(ffn_up), axis=1) / widen(ffn_gain)
    mixgain_grad = jnp.sum(branch_grad * widen(branch_proj) + lruin_grad * widen(lruin_proj), axis=1) / widen(mix_gain)
    return (
        have["block_out"], have["tokens_grad"], mixgain_grad, branch_grad, lruin_grad, small_grad[:taps],
        small_grad[taps], have["r"][0], small_grad[taps + 1], have["r"][1], small_grad[taps + 2],
        small_grad[taps + 3], have["o"], ffngain_grad, have["g"], have["u"], have["d"],
    )


def solution(mesh):
    groups, shards = mesh.shape["rep"], mesh.shape["shard"]
    whole = P(("rep", "shard"), None)
    row, vec, col = P("shard", None), P("shard"), P(None, "shard")
    in_specs = (whole, whole, vec, row, row, col, vec, row, vec, row, vec, vec, row, vec, row, row, row)
    out_specs = (whole, whole, vec, row, row, col, vec, row, vec, row, vec, vec, row, vec, row, row, row)
    return jax.shard_map(
        functools.partial(body, groups, shards), mesh=mesh, in_specs=in_specs, out_specs=out_specs, check_vma=False
    )
```

```python
import functools
import math

import jax
import jax.numpy as jnp
from jax import lax
from jax.experimental import pallas as pl
from jax.experimental.pallas import tpu as pltpu
from jax.sharding import PartitionSpec as P

EPS = 1e-06
DECAY_SCALE = 8.0
ROOT_FLOOR = 0.001
GELU_K = math.sqrt(2.0 / math.pi)
GELU_C = 0.044715
ROWS = 16
FACTORS = 7
VMEM = 44 << 20
LESS = 24 << 20
MORE = 50 << 20
PARTS = 2
STEPS = (
    "turn", "ffn_in", "away_d", "away_u", "norm_two", "home_u", "home_d", "away_g", "mixer", "away_r", "two_u",
    "two_d", "home_g", "home_r", "fold_u", "conv_in", "fold_d", "away_b", "small", "settle_u", "down", "home_b",
    "norm_one", "two_g", "two_r", "join_u", "two_b", "away_o", "fold_g", "settle_d", "home_o", "fold_r", "settle_g",
    "join_d", "two_o", "fold_b", "join_g", "settle_r", "fold_o", "result", "settle_b", "small_end", "join_r",
    "settle_o", "join_b", "join_o",
)
HINT = pl.CostEstimate(flops=100000000000, bytes_accessed=1024, transcendentals=0)
BF16 = jnp.bfloat16
F32 = jnp.float32
KEEP = BF16


def sent(shape):
    return pltpu.HBM(shape, BF16)


def matmul(left, right):
    return jnp.dot(left, right, preferred_element_type=F32)


def rows_product(left, right):
    return lax.dot_general(left, right, (((0,), (0,)), ((), ())), preferred_element_type=F32)


def cols_product(left, right):
    return lax.dot_general(left, right, (((1,), (1,)), ((), ())), preferred_element_type=F32)


def widen(value):
    return value.astype(F32)


def gelu(v):
    return 0.5 * v * (1.0 + jnp.tanh(GELU_K * (v + GELU_C * v * v * v)))


def gelu_slope(v):
    t = jnp.tanh(GELU_K * (v + GELU_C * v * v * v))
    return 0.5 * (1.0 + t) + 0.5 * v * (1.0 - t * t) * GELU_K * (1.0 + 3.0 * GELU_C * v * v)


def forward_kernel(pre_ref, gates_r_ref, gates_i_ref, admitted_ref, params_ref, mixed_ref, *factor_refs):
    width = pre_ref.shape[1]
    rbias, abias, rate = params_ref[0:1, :], params_ref[1:2, :], params_ref[2:3, :]
    row = lax.broadcasted_iota(jnp.int32, (ROWS, width), 0)

    def step(i, carry):
        at = pl.ds(pl.multiple_of(i * ROWS, ROWS), ROWS)
        gate_r = jax.nn.sigmoid(gates_r_ref[at, :] + rbias)
        gate_i = jax.nn.sigmoid(gates_i_ref[at, :] + abias)
        admitted = widen(admitted_ref[at, :])
        decay = jnp.exp(-(gate_r * rate))
        rest = 1.0 - decay * decay
        root = jnp.sqrt(jnp.maximum(rest, ROOT_FLOOR))
        through = root * gate_i
        a, b = decay, through * admitted
        for d in (1, 2, 4, 8):
            keep = row >= d
            b = b + a * jnp.where(keep, pltpu.roll(b, d, 0), 0.0)
            a = a * jnp.where(keep, pltpu.roll(a, d, 0), 1.0)
        state = b + a * carry
        before = jnp.where(row >= 1, pltpu.roll(state, 1, 0), carry)
        pre = pre_ref[at, :]
        t = jnp.tanh(GELU_K * (pre + GELU_C * pre * pre * pre))
        act = 0.5 * pre * (1.0 + t)
        slope = 0.5 * (1.0 + t) + 0.5 * pre * (1.0 - t * t) * GELU_K * (1.0 + 3.0 * GELU_C * pre * pre)
        mixed_ref[at, :] = (state * act).astype(BF16)
        share = jnp.where(rest > ROOT_FLOOR, 1.0, jnp.where(rest == ROOT_FLOOR, 0.5, 0.0))
        log = decay * (before - gate_i * admitted * (share * decay / root))
        factors = (
            decay, act, state * slope, through, through * admitted * (1.0 - gate_i),
            -(log * rate) * gate_r * (1.0 - gate_r), log * gate_r,
        )
        for ref, factor in zip(factor_refs, factors, strict=True):
            ref[at, :] = factor
        return jnp.broadcast_to(state[ROWS - 1 : ROWS, :], (ROWS, width))

    lax.fori_loop(0, pre_ref.shape[0] // ROWS, step, jnp.zeros((ROWS, width), F32))


def chain_kernel(
    side_ref, own_ref, other_ref, out_a_ref, out_b_ref, out_c_ref, recur_w_ref, admit_w_ref, decay_ref, act_ref,
    branch_f_ref, direct_f_ref, admit_f_ref, recur_f_ref, rate_f_ref,
    branch_ref, gates_cot_ref, direct_ref, sums_ref, near_ref, far_ref, cot_ref, sum_ref,
):
    length = own_ref.shape[0]
    width = act_ref.shape[1]
    out_w = jnp.concatenate([joined(out_a_ref), joined(out_b_ref), joined(out_c_ref)], axis=1)
    cot_ref[:length, :] = cols_product(own_ref[...], out_w)
    cot_ref[length:, :] = cols_product(other_ref[...], out_w)
    row = lax.broadcasted_iota(jnp.int32, (ROWS, width), 0)
    blocks = length // ROWS
    zero = jnp.zeros((ROWS, width), F32)

    def step(first, i, state):
        carry, sum_r, sum_i, sum_d = state
        at = pl.ds(pl.multiple_of(first + (blocks - 1 - i) * ROWS, ROWS), ROWS)
        cot = cot_ref[at, :]
        branch_ref[at, :] = (cot * branch_f_ref[at, :]).astype(BF16)
        own = cot * act_ref[at, :]
        f = decay_ref[at, :]
        e = f * own
        for d in (1, 2, 4, 8):
            keep = row < ROWS - d
            e = e + f * jnp.where(keep, pltpu.roll(e, ROWS - d, 0), 0.0)
            f = f * jnp.where(keep, pltpu.roll(f, ROWS - d, 0), 1.0)
        e = e + f * carry
        g = own + jnp.where(row < ROWS - 1, pltpu.roll(e, ROWS - 1, 0), carry)
        direct_ref[at, :] = g * direct_f_ref[at, :]
        recur = g * recur_f_ref[at, :]
        admit = g * admit_f_ref[at, :]
        gates_cot_ref[0, at, :] = recur.astype(BF16)
        gates_cot_ref[1, at, :] = admit.astype(BF16)
        carry = jnp.broadcast_to(e[0:1, :], (ROWS, width))
        return carry, sum_r + recur, sum_i + admit, sum_d + g * rate_f_ref[at, :]

    sums = (zero, zero, zero)
    for first in (0, length):
        _, *sums = lax.fori_loop(0, blocks, functools.partial(step, first), (zero, *sums))
    for i in range(3):
        sums_ref[i * ROWS : (i + 1) * ROWS, :] = sums[i]
    depth = sum_ref.shape[1]
    part = cols_product(gates_cot_ref[0], joined(recur_w_ref)) + cols_product(gates_cot_ref[1], joined(admit_w_ref))

    @pl.when(pl.program_id(0) == 0)
    def _():
        sum_ref[...] = part

    @pl.when(pl.program_id(0) > 0)
    def _():
        sum_ref[...] += part

    half = depth // 2
    for side in range(2):
        @pl.when((pl.program_id(0) == pl.num_programs(0) - 1) & (side_ref[0] == side))
        def _(side=side):
            near_ref[...] = sum_ref[:, side * half : (side + 1) * half]
            away = slice((1 - side) * half, (2 - side) * half)
            far_ref[:length, :] = sum_ref[length:, away].astype(BF16)
            far_ref[length:, :] = sum_ref[:length, away].astype(BF16)


def chain_back(side, own, other, whole, at, rows, factors):
    length, depth = own.shape
    tokens, width = factors[0].shape
    shards, _, tile = whole.shape
    n = width // tile
    at = at // rows
    low = jax.ShapeDtypeStruct((tokens, width), BF16)
    full = pl.BlockSpec((length, depth), lambda j, s: (0, 0))
    near = pl.BlockSpec((tokens, tile), lambda j, s: (0, j))
    fixed = pl.BlockSpec((tokens, width), lambda j, s: (0, 0))
    return pl.pallas_call(
        chain_kernel,
        grid_spec=pltpu.PrefetchScalarGridSpec(
            num_scalar_prefetch=1,
            grid=(n,),
            in_specs=[
                full, full,
                *[
                    pl.BlockSpec((tile // rows, rows, tile), lambda j, s, k=k: (s[0] * n + j, at + 2 * n + k, 0))
                    for k in range(3)
                ],
                pl.BlockSpec((shards, rows, tile), lambda j, s: (0, at + j, 0)),
                pl.BlockSpec((shards, rows, tile), lambda j, s: (0, at + n + j, 0)),
                *[near] * FACTORS,
            ],
            out_specs=[
                near, pl.BlockSpec((2, tokens, tile), lambda j, s: (0, 0, j)), near,
                pl.BlockSpec((3 * ROWS, tile), lambda j, s: (0, j)), fixed, fixed,
            ],
            scratch_shapes=[pltpu.VMEM((tokens, tile), F32), pltpu.VMEM((tokens, 2 * width), F32)],
        ),
        out_shape=[
            low, jax.ShapeDtypeStruct((2, tokens, width), BF16), jax.ShapeDtypeStruct((tokens, width), F32),
            jax.ShapeDtypeStruct((3 * ROWS, width), F32), jax.ShapeDtypeStruct((tokens, width), F32), sent((tokens, width)),
        ],
        compiler_params=pltpu.CompilerParams(vmem_limit_bytes=VMEM),
        cost_estimate=HINT,
        name="chain_back",
    )(side, own, other, *[whole] * 5, *factors)


def conv_kernel(
    direct_ref, near_in_ref, far_in_ref, lru_ref, branch_ref, taps_ref, branch_w_ref, lruin_w_ref,
    pre_cot_ref, sums_ref, near_ref, far_ref, sum_ref,
):
    tokens, width = direct_ref.shape
    length = tokens // 2
    cot = direct_ref[...] + near_in_ref[...] + widen(far_in_ref[...])
    lru = lru_ref[...]
    token = lax.broadcasted_iota(jnp.int32, (tokens, width), 0)
    token = jnp.where(token >= length, token - length, token)
    total = jnp.zeros_like(cot)
    count = 4
    for k in range(count):
        later = cot if k == 0 else jnp.where(token < length - k, pltpu.roll(cot, tokens - k, 0), 0.0)
        total = total + taps_ref[k : k + 1, :] * later
        sums_ref[k : k + 1, :] = jnp.sum(later * lru, axis=0, keepdims=True)
    sums_ref[count : count + 1, :] = jnp.sum(cot, axis=0, keepdims=True)
    low = total.astype(BF16)
    pre_cot_ref[0] = branch_ref[...]
    pre_cot_ref[1] = low
    part = cols_product(branch_ref[...], joined(branch_w_ref)) + cols_product(low, joined(lruin_w_ref))

    @pl.when(pl.program_id(0) == 0)
    def _():
        sum_ref[...] = part

    @pl.when(pl.program_id(0) > 0)
    def _():
        sum_ref[...] += part

    @pl.when(pl.program_id(0) == pl.num_programs(0) - 1)
    def _():
        near_ref[...] = sum_ref[:length, :]
        far_ref[...] = sum_ref[length:, :].astype(BF16)


def conv_back(direct, near, far, pre, branch, taps, whole, rows, depth):
    tokens, width = direct.shape
    shards, _, tile = whole.shape
    n = width // tile
    one = pl.BlockSpec((tokens, tile), lambda j: (0, j))
    half = pl.BlockSpec((tokens // 2, depth), lambda j: (0, 0))
    return pl.pallas_call(
        conv_kernel,
        grid=(n,),
        in_specs=[
            one, one, one, pl.BlockSpec((tokens, tile), lambda j: (0, j + n)), one,
            pl.BlockSpec((8, tile), lambda j: (0, j)),
            pl.BlockSpec((shards, rows, tile), lambda j: (0, j, 0)),
            pl.BlockSpec((shards, rows, tile), lambda j: (0, n + j, 0)),
        ],
        out_specs=[
            pl.BlockSpec((2, tokens, tile), lambda j: (0, 0, j)), pl.BlockSpec((8, tile), lambda j: (0, j)), half, half,
        ],
        out_shape=[
            jax.ShapeDtypeStruct((2, tokens, width), BF16), jax.ShapeDtypeStruct((8, width), F32),
            jax.ShapeDtypeStruct((tokens // 2, depth), F32), sent((tokens // 2, depth)),
        ],
        scratch_shapes=[pltpu.VMEM((tokens, depth), F32)],
        compiler_params=pltpu.CompilerParams(vmem_limit_bytes=VMEM),
        cost_estimate=HINT,
        name="conv_back",
    )(direct, near, far, pre, branch, taps, whole, whole)


def norm_kernel(near_ref, far_ref, base_ref, v_ref, gain_ref, out_ref, low_ref):
    v = widen(v_ref[...])
    scale = lax.rsqrt(jnp.mean(v * v, axis=-1, keepdims=True) + EPS)
    g = (near_ref[...] + widen(far_ref[...])) * gain_ref[0:1, :]
    out = widen(base_ref[...]) + scale * (g - v * (scale * scale * jnp.mean(g * v, axis=-1, keepdims=True)))
    out_ref[...] = out
    low_ref[...] = out.astype(BF16)


def norm_back(near, far, base, v, gain):
    rows, width = near.shape
    tile = rows // 4
    one = pl.BlockSpec((tile, width), lambda j: (j, 0))
    return pl.pallas_call(
        norm_kernel,
        grid=(rows // tile,),
        in_specs=[one, one, one, one, pl.BlockSpec((8, width), lambda j: (0, 0))],
        out_specs=[one, one],
        out_shape=[jax.ShapeDtypeStruct((rows, width), F32), sent((rows, width))],
        compiler_params=pltpu.CompilerParams(vmem_limit_bytes=LESS),
        cost_estimate=HINT,
        name="norm_back",
    )(near, far, base, v, jnp.broadcast_to(gain, (8, width)))


def flip_kernel(x_ref, out_ref):
    out_ref[...] = widen(x_ref[...]).T.astype(BF16)


def flip(x):
    tokens, n = x.shape
    tile = 256
    return pl.pallas_call(
        flip_kernel,
        grid=(n // tile,),
        in_specs=[pl.BlockSpec((tokens, tile), lambda j: (0, j))],
        out_specs=pl.BlockSpec((tile, tokens), lambda j: (j, 0)),
        out_shape=jax.ShapeDtypeStruct((n, tokens), BF16),
        compiler_params=pltpu.CompilerParams(vmem_limit_bytes=LESS),
        cost_estimate=HINT,
        name="flip",
    )(x)


def pack_kernel(block, side_ref, *refs):
    out_ref, at = refs[-1], 0
    for ref in refs[:-1]:
        rows, n = ref.shape
        for first in range(0, n, block):
            out_ref[at : at + rows, :] = ref[:, first : first + block]
            at += rows


def pack(side, halves, full, block):
    specs = [pl.BlockSpec((p.shape[0], p.shape[1] // 2), lambda j, s: (0, s[0])) for p in halves]
    specs.append(pl.BlockSpec(full.shape, lambda j, s: (0, 0)))
    size = sum(p.shape[0] * p.shape[1] // 2 for p in halves) + full.size
    return pl.pallas_call(
        functools.partial(pack_kernel, block),
        grid_spec=pltpu.PrefetchScalarGridSpec(
            num_scalar_prefetch=1, grid=(1,), in_specs=specs,
            out_specs=pl.BlockSpec((size // block, block), lambda j, s: (0, 0)),
        ),
        out_shape=jax.ShapeDtypeStruct((size // block, block), BF16),
        compiler_params=pltpu.CompilerParams(vmem_limit_bytes=LESS),
        cost_estimate=HINT,
        name="pack",
    )(side, *[pltpu.with_memory_space_constraint(p, pltpu.HBM) for p in (*halves, full)])


def columns_kernel(parts, side_ref, own_ref, got_ref, *out_refs):
    n = out_refs[0].shape[1]
    mine = pl.program_id(0) == side_ref[0]

    @pl.when(mine)
    def _():
        for i in range(parts):
            out_refs[i][...] = own_ref[:, i * n : (i + 1) * n]

    @pl.when(jnp.logical_not(mine))
    def _():
        for i in range(parts):
            out_refs[i][...] = widen(got_ref[:, i * n : (i + 1) * n])


def join_columns(side, own, got, parts):
    rows, n = own.shape[0], own.shape[1] // parts
    full = pl.BlockSpec(own.shape, lambda h, s: (0, 0))
    return pl.pallas_call(
        functools.partial(columns_kernel, parts),
        grid_spec=pltpu.PrefetchScalarGridSpec(
            num_scalar_prefetch=1, grid=(2,), in_specs=[full, full],
            out_specs=[pl.BlockSpec((rows, n), lambda h, s: (0, h))] * parts,
        ),
        out_shape=[jax.ShapeDtypeStruct((rows, 2 * n), F32)] * parts,
        compiler_params=pltpu.CompilerParams(vmem_limit_bytes=LESS),
        cost_estimate=HINT,
        name="join_columns",
    )(side, own, got)


def rows_kernel(side_ref, own_ref, got_ref, out_ref):
    mine = pl.program_id(0) == side_ref[0]

    @pl.when(mine)
    def _():
        out_ref[...] = own_ref[...]

    @pl.when(jnp.logical_not(mine))
    def _():
        out_ref[...] = widen(got_ref[...])


def join_rows(side, own, got):
    rows, n = own.shape
    full = pl.BlockSpec((rows, n), lambda h, s: (0, 0))
    return pl.pallas_call(
        rows_kernel,
        grid_spec=pltpu.PrefetchScalarGridSpec(
            num_scalar_prefetch=1, grid=(2,), in_specs=[full] * 2,
            out_specs=pl.BlockSpec((rows, n), lambda h, s: (h, 0)),
        ),
        out_shape=jax.ShapeDtypeStruct((2 * rows, n), F32),
        compiler_params=pltpu.CompilerParams(vmem_limit_bytes=LESS),
        cost_estimate=HINT,
        name="join_rows",
    )(side, own, got)


def weave_kernel(piece, side_ref, own_ref, got_ref, out_ref):
    for side in range(2):
        @pl.when(side_ref[0] == side)
        def _(side=side):
            parts = []
            for at in range(0, own_ref.shape[1], piece):
                own = own_ref[:, at : at + piece]
                got = widen(got_ref[:, at : at + piece])
                parts += [got, own] if side else [own, got]
            out_ref[...] = jnp.concatenate(parts, axis=1)


def weave(side, own, got, piece):
    rows, n = own.shape
    return pl.pallas_call(
        functools.partial(weave_kernel, piece),
        grid_spec=pltpu.PrefetchScalarGridSpec(
            num_scalar_prefetch=1, grid=(1,),
            in_specs=[pl.BlockSpec((rows, n), lambda h, s: (0, 0))] * 2,
            out_specs=pl.BlockSpec((rows, 2 * n), lambda h, s: (0, 0)),
        ),
        out_shape=jax.ShapeDtypeStruct((rows, 2 * n), F32),
        compiler_params=pltpu.CompilerParams(vmem_limit_bytes=LESS),
        cost_estimate=HINT,
        name="weave",
    )(side, own, got)


def recurrence_forward(pre, gates, admitted, params, length):
    tokens, width = admitted.shape
    tile = math.gcd(width, 512)
    n = width // tile
    near = pl.BlockSpec((length, tile), lambda s, j: (s, j))
    far = pl.BlockSpec((length, tile), lambda s, j: (s, j + n))
    vector = pl.BlockSpec((8, tile), lambda s, j: (0, j))
    return pl.pallas_call(
        forward_kernel,
        grid=(tokens // length, n),
        in_specs=[near, near, far, near, vector],
        out_specs=[near] * (1 + FACTORS),
        out_shape=[jax.ShapeDtypeStruct((tokens, width), BF16)] + [jax.ShapeDtypeStruct((tokens, width), F32)] * FACTORS,
        cost_estimate=pl.CostEstimate(flops=60 * tokens * width, bytes_accessed=20 * tokens * width, transcendentals=6 * tokens * width),
        name="recurrence_forward",
    )(pre, gates, gates, admitted, params)


def take_tile(down_a_ref, down_b_ref, down_ref):
    rows, n = down_ref.shape[0], down_a_ref.shape[2]
    for j in range(shape_rows(down_a_ref) // rows):
        @pl.when(pl.program_id(0) == j)
        def _(j=j):
            down_ref[:, :n] = joined(down_a_ref)[j * rows : (j + 1) * rows]
            down_ref[:, n:] = joined(down_b_ref)[j * rows : (j + 1) * rows]


def shape_rows(ref):
    return ref.shape[0] * ref.shape[1]


def ffn_kernel(
    x_ref, cot_ref, gate_ref, up_ref, down_a_ref, down_b_ref,
    hidden_ref, flipped_ref, gate_cot_ref, up_cot_ref, near_ref, far_ref, sum_ref, down_ref,
):
    take_tile(down_a_ref, down_b_ref, down_ref)
    gate_w, up_w, down_w = joined(gate_ref), joined(up_ref), down_ref[...]
    tokens = x_ref.shape[0]
    for first in range(0, tokens, tokens // PARTS):
        rows = slice(first, first + tokens // PARTS)
        x = x_ref[rows, :]
        gate = matmul(x, gate_w)
        up = matmul(x, up_w)
        cot = cols_product(cot_ref[rows, :], down_w)
        t = jnp.tanh(GELU_K * (gate + GELU_C * gate * gate * gate))
        act = 0.5 * gate * (1.0 + t)
        slope = 0.5 * (1.0 + t) + 0.5 * gate * (1.0 - t * t) * GELU_K * (1.0 + 3.0 * GELU_C * gate * gate)
        hidden = act * up
        hidden_ref[rows, :] = hidden.astype(BF16)
        flipped_ref[:, rows] = hidden.T.astype(BF16)
        gate_cot = (cot * up * slope).astype(BF16)
        up_cot = (cot * act).astype(BF16)
        gate_cot_ref[rows, :] = gate_cot
        up_cot_ref[rows, :] = up_cot
        part = cols_product(gate_cot, gate_w) + cols_product(up_cot, up_w)

        @pl.when(pl.program_id(0) == 0)
        def _(part=part, rows=rows):
            sum_ref[rows, :] = part

        @pl.when(pl.program_id(0) > 0)
        def _(part=part, rows=rows):
            sum_ref[rows, :] += part

    @pl.when(pl.program_id(0) == pl.num_programs(0) - 1)
    def _():
        half = near_ref.shape[0]
        near_ref[...] = sum_ref[:half, :]
        far_ref[...] = sum_ref[half:, :].astype(BF16)


def down_specs(blocks, rows, tiles, piece):
    shards, _, tile = blocks.shape
    at = 2 * tiles * rows // piece
    return [pl.BlockSpec((shards, piece, tile), lambda j, k=k: (0, at + k, 0), pipeline_mode=pl.Buffered(1)) for k in range(2)]


def ffn_pass(x, cot, blocks, rows, tiles, piece):
    tokens, depth = x.shape
    shards, _, tile = blocks.shape
    n = tiles * tile
    low = jax.ShapeDtypeStruct((tokens, n), BF16)
    fixed = pl.BlockSpec((tokens, depth), lambda j: (0, 0))
    wide = pl.BlockSpec((tokens, tile), lambda j: (0, j))
    half = pl.BlockSpec((tokens // 2, depth), lambda j: (0, 0))
    return pl.pallas_call(
        ffn_kernel,
        grid=(tiles,),
        in_specs=[
            fixed, fixed,
            pl.BlockSpec((shards, rows, tile), lambda j: (0, j, 0)),
            pl.BlockSpec((shards, rows, tile), lambda j: (0, j + tiles, 0)),
            *down_specs(blocks, rows, tiles, piece),
        ],
        out_specs=[wide, pl.BlockSpec((tile, tokens), lambda j: (j, 0)), wide, wide, half, half],
        out_shape=[
            low, sent((n, tokens)), low, low,
            jax.ShapeDtypeStruct((tokens // 2, depth), F32), sent((tokens // 2, depth)),
        ],
        scratch_shapes=[pltpu.VMEM((tokens, depth), F32), pltpu.VMEM((tile, depth), BF16)],
        compiler_params=pltpu.CompilerParams(vmem_limit_bytes=MORE),
        cost_estimate=HINT,
        name="ffn_pass",
    )(x, cot, blocks, blocks, blocks, blocks)


def down_kernel(hidden_ref, down_a_ref, down_b_ref, near_ref, far_ref, sum_ref):
    hidden = hidden_ref[...]
    n = down_a_ref.shape[2]
    first = pl.program_id(0) == 0
    for k, ref in enumerate((down_a_ref, down_b_ref)):
        at = slice(k * n, (k + 1) * n)
        part = matmul(hidden, joined(ref))

        @pl.when(first)
        def _(part=part, at=at):
            sum_ref[:, at] = part

        @pl.when(jnp.logical_not(first))
        def _(part=part, at=at):
            sum_ref[:, at] += part

    @pl.when(pl.program_id(0) == pl.num_programs(0) - 1)
    def _():
        half = near_ref.shape[0]
        near_ref[...] = sum_ref[:half, :]
        far_ref[...] = sum_ref[half:, :].astype(BF16)


def down_pass(hidden, blocks, depth, rows, tiles, piece):
    tokens, n = hidden.shape
    shards, _, tile = blocks.shape
    at = 2 * tiles * rows // piece
    half = pl.BlockSpec((tokens // 2, depth), lambda j: (0, 0))
    return pl.pallas_call(
        down_kernel,
        grid=(2,),
        in_specs=[
            pl.BlockSpec((tokens, n // 2), lambda j: (0, j)),
            *[pl.BlockSpec((shards // 2, piece, tile), lambda j, k=k: (j, at + k, 0)) for k in range(2)],
        ],
        out_specs=[half, half],
        out_shape=[jax.ShapeDtypeStruct((tokens // 2, depth), F32), sent((tokens // 2, depth))],
        scratch_shapes=[pltpu.VMEM((tokens, depth), F32)],
        compiler_params=pltpu.CompilerParams(vmem_limit_bytes=VMEM),
        cost_estimate=HINT,
        name="down_pass",
    )(hidden, blocks, blocks)


def joined(ref):
    v = ref[...]
    if v.shape[1] % 16:
        return widen(v).reshape(-1, v.shape[2]).astype(BF16)
    return v.reshape(-1, v.shape[2])


def away_kernel(at_ref, left_ref, right_ref, out_ref):
    out_ref[...] = matmul(joined(left_ref), right_ref[...]).reshape(out_ref.shape).astype(out_ref.dtype)


def home_kernel(bit, at_ref, left_ref, right_ref, got_ref, keep_ref, send_ref, sum_ref):
    v = matmul(joined(left_ref), right_ref[...]).reshape(got_ref.shape) + widen(got_ref[...])
    sum_ref[...] = v.reshape(sum_ref.shape)
    keep_ref[...] = sum_ref[:, at_ref[bit]].astype(keep_ref.dtype)
    send_ref[...] = sum_ref[:, 1 - at_ref[bit]].astype(send_ref.dtype)


def column_tile(n, choices=(1024, 768, 512, 256, 128)):
    return max(t for t in choices if n % t == 0)


def tiling(right, columns, skip):
    parts, _, n = right.shape
    tile = column_tile(columns or n)
    each = n // tile

    def index(j, at):
        at_tile = j + (at[0] if skip < 0 else skip)
        return at_tile // each, 0, at_tile % each

    return tile, columns or parts * n, index


def grad_away(left, right, at, columns=0, skip=0):
    owners, _, rows, tokens = left.shape
    tile, n, index = tiling(right, columns, skip)
    return pl.pallas_call(
        away_kernel,
        grid_spec=pltpu.PrefetchScalarGridSpec(
            num_scalar_prefetch=1,
            grid=(n // tile,),
            in_specs=[
                pl.BlockSpec((owners, None, rows, tokens), lambda j, at: (0, 1 - at[1], 0, 0)),
                pl.BlockSpec((None, tokens, tile), index),
            ],
            out_specs=pl.BlockSpec((owners, rows, tile), lambda j, at: (0, 0, j)),
        ),
        out_shape=sent((owners, rows, n)),
        compiler_params=pltpu.CompilerParams(vmem_limit_bytes=LESS),
        cost_estimate=HINT,
        name="grad_away",
    )(at, left, right)


def grad_home(left, right, got, at, bit, low, columns=0, skip=0):
    owners, _, rows, tokens = left.shape
    tile, n, index = tiling(right, columns, skip)
    high = owners // (2 * low)
    half = pl.BlockSpec((high, low, rows, tile), lambda j, at: (0, 0, 0, j))
    return pl.pallas_call(
        functools.partial(home_kernel, bit),
        grid_spec=pltpu.PrefetchScalarGridSpec(
            num_scalar_prefetch=1,
            grid=(n // tile,),
            in_specs=[
                pl.BlockSpec((owners, None, rows, tokens), lambda j, at: (0, at[1], 0, 0)),
                pl.BlockSpec((None, tokens, tile), index),
                pl.BlockSpec((owners, rows, tile), lambda j, at: (0, 0, j)),
            ],
            out_specs=[half, half],
            scratch_shapes=[pltpu.VMEM((high, 2, low, rows, tile), F32)],
        ),
        out_shape=[
            jax.ShapeDtypeStruct((high, low, rows, n), KEEP), sent((high, low, rows, n)),
        ],
        compiler_params=pltpu.CompilerParams(vmem_limit_bytes=LESS),
        cost_estimate=HINT,
        name="grad_home",
    )(at, left, right, got)


def fold_kernel(bit, at_ref, own_ref, got_ref, keep_ref, send_ref):
    mine, other = at_ref[bit], 1 - at_ref[bit]
    keep_ref[...] = (widen(own_ref[:, mine]) + widen(got_ref[:, mine])).astype(keep_ref.dtype)
    send_ref[...] = (widen(own_ref[:, other]) + widen(got_ref[:, other])).astype(BF16)


def fold(own, got, at, bit, low):
    rows, n = own.shape[2:]
    high = own.shape[0] * own.shape[1] // (2 * low)
    tile = column_tile(n, (2304, 2048, 1536, 1024, 768, 512, 256, 128))
    both = pl.BlockSpec((high, 2, low, rows, tile), lambda j, at: (0, 0, 0, 0, j))
    half = pl.BlockSpec((high, low, rows, tile), lambda j, at: (0, 0, 0, j))
    shape = (high, 2, low, rows, n)
    return pl.pallas_call(
        functools.partial(fold_kernel, bit),
        grid_spec=pltpu.PrefetchScalarGridSpec(
            num_scalar_prefetch=1, grid=(n // tile,), in_specs=[both, both], out_specs=[half, half]
        ),
        out_shape=[
            jax.ShapeDtypeStruct((high, low, rows, n), KEEP), sent((high, low, rows, n)),
        ],
        compiler_params=pltpu.CompilerParams(vmem_limit_bytes=LESS),
        cost_estimate=HINT,
        name="fold",
    )(at, own.reshape(shape), got.reshape(shape))


def settle_kernel(own_ref, got_ref, out_ref, low_ref):
    v = widen(own_ref[...]) + widen(got_ref[...])
    out_ref[...] = v
    low_ref[...] = v.astype(BF16)


def settle(own, got):
    rows, n = own.shape
    tile = column_tile(n, (2304, 2048, 1536, 1024, 768, 512, 256, 128))
    one = pl.BlockSpec((rows, tile), lambda j: (0, j))
    return pl.pallas_call(
        settle_kernel,
        grid=(n // tile,),
        in_specs=[one, one],
        out_specs=[one, one],
        out_shape=[jax.ShapeDtypeStruct((rows, n), F32), sent((rows, n))],
        compiler_params=pltpu.CompilerParams(vmem_limit_bytes=LESS),
        cost_estimate=HINT,
        name="settle",
    )(own, got)


def shifted(values, offset):
    if offset == 0:
        return values
    if offset > 0:
        return jnp.pad(values, ((0, 0), (offset, 0), (0, 0)))[:, : values.shape[1]]
    return jnp.pad(values, ((0, 0), (0, -offset), (0, 0)))[:, -offset:]


def body(
    groups, shards,
    tokens, cotangent, mix_gain, branch_proj, lruin_proj, conv_kernel, conv_bias, recur_proj, recur_bias,
    admit_proj, admit_bias, decay_param, out_proj, ffn_gain, ffn_gate, ffn_up, ffn_down,
):
    cores, bits = 2, shards.bit_length() - 1
    side = lax.axis_index("rep") % 2
    here = lax.axis_index("shard")
    taps = conv_kernel.shape[0]
    length, width = tokens.shape
    low_r = branch_proj.shape[1]
    half_r = low_r // 2
    half_f = ffn_gate.shape[1] // 2
    piece_f = half_f // shards

    def swap(v):
        return lax.ppermute(v, "rep", [(i, i ^ 1) for i in range(groups)])

    def swap_rows(v):
        v = swap(v)
        return jnp.concatenate([v[length:], v[:length]], axis=0)

    def mine(v, size, axis):
        return lax.dynamic_slice_in_dim(v, side * size, size, axis)

    def theirs(v, size, axis):
        return lax.dynamic_slice_in_dim(v, (1 - side) * size, size, axis)

    def natural(own, other):
        first = jnp.where(side == 0, own, other)
        second = jnp.where(side == 0, other, own)
        return jnp.concatenate([first, second], axis=-1)

    def with_pair(own):
        return jnp.concatenate([own, swap(own)], axis=0)

    clock = []

    def tick(*xs):
        return lax.optimization_barrier(tuple(xs) + tuple(clock))[: len(xs)]

    def tock(*ys):
        clock[:] = ys

    place = jnp.stack([side] + [(here >> i) & 1 for i in range(bits)]).astype(jnp.int32)
    here_side = place[:1]

    def cross(v, bit):
        return lax.ppermute(v, "shard", [(i, i ^ (1 << bit)) for i in range(shards)])

    class Scatter:
        def __init__(self, left, right, order=None, columns=0, skip=0):
            self.right, = tick(right if right.ndim == 3 else right[None])
            self.left = left.reshape(shards // cores, cores, left.shape[0] // shards, left.shape[1])
            self.order = list(order or range(1, bits))
            self.span = dict(columns=columns, skip=skip)
            send = grad_away(self.left, self.right, place, **self.span)
            tock(send)
            self.got = cross(send, 0)

        def next(self):
            bit, rest = self.order[0], self.order[1:]
            self.order = rest
            return bit, 2 ** sum(other < bit for other in rest)

        def home(self):
            right, got = tick(self.right, self.got)
            bit, low = self.next()
            self.v, send = grad_home(self.left, right, got, place, bit + 1, low, **self.span)
            tock(self.v, send)
            self.got = cross(send, bit)

        def fold(self):
            v, got = tick(self.v, self.got)
            bit, low = self.next()
            self.v, send = fold(v, got, place, bit + 1, low)
            tock(self.v, send)
            self.got = cross(send, bit)

        def two(self):
            while len(self.order) > 1:
                self.fold()

        def settle(self):
            v, got = tick(self.v, self.got)
            v, send = settle(v.reshape(v.shape[2:]), got.reshape(got.shape[2:]))
            tock(v, send)
            if groups > 2:
                total = v
                for k in range(1, groups // 2):
                    total = total + lax.ppermute(v, "rep", [(i, (i + 2 * k) % groups) for i in range(groups)])
                v, send = total, total.astype(BF16)
            self.v, self.got = v, swap(send)

        def both(self):
            return tick(self.v, self.got)

    per_d, per_r = mix_gain.shape[0], conv_bias.shape[0]
    vectors = jnp.concatenate(
        [mix_gain, ffn_gain, conv_kernel.reshape(-1), conv_bias, recur_bias, admit_bias, decay_param]
    )
    count = vectors.shape[0]
    vectors = jnp.pad(vectors, (0, -count % 128)).reshape(-1, 128)
    vectors = lax.all_gather(vectors, "shard", axis=0).reshape(shards, -1)[:, :count]
    gain_one = widen(vectors[:, :per_d].reshape(width))
    gain_two = widen(vectors[:, per_d : 2 * per_d].reshape(width))
    channel = vectors[:, 2 * per_d :].reshape(shards, taps + 4, per_r).transpose(1, 0, 2).reshape(taps + 4, low_r)
    channel = widen(mine(channel, half_r, 1))
    taps_half, cbias = channel[:taps], channel[taps]
    rbias, abias, lam = channel[taps + 1], channel[taps + 2], channel[taps + 3]
    rate = DECAY_SCALE * jax.nn.softplus(-lam)
    params = jnp.concatenate([jnp.stack([rbias, abias, rate]), jnp.zeros((5, half_r), F32)])

    def ffn_half(v):
        return lax.dynamic_index_in_dim(v.reshape(v.shape[0], shards, 2, piece_f), side, 2, False).reshape(v.shape[0], half_f)

    def gather_blocks(parts, block):
        rows = [p[:, at : at + block] for p in parts for at in range(0, p.shape[1], block)]
        return lax.all_gather(jnp.concatenate(rows, axis=0), "shard", axis=0)

    def unpack(whole, at, rows, columns):
        block = whole.shape[2]
        cols = [whole[:, at + i * rows : at + (i + 1) * rows].reshape(shards * rows, block) for i in range(columns // block)]
        return jnp.concatenate(cols, axis=1)

    per_f, tiles = 2 * piece_f, 3
    whole = lax.all_gather(
        pack(here_side, [branch_proj, lruin_proj, recur_proj, admit_proj], out_proj, 512), "shard", axis=0
    )
    ffn_blocks = gather_blocks(
        [ffn_half(ffn_gate), ffn_half(ffn_up), mine(ffn_down, piece_f, 0)], half_f // tiles
    )
    cot_pair = with_pair(cotangent)
    values = widen(with_pair(tokens))
    scale_one = lax.rsqrt(jnp.mean(values * values, axis=-1, keepdims=True) + EPS)
    normed = (values * scale_one * gain_one).astype(BF16)
    normed_t = flip(normed)
    tock(normed_t, cot_pair)
    whole, = tick(whole)
    at = low_r // 512 * per_d
    w1 = unpack(whole, 0, per_d, low_r)
    w2 = unpack(whole, at, per_r, low_r)
    w3 = unpack(whole, at + low_r // 512 * per_r, per_r, width)
    pre = matmul(normed, w1)
    lru_pre = pre[:, half_r:].reshape(2, length, half_r)
    conv = cbias
    for k in range(taps):
        conv = conv + taps_half[k] * shifted(lru_pre, k)
    admitted = conv.reshape(2 * length, half_r).astype(BF16)
    admitted_all = natural(admitted, swap_rows(admitted))
    gates = matmul(admitted_all, w2)
    mixed, *factors = recurrence_forward(pre, gates, admitted, params, length)
    tock(mixed)
    admitted_all, = tick(admitted_all)
    admitted_t = flip(admitted_all)
    tock(admitted_t)
    mixed_other, = tick(swap(mixed[length:]))
    mixed_own = natural(mixed[:length], mixed_other)
    middle = widen(tokens) + matmul(mixed_own, w3)
    scale_two = lax.rsqrt(jnp.mean(middle * middle, axis=-1, keepdims=True) + EPS)
    normed_two = (middle * scale_two * gain_two).astype(BF16)
    tock(normed_two)
    mixed_late, mixed_far = tick(mixed[length:], swap(mixed[:length]))
    mixed_t = flip(jnp.concatenate([mixed_own, natural(mixed_late, mixed_far)], axis=0))
    tock(mixed_t)
    normed_two = jnp.concatenate([normed_two, *tick(swap(normed_two))], axis=0)
    tock(normed_two)
    ffn_blocks, = tick(ffn_blocks)

    ffn = dict(rows=per_d, tiles=tiles)
    have, grads, steps = {}, {}, {}

    def step(run):
        steps[run.__name__] = run
        return run

    @step
    def ffn_in():
        x, = tick(normed_two)
        have["hidden"], have["hidden_t"], have["gate_cot"], have["up_cot"], near, far = ffn_pass(
            x, cot_pair, ffn_blocks, piece=piece_f, **ffn
        )
        tock(near, far)
        have["ffn"] = near, swap(far)

    @step
    def turn():
        x, = tick(normed_two)
        have["normed_two_t"] = flip(x)
        tock(have["normed_two_t"])

    @step
    def norm_two():
        near, far = tick(*have["ffn"])
        have["middle_cot"], low = norm_back(near, far, cotangent, middle, gain_two)
        tock(have["middle_cot"], low)
        have["middle_low"] = low, swap(low)

    @step
    def mixer():
        low, other = tick(*have["middle_low"])
        have["branch_low"], have["gates_cot"], have["direct"], have["sums"], near, far = chain_back(
            here_side, low, other, whole, at, per_r, factors
        )
        have["out_cot"] = jnp.concatenate([low, other], axis=0)
        tock(near, far)
        have["admitted"] = near, swap(far)

    @step
    def conv_in():
        direct, near, far = tick(have["direct"], *have["admitted"])
        have["pre_cot"], have["conv_sums"], near, far = conv_back(
            direct, near, far, pre, have["branch_low"], channel, whole, per_d, width
        )
        tock(near, far, have["pre_cot"])
        have["normed"] = near, swap(far)

    @step
    def norm_one():
        near, far = tick(*have["normed"])
        have["tokens_grad"], _ = norm_back(near, far, have["middle_cot"], tokens, gain_one)
        tock(have["tokens_grad"])

    @step
    def down():
        x, = tick(have["hidden"])
        near, far = down_pass(x, ffn_blocks, width, piece=piece_f, **ffn)
        tock(near, far)
        have["down"] = near, swap(far)

    @step
    def result():
        near, far = tick(*have["down"])
        have["block_out"] = (middle + near + widen(far)).astype(BF16)
        tock(have["block_out"])

    @step
    def small():
        conv_sums, sums = tick(have["conv_sums"], have["sums"])
        sums = jnp.sum(sums.reshape(3, ROWS, half_r), axis=1)
        v = jnp.concatenate([conv_sums[: taps + 1], sums[:2], sums[2:] * (DECAY_SCALE * jax.nn.sigmoid(-lam))])
        v = natural(v, jnp.zeros_like(v))
        tock(v)
        have["small"] = lax.psum(v, ("rep", "shard"))

    @step
    def small_end():
        v, = tick(have["small"])
        have["small"] = lax.dynamic_slice_in_dim(v, here * per_r, per_r, 1)
        tock(have["small"])

    def late(name, left, right, order=None, **span):
        def away():
            grads[name] = Scatter(left(), right(), order, **span)

        steps["away_" + name] = away
        for stage in ("home", "two", "fold", "settle"):
            steps[stage + "_" + name] = lambda stage=stage: getattr(grads[name], stage)()

    z_first = [2, 1] + list(range(3, bits))
    late("d", lambda: have["hidden_t"], lambda: cot_pair)
    late("g", lambda: have["normed_two_t"], lambda: have["gate_cot"])
    late("u", lambda: have["normed_two_t"], lambda: have["up_cot"], z_first)
    late("r", lambda: admitted_t, lambda: have["gates_cot"], z_first)
    late("b", lambda: normed_t, lambda: have["pre_cot"])
    late("o", lambda: mixed_t, lambda: have["out_cot"], columns=width // 2, skip=-1)

    @step
    def join_d():
        v, got = grads["d"].both()
        have["d"] = join_rows(here_side, v, got)
        tock(have["d"])

    @step
    def join_g():
        have["g"] = weave(here_side, *grads["g"].both(), piece_f)
        tock(have["g"])

    @step
    def join_u():
        have["u"] = weave(here_side, *grads["u"].both(), piece_f)
        tock(have["u"])

    @step
    def join_r():
        have["r"] = join_columns(here_side, *grads["r"].both(), 2)
        tock(*have["r"])

    @step
    def join_b():
        have["b"] = join_columns(here_side, *grads["b"].both(), 2)
        tock(*have["b"])

    @step
    def join_o():
        have["o"], = join_columns(here_side, *grads["o"].both(), 1)
        tock(have["o"])

    for name in STEPS:
        steps[name]()
    small_grad, (branch_grad, lruin_grad) = have["small"], have["b"]
    ffngain_grad = jnp.sum(have["g"] * widen(ffn_gate) + have["u"] * widen(ffn_up), axis=1) / widen(ffn_gain)
    mixgain_grad = jnp.sum(branch_grad * widen(branch_proj) + lruin_grad * widen(lruin_proj), axis=1) / widen(mix_gain)
    return (
        have["block_out"], have["tokens_grad"], mixgain_grad, branch_grad, lruin_grad, small_grad[:taps],
        small_grad[taps], have["r"][0], small_grad[taps + 1], have["r"][1], small_grad[taps + 2],
        small_grad[taps + 3], have["o"], ffngain_grad, have["g"], have["u"], have["d"],
    )


def solution(mesh):
    groups, shards = mesh.shape["rep"], mesh.shape["shard"]
    whole = P(("rep", "shard"), None)
    row, vec, col = P("shard", None), P("shard"), P(None, "shard")
    in_specs = (whole, whole, vec, row, row, col, vec, row, vec, row, vec, vec, row, vec, row, row, row)
    out_specs = (whole, whole, vec, row, row, col, vec, row, vec, row, vec, vec, row, vec, row, row, row)
    return jax.shard_map(
        functools.partial(body, groups, shards), mesh=mesh, in_specs=in_specs, out_specs=out_specs, check_vma=False
    )
```
